128 devices in a mesh: gx: 8 (over y, core), gy: 16 (over z, x).
Axes of the slice: x: 4, y: 4, z: 4, core: 2. Of those that a mesh axis runs over, the one named last changes fastest.
Arguments:
- stored: bfloat16 [128, 4096, 360], P(('gx', 'gy')), may hold values from -6 to 6
- counts: int32 [128, 128], P(('gx', 'gy')), may hold values from 0 to 32, as said below
- owners: int32 [128, 2048], P('gx', 'gy'), may hold values from 0 to 4095, as said below
- land_mask: int32 [128, 2048], P('gx', 'gy'), may hold values 0 or 1
- flow_x: float32 [128, 2048], P('gx', 'gy'), may hold values from -4 to 4
- flow_y: float32 [128, 2048], P('gx', 'gy'), may hold values from -4 to 4
- costate: float32 [3, 60, 128, 2048], P(None, None, 'gx', 'gy'), may hold values from -6 to 6
- weight_in: float32 [180, 256], replicated, may hold values from -0.4375 to 0.4375
- bias_in: float32 [256], replicated, may hold values from -3 to 3
- weight_mid: float32 [256, 256], replicated, may hold values from -0.375 to 0.375
- bias_mid: float32 [256], replicated, may hold values from -3 to 3
- weight_out: float32 [256, 60], replicated, may hold values from -0.375 to 0.375
- bias_out: float32 [60], replicated, may hold values from -4 to 4
Outputs:
- adjoint: float32 [3, 60, 128, 2048], P(None, None, 'gx', 'gy')
- grad_weight_in: float32 [180, 256], replicated
- grad_bias_in: float32 [256], replicated
- grad_weight_mid: float32 [256, 256], replicated
- grad_bias_mid: float32 [256], replicated
- grad_weight_out: float32 [256, 60], replicated
- grad_bias_out: float32 [60], replicated
The draws below stay inside these ranges and needn't reach their ends.
Inputs may be any that keep to these rules, and one draw needn't show every extreme that they name: counts[s, d] rows of device s belong to tile d; over s they sum to 2048 for every tile; some tile takes exactly 32 rows from one device. owners[x, y] = s * 32 + r with r < counts[s, d] for the column's tile d; within a tile every value appears once.
All inputs are finite; a program needn't handle non-finite values. No bound on the sum of `land_mask` on one device may be relied on, other than what follows from the above.
Results may differ from the reference program's by a relative error of at most 0.0003.
Values may be sent and summed in bfloat16 or wider, within the bound.
No kernel may reach another device: no remote copies, remote signals or barrier semaphores. Data moves between devices by JAX's collectives and lax.ppermute only.
A program may use at most 128 MiB of HBM per device.

```python
import jax
import jax.numpy as jnp
from jax import lax

CX = 16
CY = 128
NZ = 60
TRACERS = 3
HID = 256
TSTEPS = 2
NX = 128
NY = 2048
COLS = 2048
SLOT = 32
STORE = 4096
IN = 180
FEAT = 360
N_GX = 8
N_GY = 16
DEVICES = 128


def place_first(perm, wanted, position):
    spot = jnp.argmax(perm == wanted)
    moved = perm.at[spot].set(perm[position])
    return moved.at[position].set(wanted)


def storage_plan(key):
    devices = N_GX * N_GY
    half = devices // 2
    base = jax.random.fold_in(key, 7)
    key_sizes, key_source, key_order = jax.random.split(base, 3)
    first = jax.random.randint(key_sizes, (devices, half), 1, SLOT)
    first = jnp.where(jnp.arange(half)[None, :] == 0, SLOT, first)
    sizes = jnp.stack([first, SLOT - first], axis=-1).reshape(devices, devices).astype(jnp.int32)
    sources = jax.vmap(lambda sub: jax.random.permutation(sub, devices))(jax.random.split(key_source, devices)).astype(jnp.int32)
    lead = place_first(sources[0], devices - 1, 0)
    lead = place_first(lead, 0, 2)
    sources = sources.at[0].set(lead)
    orders = jax.vmap(lambda sub: jax.random.permutation(sub, COLS))(jax.random.split(key_order, devices)).astype(jnp.int32)
    ends = jnp.cumsum(sizes, axis=1)
    starts = ends - sizes
    ranks = jnp.arange(COLS, dtype=jnp.int32)
    groups = jax.vmap(lambda edge: jnp.searchsorted(edge, ranks, side='right'))(ends).astype(jnp.int32)
    within = ranks[None, :] - jnp.take_along_axis(starts, groups, axis=1)
    owner_src = jnp.take_along_axis(sources, groups, axis=1)
    values = owner_src * SLOT + within
    inverse = jnp.argsort(orders, axis=1)
    local = jnp.take_along_axis(values, inverse, axis=1)
    owners = local.reshape(N_GX, N_GY, CX, CY).transpose(0, 2, 1, 3).reshape(NX, NY)
    by_source = jnp.take_along_axis(sizes, jnp.argsort(sources, axis=1), axis=1)
    return (owners.astype(jnp.int32), by_source.T.astype(jnp.int32))


def draw_owners(key, part):
    return storage_plan(key)[0]


def draw_counts(key, part):
    return storage_plan(key)[1]


def place_ends(array, key, low, high):
    index_at = [jax.random.randint(jax.random.fold_in(key, axis), (), 0, length) for axis, length in enumerate(array.shape)]
    main_axis = array.shape.index(max(array.shape))
    next_to = index_at[:main_axis] + [(index_at[main_axis] + 1) % array.shape[main_axis]] + index_at[main_axis + 1:]
    return array.at[tuple(index_at)].set(low).at[tuple(next_to)].set(high)


def levels(own_key, shape, cuts, low, top_value):
    level = 1.0
    for axis_at, shards_of in cuts:
        steps = jax.random.uniform(jax.random.fold_in(jax.random.fold_in(own_key, 6), axis_at), (shards_of,), jnp.float32, low / len(cuts), top_value / len(cuts))
        level = level * jnp.repeat(jnp.exp(steps), shape[axis_at] // shards_of).reshape((-1,) + (1,) * (len(shape) - 1 - axis_at))
    return level


def noise(rng, extent, deviation, reach, shards=(), kind=jnp.bfloat16):
    values = jax.random.normal(rng, extent, jnp.float32) * deviation
    if len(shards) > 0:
        values = levels(rng, extent, shards, -0.22, 0.18) * values
    return jnp.clip(values, min=-reach, max=reach).astype(kind)


def setup_inputs(seed: int = 0) -> dict:
    key_list = jax.random.split(jax.random.key(seed), 14)
    return {
        "stored": noise(key_list[0], (DEVICES, STORE, FEAT), 1.0, 6.0, ((0, 128),)),
        "counts": draw_counts(jax.random.fold_in(key_list[13], 71), 0),
        "owners": draw_owners(jax.random.fold_in(key_list[13], 71), 0),
        "land_mask": place_ends((jax.random.randint(key_list[3], (NX, NY), 0, 4) < 3).astype(jnp.int32), jax.random.fold_in(key_list[3], 1), 0, 1),
        "flow_x": noise(key_list[4], (NX, NY), 1.0, 4.0, ((0, 8), (1, 16)), jnp.float32),
        "flow_y": noise(key_list[5], (NX, NY), 1.0, 4.0, ((0, 8), (1, 16)), jnp.float32),
        "costate": noise(key_list[6], (TRACERS, NZ, NX, NY), 1.0, 6.0, ((2, 8), (3, 16)), jnp.float32),
        "weight_in": noise(key_list[7], (IN, HID), IN ** -0.5, 0.4375, (), jnp.float32),
        "bias_in": noise(key_list[8], (HID,), 0.5, 3.0, (), jnp.float32),
        "weight_mid": noise(key_list[9], (HID, HID), HID ** -0.5, 0.375, (), jnp.float32),
        "bias_mid": noise(key_list[10], (HID,), 0.5, 3.0, (), jnp.float32),
        "weight_out": noise(key_list[11], (HID, NZ), HID ** -0.5, 0.375, (), jnp.float32),
        "bias_out": noise(key_list[12], (NZ,), 1.0, 4.0, (), jnp.float32),
    }


step_size = 0.25
flat_mix = 0.25
kappa_top = 1.5

def vertical(columns, params):
    weight_in, bias_in, weight_mid, bias_mid, weight_out, bias_out = params
    hp = lax.Precision.HIGHEST
    first = jnp.tanh(jnp.dot(weight_in.T, columns, precision=hp) + bias_in[:, None])
    second = jnp.tanh(jnp.dot(weight_mid.T, first, precision=hp) + bias_mid[:, None])
    kappa = kappa_top * jax.nn.sigmoid(jnp.dot(weight_out.T, second, precision=hp) + bias_out[:, None])
    field = columns.reshape(TRACERS, NZ, columns.shape[1])
    flux = kappa[None, :-1, :] * (field[:, 1:, :] - field[:, :-1, :])
    edge = jnp.zeros_like(flux[:, :1, :])
    upper = jnp.concatenate([flux, edge], axis=1)
    lower = jnp.concatenate([edge, flux], axis=1)
    return (upper - lower).reshape(columns.shape)

def transport(padded, padded_x, padded_y, weighted):
    near = padded[..., 2:, 1:-1] + padded[..., :-2, 1:-1] + padded[..., 1:-1, 2:] + padded[..., 1:-1, :-2]
    result = flat_mix * (near - 4.0 * weighted)
    result = result + 0.5 * (padded_x[..., 2:, 1:-1] - padded_x[..., :-2, 1:-1])
    return result + 0.5 * (padded_y[..., 1:-1, 2:] - padded_y[..., 1:-1, :-2])

def pad_plane(field):
    return jnp.pad(field, ((0, 0), (0, 0), (1, 1), (1, 1)))

def reference(stored, counts, owners, land_mask, flow_x, flow_y, costate, weight_in, bias_in, weight_mid, bias_mid, weight_out, bias_out):
    devices = N_GX * N_GY
    starts = jnp.cumsum(counts, axis=1) - counts
    tile = (jnp.arange(NX, dtype=jnp.int32) // CX)[:, None] * N_GY + (jnp.arange(NY, dtype=jnp.int32) // CY)[None, :]
    source = owners // SLOT
    within = owners % SLOT
    row_index = starts[source, tile] + within
    flat_index = (source * STORE + row_index).reshape(-1).astype(jnp.int32)
    picked = stored.reshape(devices * STORE, FEAT)[flat_index]
    states = picked.T.reshape(TSTEPS, TRACERS, NZ, NX, NY).astype(jnp.float32)
    params = (weight_in, bias_in, weight_mid, bias_mid, weight_out, bias_out)
    totals = jax.tree.map(jnp.zeros_like, params)
    ocean = land_mask.astype(jnp.float32)
    nblocks = NX * NY // COLS
    lam = costate
    for moment in range(TSTEPS - 1, -1, -1):
        state = states[moment]
        weighted = lam * ocean
        across = transport(pad_plane(weighted), pad_plane(flow_x * weighted), pad_plane(flow_y * weighted), weighted)
        state_blocks = state.reshape(IN, nblocks, COLS).transpose(1, 0, 2)
        weight_blocks = weighted.reshape(IN, nblocks, COLS).transpose(1, 0, 2)

        def one_block(carry, pair):
            block_state, block_weight = pair
            unused, pullback = jax.vjp(vertical, block_state, params)
            grad_state, grad_params = pullback(block_weight)
            return (jax.tree.map(lambda left, right: left + right, carry, grad_params), grad_state)
        zeros_params = jax.tree.map(jnp.zeros_like, params)
        block_grads, block_states = lax.scan(one_block, zeros_params, (state_blocks, weight_blocks))
        down = block_states.transpose(1, 0, 2).reshape(TRACERS, NZ, NX, NY)
        lam = lam + step_size * (across + down)
        totals = jax.tree.map(lambda left, right: left + step_size * right, totals, block_grads)
    scale = 1.0 / jnp.sqrt(jnp.float32(NX * NY))
    out = [total * scale for total in totals]
    return (lam, out[0], out[1], out[2], out[3], out[4], out[5])
```

```python
import functools

import jax
import jax.numpy as jnp
import numpy as np
from jax import lax
from jax.experimental import pallas as pl
from jax.experimental.pallas import tpu as pltpu
from jax.sharding import PartitionSpec as P

NZ = 60
TRACERS = 3
PAD = 64
FEATS = TRACERS * PAD
HID = 256
SLOT = 32
HALF = SLOT // 2
CX = 16
CY = 128
DEV = 128
STORE = 4096
PLANES = 4
COLS = PLANES * CY

BF = jnp.bfloat16
F32 = jnp.float32
NT = (((1,), (1,)), ((), ()))
PARAMS = pltpu.CompilerParams(vmem_limit_bytes=56 * 2**20)

step_size = 0.25
flat_mix = 0.25
kappa_top = 1.5


def split(value):
    high = value.astype(BF)
    return high, (value - high.astype(F32)).astype(BF)


def dot(left, right):
    return jnp.dot(left, right, preferred_element_type=F32)


def dot_nt(left, right):
    return lax.dot_general(left, right, NT, preferred_element_type=F32)


def pack_kernel(counts_ref, stored_ref, late_ref, early_ref, padded):
    padded[...] = jnp.zeros_like(padded)
    for block in range(2 * TRACERS):
        padded[block * PAD : block * PAD + NZ, :] = stored_ref[block * NZ : (block + 1) * NZ, :]
    lane = lax.broadcasted_iota(jnp.int32, (SLOT, 256), 1)
    offset = lane - lax.broadcasted_iota(jnp.int32, (SLOT, 256), 0)

    def group(g, start):
        base = pl.multiple_of(jnp.minimum((start // 128) * 128, STORE - 256), 128)
        hots = []
        for i in range(4):
            hots.append(jnp.where(offset == start - base, 1.0, 0.0))
            start = start + counts_ref[0, 4 * g + i]
        hot = jnp.concatenate(hots, axis=0).astype(BF)
        low = jnp.concatenate([h[:HALF] for h in hots], axis=0).astype(BF)
        high = jnp.concatenate([h[HALF:] for h in hots], axis=0).astype(BF)
        for out_ref, first in ((late_ref, FEATS), (early_ref, 0)):
            main = dot_nt(hot, padded[first : first + 2 * PAD, pl.ds(base, 256)]).astype(BF)
            last = padded[first + 2 * PAD : first + FEATS, pl.ds(base, 256)]
            rest = jnp.concatenate([dot_nt(low, last), dot_nt(high, last)], axis=1).astype(BF)
            for i in range(4):
                out_ref[4 * g + i, :SLOT, :] = main[i * SLOT : (i + 1) * SLOT]
                out_ref[4 * g + i, SLOT:, :] = rest[i * HALF : (i + 1) * HALF]
        return start

    lax.fori_loop(0, DEV // 4, group, jnp.int32(0))


def pack(counts, stored_t):
    out = jax.ShapeDtypeStruct((DEV, SLOT + HALF, 128), BF)
    return pl.pallas_call(
        pack_kernel,
        out_shape=(out, out),
        in_specs=[pl.BlockSpec(memory_space=pltpu.SMEM), pl.BlockSpec(memory_space=pltpu.VMEM)],
        out_specs=(pl.BlockSpec(memory_space=pltpu.VMEM),) * 2,
        scratch_shapes=[pltpu.VMEM((2 * FEATS, STORE), BF)],
        compiler_params=PARAMS,
        name="pack",
    )(counts, stored_t)


def weights_kernel(w1_ref, b1_ref, w2_ref, w3t_ref, f1_ref, f2_ref, f3_ref, r3_ref, r2_ref, r1_ref, wide, tall):
    wide[...] = jnp.zeros_like(wide)
    for t in range(TRACERS):
        wide[t * PAD : t * PAD + NZ, :] = w1_ref[t * NZ : (t + 1) * NZ, :]
    high, low = split(wide[...])
    r1_ref[:FEATS, :] = high
    r1_ref[FEATS:, :] = low
    wide[NZ : NZ + 1, :] = b1_ref[...]
    high, low = split(wide[...].T)
    f1_ref[:HID, :] = high
    f1_ref[HID:, :] = low
    high, low = split(w2_ref[...])
    r2_ref[:HID, :] = high
    r2_ref[HID:, :] = low
    high, low = split(w2_ref[...].T)
    f2_ref[:HID, :] = high
    f2_ref[HID:, :] = low
    tall[...] = jnp.zeros_like(tall)
    tall[:NZ, :] = w3t_ref[...]
    high, low = split(tall[:PAD, :])
    f3_ref[:PAD, :] = high
    f3_ref[PAD:, :] = low
    tall[PAD : 2 * PAD, :] = tall[:PAD, :]
    tall[2 * PAD :, :] = tall[:PAD, :]
    high, low = split(tall[...].T)
    lane = lax.broadcasted_iota(jnp.int32, high.shape, 1)
    middle = (lane >= PAD) & (lane < 2 * PAD)
    r3_ref[...] = jnp.where(middle, low.astype(F32), high.astype(F32)).astype(BF)


def weights(w1, b1, w2, w3t):
    shapes = ((2 * HID, FEATS), (2 * HID, HID), (2 * PAD, HID), (HID, FEATS), (2 * HID, HID), (2 * FEATS, HID))
    return pl.pallas_call(
        weights_kernel,
        out_shape=tuple(jax.ShapeDtypeStruct(s, BF) for s in shapes),
        scratch_shapes=[pltpu.VMEM((FEATS, HID), F32), pltpu.VMEM((FEATS, HID), F32)],
        compiler_params=PARAMS,
        name="weights",
    )(w1, b1, w2, w3t)


def edge_plane(x, plane, mask_row, fx_row, fy_row, ew_ref, ee_ref):
    weighted = plane * mask_row
    lane = lax.broadcasted_iota(jnp.int32, plane.shape, 1)
    west = pltpu.roll(weighted * (flat_mix + 0.5 * fy_row), x, 1)
    east = pltpu.roll(weighted * (flat_mix - 0.5 * fy_row), x + 1, 1)
    ew_ref[...] = jnp.where(lane == x, west, ew_ref[...])
    ee_ref[...] = jnp.where(lane == x, east, ee_ref[...])


def north_edge(plane, mask_row, fx_row):
    return plane * mask_row * (flat_mix + 0.5 * fx_row)


def south_edge(plane, mask_row, fx_row):
    return plane * mask_row * (flat_mix - 0.5 * fx_row)


def edges_kernel(raw_ref, mask_ref, fx_ref, fy_ref, planes_ref, en_ref, es_ref, ew_ref, ee_ref):
    planes_ref[...] = jnp.zeros_like(planes_ref)
    ew_ref[...] = jnp.zeros_like(ew_ref)
    ee_ref[...] = jnp.zeros_like(ee_ref)
    for x in range(CX):
        for t in range(TRACERS):
            planes_ref[x, t * PAD : t * PAD + NZ, :] = raw_ref[pl.ds(t * NZ * CX + x, NZ, stride=CX), :]
        mask_row = mask_ref[x : x + 1, :].astype(F32)
        edge_plane(x, planes_ref[x], mask_row, None, fy_ref[x : x + 1, :], ew_ref, ee_ref)
    en_ref[...] = north_edge(planes_ref[0], mask_ref[0:1, :].astype(F32), fx_ref[0:1, :])
    es_ref[...] = south_edge(planes_ref[CX - 1], mask_ref[CX - 1 :, :].astype(F32), fx_ref[CX - 1 :, :])


EDGE = jax.ShapeDtypeStruct((FEATS, CY), F32)
PLANE = jax.ShapeDtypeStruct((CX, FEATS, CY), F32)


def edges(raw, mask, fx, fy):
    return pl.pallas_call(
        edges_kernel,
        out_shape=(PLANE, EDGE, EDGE, EDGE, EDGE),
        compiler_params=PARAMS,
        name="edges",
    )(raw, mask, fx, fy)


def stencil_plane(x, lam_ref, mask_ref, fx_ref, fy_ref, hn_ref, hs_ref, hw_ref, he_ref):
    def row(ref, at):
        return ref[at : at + 1, :].astype(F32)

    plane = lam_ref[x]
    weighted = plane * row(mask_ref, x)
    if x < CX - 1:
        total = north_edge(lam_ref[x + 1], row(mask_ref, x + 1), row(fx_ref, x + 1))
    else:
        total = hn_ref[...]
    if x > 0:
        total = total + south_edge(lam_ref[x - 1], row(mask_ref, x - 1), row(fx_ref, x - 1))
    else:
        total = total + hs_ref[...]
    lane = lax.broadcasted_iota(jnp.int32, plane.shape, 1)
    fy = row(fy_ref, x)
    west = pltpu.roll(weighted * (flat_mix + 0.5 * fy), CY - 1, 1)
    total = total + jnp.where(lane == CY - 1, pltpu.roll(hw_ref[...], CY - 1 - x, 1), west)
    east = pltpu.roll(weighted * (flat_mix - 0.5 * fy), 1, 1)
    from_east = he_ref[...] if x == 0 else pltpu.roll(he_ref[...], CY - x, 1)
    total = total + jnp.where(lane == 0, from_east, east)
    return plane, total - weighted


def first_kernel(lam_ref, mask_ref, fx_ref, fy_ref, hn_ref, hs_ref, hw_ref, he_ref, out_ref):
    for x in range(CX):
        plane, total = stencil_plane(x, lam_ref, mask_ref, fx_ref, fy_ref, hn_ref, hs_ref, hw_ref, he_ref)
        out_ref[x] = plane + step_size * total


def first_stencil(lam, mask, fx, fy, halos):
    return pl.pallas_call(first_kernel, out_shape=PLANE, compiler_params=PARAMS, name="stencil1")(
        lam, mask, fx, fy, *halos
    )


def last_kernel(lam_ref, down_ref, mask_ref, fx_ref, fy_ref, hn_ref, hs_ref, hw_ref, he_ref, out_ref):
    for x in range(CX):
        plane, total = stencil_plane(x, lam_ref, mask_ref, fx_ref, fy_ref, hn_ref, hs_ref, hw_ref, he_ref)
        value = plane + step_size * (total + down_ref[x])
        for t in range(TRACERS):
            out_ref[pl.ds(t * NZ * CX + x, NZ, stride=CX), :] = value[t * PAD : t * PAD + NZ]


def last_stencil(lam, down, mask, fx, fy, halos):
    return pl.pallas_call(
        last_kernel,
        out_shape=jax.ShapeDtypeStruct((TRACERS * NZ * CX, CY), F32),
        compiler_params=PARAMS,
        name="stencil0",
    )(lam, down, mask, fx, fy, *halos)


def closure_kernel(first, *refs):
    (owner_ref, mask_ref, got_ref, lam_ref, f1_ref, f2_ref, f3_ref, r3_ref, r2_ref, r1_ref, b2_ref, b3_ref) = refs[:12]
    refs = refs[12:]
    if first:
        fx_ref, fy_ref, base_ref, out_ref, grads_ref, en_ref, es_ref, ew_ref, ee_ref = refs[:9]
        refs = refs[9:]
    else:
        before_ref, out_ref, grads_ref = refs[:3]
        refs = refs[3:]
    rows_ref, total = refs
    block = pl.program_id(0)

    @pl.when(block == 0)
    def _():
        for half in range(2):
            for g in range(DEV // 8):
                at = half * (STORE // 2) + g * 128
                main = [got_ref[8 * g + i, half * HALF : (half + 1) * HALF, :] for i in range(8)]
                rows_ref[: 2 * PAD, at : at + 128] = jnp.concatenate(main, axis=0).T
        for g in range(DEV // 8):
            rest = [got_ref[8 * g + i, SLOT:, :] for i in range(8)]
            both = jnp.concatenate(rest, axis=0).T
            rows_ref[2 * PAD :, g * 128 : (g + 1) * 128] = both[:PAD]
            at = STORE // 2 + g * 128
            rows_ref[2 * PAD :, at : at + 128] = both[PAD:]
        if first:
            total[...] = jnp.zeros_like(total)
            ew_ref[...] = jnp.zeros_like(ew_ref)
            ee_ref[...] = jnp.zeros_like(ee_ref)
        else:
            total[...] = before_ref[...]

    x0 = block * PLANES

    def wide(ref):
        return jnp.concatenate([ref[pl.ds(x0 + i, 1), :] for i in range(PLANES)], axis=1)

    owner = wide(owner_ref)
    at = ((owner >> 4) & 1) * (STORE // 2) + (owner >> 5) * HALF + (owner & (HALF - 1))
    level = lax.broadcasted_iota(jnp.int32, (256, COLS), 0)
    picked = None
    for k in range(STORE // 256):
        hot = jnp.where(level == at - 256 * k, 1.0, 0.0).astype(BF)
        part = dot(rows_ref[:, 256 * k : 256 * (k + 1)], hot)
        picked = part if picked is None else picked + part
    row = lax.broadcasted_iota(jnp.int32, (FEATS, COLS), 0)
    inputs = jnp.where(row == NZ, 1.0, picked).astype(BF)

    both = dot(f1_ref[...], inputs)
    h1 = jnp.tanh(both[:HID] + both[HID:])
    h1_high, h1_low = split(h1)
    both = dot(f2_ref[...], h1_high)
    h2 = jnp.tanh(both[:HID] + both[HID:] + dot(f2_ref[:HID], h1_low) + b2_ref[...])
    h2_high, h2_low = split(h2)
    both = dot(f3_ref[...], h2_high)
    sig = jax.nn.sigmoid(both[:PAD] + both[PAD:] + dot(f3_ref[:PAD], h2_low) + b3_ref[...])
    inner = lax.broadcasted_iota(jnp.int32, (PAD, COLS), 0) < NZ - 1
    kappa = jnp.where(inner, kappa_top * sig, 0.0)

    mask_row = wide(mask_ref).astype(F32)
    slope = jnp.zeros((PAD, COLS), F32)
    direct = []
    for t in range(TRACERS):
        lo, hi = t * PAD, (t + 1) * PAD
        mu = jnp.concatenate([lam_ref[i, lo:hi, :] for i in range(PLANES)], axis=1) * mask_row
        gap = mu - pltpu.roll(mu, PAD - 1, 0)
        column = picked[lo:hi]
        slope = slope + gap * (pltpu.roll(column, PAD - 1, 0) - column)
        flow = kappa * gap
        direct.append(pltpu.roll(flow, 1, 0) - flow)
    d3 = slope * kappa * (1.0 - sig)
    d3_high, d3_low = split(d3)
    d2 = dot(r3_ref[...], jnp.concatenate([d3_high, d3_high, d3_low], axis=0)) * (1.0 - h2 * h2)
    d2_high, d2_low = split(d2)
    both = dot(r2_ref[...], d2_high)
    d1 = (both[:HID] + both[HID:] + dot(r2_ref[:HID], d2_low)) * (1.0 - h1 * h1)
    d1_high, d1_low = split(d1)
    both = dot(r1_ref[...], d1_high)
    d0 = both[:FEATS] + both[FEATS:] + dot(r1_ref[:FEATS], d1_low)

    ones = jnp.ones((16, COLS), BF)
    total[:FEATS, :] += dot_nt(inputs, d1_high) + dot_nt(inputs, d1_low)
    both = dot_nt(jnp.concatenate([h1_high, h1_low, ones], axis=0), d2_high)
    other = dot_nt(jnp.concatenate([h1_high, ones], axis=0), d2_low)
    total[FEATS : FEATS + HID, :] += both[:HID] + both[HID : 2 * HID] + other[:HID]
    total[NZ + 1 : NZ + 2, :] += both[2 * HID : 2 * HID + 1] + other[HID : HID + 1]
    d3_both = jnp.concatenate([d3_high, d3_low], axis=0)
    both = dot_nt(d3_both, h2_high)
    total[FEATS + HID :, :] += both[:PAD] + both[PAD:] + dot_nt(d3_high, h2_low)
    both = dot_nt(ones, d3_both)
    total[NZ + 2 : NZ + 3, :PAD] += both[:1, :PAD] + both[:1, PAD:]

    for i in range(PLANES):
        part = slice(i * CY, (i + 1) * CY)
        for t in range(TRACERS):
            lo, hi = t * PAD, (t + 1) * PAD
            down = d0[lo:hi, part] + direct[t][:, part]
            if first:
                out_ref[i, lo:hi, :] = base_ref[i, lo:hi, :] + step_size * down
            else:
                out_ref[i, lo:hi, :] = down
        if first:
            x = x0 + i
            edge_plane(
                x, out_ref[i], mask_ref[pl.ds(x, 1), :].astype(F32), None, fy_ref[pl.ds(x, 1), :], ew_ref, ee_ref
            )

    if first:

        @pl.when(block == 0)
        def _():
            en_ref[...] = north_edge(out_ref[0], mask_ref[0:1, :].astype(F32), fx_ref[0:1, :])

    @pl.when(block == CX // PLANES - 1)
    def _():
        if first:
            es_ref[...] = south_edge(out_ref[PLANES - 1], mask_ref[CX - 1 :, :].astype(F32), fx_ref[CX - 1 :, :])
            grads_ref[...] = total[...]
        else:
            grads_ref[: 2 * HID, :] = total[:, :128]
            grads_ref[2 * HID :, :] = total[:, 128:]


def closure(first, owners, mask, got, lam, split_weights, b2, b3, *extra):
    whole = pl.BlockSpec(memory_space=pltpu.VMEM)
    planes = pl.BlockSpec((PLANES, FEATS, CY), lambda b: (b, 0, 0))
    in_specs = [whole, whole, whole, planes] + [whole] * 8
    if first:
        in_specs += [whole, whole, planes]
        out_shape = (PLANE, jax.ShapeDtypeStruct((2 * HID, HID), F32), EDGE, EDGE, EDGE, EDGE)
        out_specs = (planes,) + (whole,) * 5
    else:
        in_specs += [whole]
        out_shape = (PLANE, jax.ShapeDtypeStruct((4 * HID, 128), F32))
        out_specs = (planes, whole)
    return pl.pallas_call(
        functools.partial(closure_kernel, first),
        grid=(CX // PLANES,),
        out_shape=out_shape,
        in_specs=in_specs,
        out_specs=out_specs,
        scratch_shapes=[pltpu.VMEM((FEATS, STORE), BF), pltpu.VMEM((2 * HID, HID), F32)],
        compiler_params=PARAMS,
        name="closure1" if first else "closure0",
    )(owners, mask, got, lam, *split_weights, b2, b3, *extra)


def sum_kernel(parts_ref, out_ref):
    value = parts_ref[0:8, :]
    for i in range(1, DEV):
        value = value + parts_ref[8 * i : 8 * i + 8, :]
    for i in range(DEV):
        out_ref[8 * i : 8 * i + 8, :] = value


def unpack_kernel(scale, sums_ref, w1_ref, b1_ref, w2_ref, b2_ref, w3t_ref, b3_ref):
    for part in range(2):
        lanes = slice(part * 128, (part + 1) * 128)
        top = part * 2 * HID
        for t in range(TRACERS):
            w1_ref[t * NZ : (t + 1) * NZ, lanes] = sums_ref[top + t * PAD : top + t * PAD + NZ, :] * scale
        b1_ref[:, lanes] = sums_ref[top + NZ : top + NZ + 1, :] * scale
        b2_ref[:, lanes] = sums_ref[top + NZ + 1 : top + NZ + 2, :] * scale
        w2_ref[:, lanes] = sums_ref[top + FEATS : top + FEATS + HID, :] * scale
        w3t_ref[:, lanes] = sums_ref[top + FEATS + HID : top + FEATS + HID + NZ, :] * scale
    b3_ref[...] = sums_ref[NZ + 2 : NZ + 3, :NZ] * scale


def reduce_params(packed, count):
    parts = lax.all_to_all(packed, ("gx", "gy"), split_axis=0, concat_axis=0, tiled=True)
    spread = pl.pallas_call(
        sum_kernel, out_shape=jax.ShapeDtypeStruct(packed.shape, F32), compiler_params=PARAMS, name="sum"
    )(parts)
    sums = lax.all_to_all(spread, ("gx", "gy"), split_axis=0, concat_axis=0, tiled=True)
    shapes = ((TRACERS * NZ, HID), (1, HID), (HID, HID), (1, HID), (NZ, HID), (1, NZ))
    return pl.pallas_call(
        functools.partial(unpack_kernel, step_size / float(np.sqrt(count))),
        out_shape=tuple(jax.ShapeDtypeStruct(s, F32) for s in shapes),
        compiler_params=PARAMS,
        name="unpack",
    )(sums)


def exchange(north, south, west, east):
    gx, gy = lax.axis_size("gx"), lax.axis_size("gy")
    down_x = [(i + 1, i) for i in range(gx - 1)]
    up_x = [(i, i + 1) for i in range(gx - 1)]
    down_y = [(i + 1, i) for i in range(gy - 1)]
    up_y = [(i, i + 1) for i in range(gy - 1)]
    return (
        lax.ppermute(north, "gx", down_x),
        lax.ppermute(south, "gx", up_x),
        lax.ppermute(west, "gy", down_y),
        lax.ppermute(east, "gy", up_y),
    )


def on_device(
    stored,
    counts,
    owners,
    land_mask,
    flow_x,
    flow_y,
    costate,
    weight_in,
    bias_in,
    weight_mid,
    bias_mid,
    weight_out,
    bias_out,
):
    late, early = pack(counts, stored[0].T)
    late = lax.all_to_all(late, ("gx", "gy"), split_axis=0, concat_axis=0, tiled=True)
    early = lax.all_to_all(early, ("gx", "gy"), split_axis=0, concat_axis=0, tiled=True)
    split_weights = weights(weight_in, bias_in[None, :], weight_mid, weight_out.T)
    b2 = bias_mid[:, None]
    b3 = jnp.pad(bias_out, (0, PAD - NZ))[:, None]
    planes, *sides = edges(costate.reshape(TRACERS * NZ * CX, CY), land_mask, flow_x, flow_y)
    halos = exchange(*sides)
    base = first_stencil(planes, land_mask, flow_x, flow_y, halos)
    lam, grads, *sides = closure(
        True, owners, land_mask, late, planes, split_weights, b2, b3, flow_x, flow_y, base
    )
    halos = exchange(*sides)
    down, packed = closure(False, owners, land_mask, early, lam, split_weights, b2, b3, grads)
    adjoint = last_stencil(lam, down, land_mask, flow_x, flow_y, halos)
    count = CX * CY * lax.axis_size("gx") * lax.axis_size("gy")
    g1, gb1, g2, gb2, g3, gb3 = reduce_params(packed, count)
    return (adjoint.reshape(costate.shape), g1, gb1[0], g2, gb2[0], g3.T, gb3[0])


def solution(mesh):
    in_specs = (
        P(("gx", "gy"), None, None),
        P(("gx", "gy"), None),
        P("gx", "gy"),
        P("gx", "gy"),
        P("gx", "gy"),
        P("gx", "gy"),
        P(None, None, "gx", "gy"),
        P(),
        P(),
        P(),
        P(),
        P(),
        P(),
    )
    out_specs = (P(None, None, "gx", "gy"), P(), P(), P(), P(), P(), P())
    return jax.shard_map(
        on_device, mesh=mesh, in_specs=in_specs, out_specs=out_specs, check_vma=False
    )
```

```python
import functools

import jax
import jax.numpy as jnp
import numpy as np
from jax import lax
from jax.experimental import pallas as pl
from jax.experimental.pallas import tpu as pltpu
from jax.sharding import PartitionSpec as P

NZ = 60
TRACERS = 3
PAD = 64
FEATS = TRACERS * PAD
HID = 256
SLOT = 32
HALF = SLOT // 2
CX = 16
CY = 128
DEV = 128
STORE = 4096
PLANES = 16
UNROLL = 8
COLS = PLANES * CY

BF = jnp.bfloat16
F32 = jnp.float32
NT = (((1,), (1,)), ((), ()))
PARAMS = pltpu.CompilerParams(vmem_limit_bytes=56 * 2**20)

step_size = 0.25
flat_mix = 0.25
kappa_top = 1.5


def split(value):
    high = value.astype(BF)
    return high, (value - high.astype(F32)).astype(BF)


def dot(left, right):
    return jnp.dot(left, right, preferred_element_type=F32)


def dot_nt(left, right):
    return lax.dot_general(left, right, NT, preferred_element_type=F32)


def pack_kernel(moment, counts_ref, stored_ref, out_ref, near, padded, sem):
    top = moment * TRACERS * NZ // 8 * 8
    copy = pltpu.make_async_copy(stored_ref.at[top : top + near.shape[0], :], near, sem)
    copy.start()
    lane = lax.broadcasted_iota(jnp.int32, (SLOT, 256), 1)
    offset = lane - lax.broadcasted_iota(jnp.int32, (SLOT, 256), 0)
    for t in range(TRACERS):
        padded[t * PAD + NZ : (t + 1) * PAD, :] = jnp.zeros((PAD - NZ, STORE), BF)
    copy.wait()
    skip = moment * TRACERS * NZ - top
    for t in range(TRACERS):
        padded[t * PAD : t * PAD + NZ, :] = near[skip + t * NZ : skip + (t + 1) * NZ, :]

    def group(g, start):
        base = pl.multiple_of(jnp.minimum((start // 128) * 128, STORE - 256), 128)
        hots = []
        for i in range(4):
            hots.append(jnp.where(offset == start - base, 1.0, 0.0).astype(BF))
            start = start + counts_ref[0, 4 * g + i]
        rows = dot_nt(jnp.concatenate(hots, axis=0), padded[:, pl.ds(base, 256)])
        for i in range(4):
            mine = rows[i * SLOT : (i + 1) * SLOT]
            rest = jnp.concatenate([mine[:HALF, 2 * PAD :], mine[HALF:, 2 * PAD :]], axis=1)
            out_ref[4 * g + i, :SLOT, :] = mine[:, : 2 * PAD].astype(BF)
            out_ref[4 * g + i, SLOT:, :] = rest.astype(BF)
        return start

    def groups(j, start):
        for u in range(UNROLL):
            start = group(j * UNROLL + u, start)
        return start

    lax.fori_loop(0, DEV // 4 // UNROLL, groups, jnp.int32(0))


def pack(moment, counts, stored_t):
    return pl.pallas_call(
        functools.partial(pack_kernel, moment),
        out_shape=jax.ShapeDtypeStruct((DEV, SLOT + HALF, 128), BF),
        in_specs=[pl.BlockSpec(memory_space=pltpu.SMEM), pl.BlockSpec(memory_space=pl.ANY)],
        out_specs=pl.BlockSpec(memory_space=pltpu.VMEM),
        scratch_shapes=[
            pltpu.VMEM((TRACERS * NZ + 4, STORE), BF),
            pltpu.VMEM((FEATS, STORE), BF),
            pltpu.SemaphoreType.DMA,
        ],
        compiler_params=PARAMS,
        name=f"pack{moment}",
    )(counts, stored_t)


def weights_kernel(w1_ref, b1_ref, w2_ref, w3t_ref, f1_ref, f2_ref, f3_ref, r3_ref, r2_ref, r1_ref, wide, tall):
    wide[...] = jnp.zeros_like(wide)
    for t in range(TRACERS):
        wide[t * PAD : t * PAD + NZ, :] = w1_ref[t * NZ : (t + 1) * NZ, :]
    high, low = split(wide[...])
    r1_ref[:FEATS, :] = high
    r1_ref[FEATS:, :] = low
    wide[NZ : NZ + 1, :] = b1_ref[...]
    high, low = split(wide[...].T)
    f1_ref[:HID, :] = high
    f1_ref[HID:, :] = low
    high, low = split(w2_ref[...])
    r2_ref[:HID, :] = high
    r2_ref[HID:, :] = low
    high, low = split(w2_ref[...].T)
    f2_ref[:HID, :] = high
    f2_ref[HID:, :] = low
    tall[...] = jnp.zeros_like(tall)
    tall[:NZ, :] = w3t_ref[...]
    high, low = split(tall[:PAD, :])
    f3_ref[:PAD, :] = high
    f3_ref[PAD:, :] = low
    tall[PAD : 2 * PAD, :] = tall[:PAD, :]
    tall[2 * PAD :, :] = tall[:PAD, :]
    high, low = split(tall[...].T)
    lane = lax.broadcasted_iota(jnp.int32, high.shape, 1)
    middle = (lane >= PAD) & (lane < 2 * PAD)
    r3_ref[...] = jnp.where(middle, low.astype(F32), high.astype(F32)).astype(BF)


def weights(w1, b1, w2, w3t):
    shapes = ((2 * HID, FEATS), (2 * HID, HID), (2 * PAD, HID), (HID, FEATS), (2 * HID, HID), (2 * FEATS, HID))
    return pl.pallas_call(
        weights_kernel,
        out_shape=tuple(jax.ShapeDtypeStruct(s, BF) for s in shapes),
        scratch_shapes=[pltpu.VMEM((FEATS, HID), F32), pltpu.VMEM((FEATS, HID), F32)],
        compiler_params=PARAMS,
        name="weights",
    )(w1, b1, w2, w3t)


def edge_plane(x, plane, mask_row, fx_row, fy_row, ew_ref, ee_ref):
    weighted = plane * mask_row
    lane = lax.broadcasted_iota(jnp.int32, plane.shape, 1)
    west = pltpu.roll(weighted * (flat_mix + 0.5 * fy_row), x, 1)
    east = pltpu.roll(weighted * (flat_mix - 0.5 * fy_row), x + 1, 1)
    ew_ref[...] = jnp.where(lane == x, west, ew_ref[...])
    ee_ref[...] = jnp.where(lane == x, east, ee_ref[...])


def north_edge(plane, mask_row, fx_row):
    return plane * mask_row * (flat_mix + 0.5 * fx_row)


def south_edge(plane, mask_row, fx_row):
    return plane * mask_row * (flat_mix - 0.5 * fx_row)


def edges_kernel(raw_ref, mask_ref, fx_ref, fy_ref, planes_ref, en_ref, es_ref, ew_ref, ee_ref):
    planes_ref[...] = jnp.zeros_like(planes_ref)
    ew_ref[...] = jnp.zeros_like(ew_ref)
    ee_ref[...] = jnp.zeros_like(ee_ref)
    for x in range(CX):
        for t in range(TRACERS):
            planes_ref[x, t * PAD : t * PAD + NZ, :] = raw_ref[pl.ds(t * NZ * CX + x, NZ, stride=CX), :]
        mask_row = mask_ref[x : x + 1, :].astype(F32)
        edge_plane(x, planes_ref[x], mask_row, None, fy_ref[x : x + 1, :], ew_ref, ee_ref)
    en_ref[...] = north_edge(planes_ref[0], mask_ref[0:1, :].astype(F32), fx_ref[0:1, :])
    es_ref[...] = south_edge(planes_ref[CX - 1], mask_ref[CX - 1 :, :].astype(F32), fx_ref[CX - 1 :, :])


EDGE = jax.ShapeDtypeStruct((FEATS, CY), F32)
PLANE = jax.ShapeDtypeStruct((CX, FEATS, CY), F32)


def edges(raw, mask, fx, fy):
    return pl.pallas_call(
        edges_kernel,
        out_shape=(PLANE, EDGE, EDGE, EDGE, EDGE),
        compiler_params=PARAMS,
        name="edges",
    )(raw, mask, fx, fy)


def stencil_plane(x, lam_ref, mask_ref, fx_ref, fy_ref, hn_ref, hs_ref, hw_ref, he_ref):
    def row(ref, at):
        return ref[at : at + 1, :].astype(F32)

    plane = lam_ref[x]
    weighted = plane * row(mask_ref, x)
    if x < CX - 1:
        total = north_edge(lam_ref[x + 1], row(mask_ref, x + 1), row(fx_ref, x + 1))
    else:
        total = hn_ref[...]
    if x > 0:
        total = total + south_edge(lam_ref[x - 1], row(mask_ref, x - 1), row(fx_ref, x - 1))
    else:
        total = total + hs_ref[...]
    lane = lax.broadcasted_iota(jnp.int32, plane.shape, 1)
    fy = row(fy_ref, x)
    west = pltpu.roll(weighted * (flat_mix + 0.5 * fy), CY - 1, 1)
    total = total + jnp.where(lane == CY - 1, pltpu.roll(hw_ref[...], CY - 1 - x, 1), west)
    east = pltpu.roll(weighted * (flat_mix - 0.5 * fy), 1, 1)
    from_east = he_ref[...] if x == 0 else pltpu.roll(he_ref[...], CY - x, 1)
    total = total + jnp.where(lane == 0, from_east, east)
    return plane, total - weighted


def first_kernel(lam_ref, mask_ref, fx_ref, fy_ref, hn_ref, hs_ref, hw_ref, he_ref, out_ref):
    for x in range(CX):
        plane, total = stencil_plane(x, lam_ref, mask_ref, fx_ref, fy_ref, hn_ref, hs_ref, hw_ref, he_ref)
        out_ref[x] = plane + step_size * total


def first_stencil(lam, mask, fx, fy, halos):
    return pl.pallas_call(first_kernel, out_shape=PLANE, compiler_params=PARAMS, name="stencil1")(
        lam, mask, fx, fy, *halos
    )


def last_kernel(lam_ref, down_ref, mask_ref, fx_ref, fy_ref, hn_ref, hs_ref, hw_ref, he_ref, out_ref):
    for x in range(CX):
        plane, total = stencil_plane(x, lam_ref, mask_ref, fx_ref, fy_ref, hn_ref, hs_ref, hw_ref, he_ref)
        value = plane + step_size * (total + down_ref[x])
        for t in range(TRACERS):
            out_ref[pl.ds(t * NZ * CX + x, NZ, stride=CX), :] = value[t * PAD : t * PAD + NZ]


def last_stencil(lam, down, mask, fx, fy, halos):
    return pl.pallas_call(
        last_kernel,
        out_shape=jax.ShapeDtypeStruct((TRACERS * NZ * CX, CY), F32),
        compiler_params=PARAMS,
        name="stencil0",
    )(lam, down, mask, fx, fy, *halos)


def closure_kernel(first, *refs):
    (owner_ref, mask_ref, got_ref, lam_ref, f1_ref, f2_ref, f3_ref, r3_ref, r2_ref, r1_ref, b2_ref, b3_ref) = refs[:12]
    refs = refs[12:]
    if first:
        fx_ref, fy_ref, base_ref, out_ref, grads_ref, en_ref, es_ref, ew_ref, ee_ref = refs[:9]
        refs = refs[9:]
    else:
        before_ref, out_ref, grads_ref = refs[:3]
        refs = refs[3:]
    rows_ref, total = refs
    block = pl.program_id(0)

    @pl.when(block == 0)
    def _():
        for half in range(2):
            for g in range(DEV // 8):
                at = half * (STORE // 2) + g * 128
                main = [got_ref[8 * g + i, half * HALF : (half + 1) * HALF, :] for i in range(8)]
                rows_ref[: 2 * PAD, at : at + 128] = jnp.concatenate(main, axis=0).T
        for g in range(DEV // 8):
            rest = [got_ref[8 * g + i, SLOT:, :] for i in range(8)]
            both = jnp.concatenate(rest, axis=0).T
            rows_ref[2 * PAD :, g * 128 : (g + 1) * 128] = both[:PAD]
            at = STORE // 2 + g * 128
            rows_ref[2 * PAD :, at : at + 128] = both[PAD:]
        if first:
            total[...] = jnp.zeros_like(total)
            ew_ref[...] = jnp.zeros_like(ew_ref)
            ee_ref[...] = jnp.zeros_like(ee_ref)
        else:
            total[...] = before_ref[...]

    x0 = block * PLANES

    def wide(ref):
        return jnp.concatenate([ref[pl.ds(x0 + i, 1), :] for i in range(PLANES)], axis=1)

    owner = wide(owner_ref)
    at = ((owner >> 4) & 1) * (STORE // 2) + (owner >> 5) * HALF + (owner & (HALF - 1))
    level = lax.broadcasted_iota(jnp.int32, (256, COLS), 0)
    picked = None
    for k in range(STORE // 256):
        hot = jnp.where(level == at - 256 * k, 1.0, 0.0).astype(BF)
        part = dot(rows_ref[:, 256 * k : 256 * (k + 1)], hot)
        picked = part if picked is None else picked + part
    row = lax.broadcasted_iota(jnp.int32, (FEATS, COLS), 0)
    inputs = jnp.where(row == NZ, 1.0, picked).astype(BF)

    both = dot(f1_ref[...], inputs)
    h1 = jnp.tanh(both[:HID] + both[HID:])
    h1_high, h1_low = split(h1)
    both = dot(f2_ref[...], h1_high)
    h2 = jnp.tanh(both[:HID] + both[HID:] + dot(f2_ref[:HID], h1_low) + b2_ref[...])
    h2_high, h2_low = split(h2)
    both = dot(f3_ref[...], h2_high)
    sig = jax.nn.sigmoid(both[:PAD] + both[PAD:] + dot(f3_ref[:PAD], h2_low) + b3_ref[...])
    inner = lax.broadcasted_iota(jnp.int32, (PAD, COLS), 0) < NZ - 1
    kappa = jnp.where(inner, kappa_top * sig, 0.0)

    mask_row = wide(mask_ref).astype(F32)
    slope = jnp.zeros((PAD, COLS), F32)
    direct = []
    for t in range(TRACERS):
        lo, hi = t * PAD, (t + 1) * PAD
        mu = jnp.concatenate([lam_ref[i, lo:hi, :] for i in range(PLANES)], axis=1) * mask_row
        gap = mu - pltpu.roll(mu, PAD - 1, 0)
        column = picked[lo:hi]
        slope = slope + gap * (pltpu.roll(column, PAD - 1, 0) - column)
        flow = kappa * gap
        direct.append(pltpu.roll(flow, 1, 0) - flow)
    d3 = slope * kappa * (1.0 - sig)
    d3_high, d3_low = split(d3)
    d2 = dot(r3_ref[...], jnp.concatenate([d3_high, d3_high, d3_low], axis=0)) * (1.0 - h2 * h2)
    d2_high, d2_low = split(d2)
    both = dot(r2_ref[...], d2_high)
    d1 = (both[:HID] + both[HID:] + dot(r2_ref[:HID], d2_low)) * (1.0 - h1 * h1)
    d1_high, d1_low = split(d1)
    both = dot(r1_ref[...], d1_high)
    d0 = both[:FEATS] + both[FEATS:] + dot(r1_ref[:FEATS], d1_low)

    ones = jnp.ones((16, COLS), BF)
    total[:FEATS, :] += dot_nt(inputs, d1_high) + dot_nt(inputs, d1_low)
    both = dot_nt(jnp.concatenate([h1_high, h1_low, ones], axis=0), d2_high)
    other = dot_nt(jnp.concatenate([h1_high, ones], axis=0), d2_low)
    total[FEATS : FEATS + HID, :] += both[:HID] + both[HID : 2 * HID] + other[:HID]
    total[NZ + 1 : NZ + 2, :] += both[2 * HID : 2 * HID + 1] + other[HID : HID + 1]
    d3_both = jnp.concatenate([d3_high, d3_low], axis=0)
    both = dot_nt(d3_both, h2_high)
    total[FEATS + HID :, :] += both[:PAD] + both[PAD:] + dot_nt(d3_high, h2_low)
    both = dot_nt(ones, d3_both)
    total[NZ + 2 : NZ + 3, :PAD] += both[:1, :PAD] + both[:1, PAD:]

    for i in range(PLANES):
        part = slice(i * CY, (i + 1) * CY)
        for t in range(TRACERS):
            lo, hi = t * PAD, (t + 1) * PAD
            down = d0[lo:hi, part] + direct[t][:, part]
            if first:
                out_ref[i, lo:hi, :] = base_ref[i, lo:hi, :] + step_size * down
            else:
                out_ref[i, lo:hi, :] = down
        if first:
            x = x0 + i
            edge_plane(
                x, out_ref[i], mask_ref[pl.ds(x, 1), :].astype(F32), None, fy_ref[pl.ds(x, 1), :], ew_ref, ee_ref
            )

    if first:

        @pl.when(block == 0)
        def _():
            en_ref[...] = north_edge(out_ref[0], mask_ref[0:1, :].astype(F32), fx_ref[0:1, :])

    @pl.when(block == CX // PLANES - 1)
    def _():
        if first:
            es_ref[...] = south_edge(out_ref[PLANES - 1], mask_ref[CX - 1 :, :].astype(F32), fx_ref[CX - 1 :, :])
            grads_ref[...] = total[...]
        else:
            grads_ref[: 2 * HID, :] = total[:, :128]
            grads_ref[2 * HID :, :] = total[:, 128:]


def closure(first, owners, mask, got, lam, split_weights, b2, b3, *extra):
    whole = pl.BlockSpec(memory_space=pltpu.VMEM)
    planes = pl.BlockSpec((PLANES, FEATS, CY), lambda b: (b, 0, 0))
    in_specs = [whole, whole, whole, planes] + [whole] * 8
    if first:
        in_specs += [whole, whole, planes]
        out_shape = (PLANE, jax.ShapeDtypeStruct((2 * HID, HID), F32), EDGE, EDGE, EDGE, EDGE)
        out_specs = (planes,) + (whole,) * 5
    else:
        in_specs += [whole]
        out_shape = (PLANE, jax.ShapeDtypeStruct((4 * HID, 128), F32))
        out_specs = (planes, whole)
    return pl.pallas_call(
        functools.partial(closure_kernel, first),
        grid=(CX // PLANES,),
        out_shape=out_shape,
        in_specs=in_specs,
        out_specs=out_specs,
        scratch_shapes=[pltpu.VMEM((FEATS, STORE), BF), pltpu.VMEM((2 * HID, HID), F32)],
        compiler_params=PARAMS,
        name="closure1" if first else "closure0",
    )(owners, mask, got, lam, *split_weights, b2, b3, *extra)


def sum_kernel(parts_ref, out_ref):
    value = parts_ref[0:8, :]
    for i in range(1, DEV):
        value = value + parts_ref[8 * i : 8 * i + 8, :]
    for i in range(DEV):
        out_ref[8 * i : 8 * i + 8, :] = value


def unpack_kernel(scale, sums_ref, w1_ref, b1_ref, w2_ref, b2_ref, w3t_ref, b3_ref):
    for part in range(2):
        lanes = slice(part * 128, (part + 1) * 128)
        top = part * 2 * HID
        for t in range(TRACERS):
            w1_ref[t * NZ : (t + 1) * NZ, lanes] = sums_ref[top + t * PAD : top + t * PAD + NZ, :] * scale
        b1_ref[:, lanes] = sums_ref[top + NZ : top + NZ + 1, :] * scale
        b2_ref[:, lanes] = sums_ref[top + NZ + 1 : top + NZ + 2, :] * scale
        w2_ref[:, lanes] = sums_ref[top + FEATS : top + FEATS + HID, :] * scale
        w3t_ref[:, lanes] = sums_ref[top + FEATS + HID : top + FEATS + HID + NZ, :] * scale
    b3_ref[...] = sums_ref[NZ + 2 : NZ + 3, :NZ] * scale


def reduce_params(packed, count):
    parts = lax.all_to_all(packed, ("gx", "gy"), split_axis=0, concat_axis=0, tiled=True)
    spread = pl.pallas_call(
        sum_kernel, out_shape=jax.ShapeDtypeStruct(packed.shape, F32), compiler_params=PARAMS, name="sum"
    )(parts)
    sums = lax.all_to_all(spread, ("gx", "gy"), split_axis=0, concat_axis=0, tiled=True)
    shapes = ((TRACERS * NZ, HID), (1, HID), (HID, HID), (1, HID), (NZ, HID), (1, NZ))
    return pl.pallas_call(
        functools.partial(unpack_kernel, step_size / float(np.sqrt(count))),
        out_shape=tuple(jax.ShapeDtypeStruct(s, F32) for s in shapes),
        compiler_params=PARAMS,
        name="unpack",
    )(sums)


def exchange(north, south, west, east):
    gx, gy = lax.axis_size("gx"), lax.axis_size("gy")
    down_x = [(i + 1, i) for i in range(gx - 1)]
    up_x = [(i, i + 1) for i in range(gx - 1)]
    down_y = [(i + 1, i) for i in range(gy - 1)]
    up_y = [(i, i + 1) for i in range(gy - 1)]
    return (
        lax.ppermute(north, "gx", down_x),
        lax.ppermute(south, "gx", up_x),
        lax.ppermute(west, "gy", down_y),
        lax.ppermute(east, "gy", up_y),
    )


def on_device(
    stored,
    counts,
    owners,
    land_mask,
    flow_x,
    flow_y,
    costate,
    weight_in,
    bias_in,
    weight_mid,
    bias_mid,
    weight_out,
    bias_out,
):
    stored_t = stored[0].T
    late = pack(1, counts, stored_t)
    stored_t, costate, weight_mid, late = lax.optimization_barrier((stored_t, costate, weight_mid, late))
    late = lax.all_to_all(late, ("gx", "gy"), split_axis=0, concat_axis=0, tiled=True)
    early = pack(0, counts, stored_t)
    split_weights = weights(weight_in, bias_in[None, :], weight_mid, weight_out.T)
    b2 = bias_mid[:, None]
    b3 = jnp.pad(bias_out, (0, PAD - NZ))[:, None]
    planes, *sides = edges(costate.reshape(TRACERS * NZ * CX, CY), land_mask, flow_x, flow_y)
    halos = exchange(*sides)
    base = first_stencil(planes, land_mask, flow_x, flow_y, halos)
    early, base, split_weights = lax.optimization_barrier((early, base, split_weights))
    early = lax.all_to_all(early, ("gx", "gy"), split_axis=0, concat_axis=0, tiled=True)
    lam, grads, *sides = closure(
        True, owners, land_mask, late, planes, split_weights, b2, b3, flow_x, flow_y, base
    )
    halos = exchange(*sides)
    down, packed = closure(False, owners, land_mask, early, lam, split_weights, b2, b3, grads)
    adjoint = last_stencil(lam, down, land_mask, flow_x, flow_y, halos)
    count = CX * CY * lax.axis_size("gx") * lax.axis_size("gy")
    g1, gb1, g2, gb2, g3, gb3 = reduce_params(packed, count)
    return (adjoint.reshape(costate.shape), g1, gb1[0], g2, gb2[0], g3.T, gb3[0])


def solution(mesh):
    in_specs = (
        P(("gx", "gy"), None, None),
        P(("gx", "gy"), None),
        P("gx", "gy"),
        P("gx", "gy"),
        P("gx", "gy"),
        P("gx", "gy"),
        P(None, None, "gx", "gy"),
        P(),
        P(),
        P(),
        P(),
        P(),
        P(),
    )
    out_specs = (P(None, None, "gx", "gy"), P(), P(), P(), P(), P(), P())
    return jax.shard_map(
        on_device, mesh=mesh, in_specs=in_specs, out_specs=out_specs, check_vma=False
    )
```

```python
import functools

import jax
import jax.numpy as jnp
import numpy as np
from jax import lax
from jax.experimental import pallas as pl
from jax.experimental.pallas import tpu as pltpu
from jax.sharding import PartitionSpec as P

NZ = 60
TRACERS = 3
PAD = 64
FEATS = TRACERS * PAD
HID = 256
SLOT = 32
HALF = SLOT // 2
CX = 16
CY = 128
DEV = 128
STORE = 4096
UNROLL = 8
COLS = CX * CY

CLOSURE_MIB = 24

BF = jnp.bfloat16
F32 = jnp.float32
NT = (((1,), (1,)), ((), ()))

step_size = 0.25
flat_mix = 0.25
kappa_top = 1.5


def split(value):
    high = value.astype(BF)
    return high, (value - high.astype(F32)).astype(BF)


def dot(left, right):
    return jnp.dot(left, right, preferred_element_type=F32)


def dot_nt(left, right):
    return lax.dot_general(left, right, NT, preferred_element_type=F32)


def params(mib):
    return pltpu.CompilerParams(vmem_limit_bytes=mib * 2**20)


def near_shape(*shape, dtype=F32):
    return pltpu.VMEM(shape, dtype)


def call(kernel, name, out_shape, args, scratch=(), mib=4):
    args = [pltpu.with_memory_space_constraint(a, pltpu.VMEM) for a in args]
    return pl.pallas_call(
        kernel,
        out_shape=out_shape,
        in_specs=[pl.BlockSpec(memory_space=pltpu.VMEM)] * len(args),
        scratch_shapes=list(scratch),
        compiler_params=params(mib),
        name=name,
    )(*args)


def pack_kernel(moment, counts_ref, stored_ref, out_ref, near, padded, sem):
    top = moment * TRACERS * NZ // 8 * 8
    copy = pltpu.make_async_copy(stored_ref.at[top : top + near.shape[0], :], near, sem)
    copy.start()
    lane = lax.broadcasted_iota(jnp.int32, (SLOT, 256), 1)
    offset = lane - lax.broadcasted_iota(jnp.int32, (SLOT, 256), 0)
    for t in range(TRACERS):
        padded[t * PAD + NZ : (t + 1) * PAD, :] = jnp.zeros((PAD - NZ, STORE), BF)
    copy.wait()
    skip = moment * TRACERS * NZ - top
    for t in range(TRACERS):
        padded[t * PAD : t * PAD + NZ, :] = near[skip + t * NZ : skip + (t + 1) * NZ, :]

    def group(g, start):
        base = pl.multiple_of(jnp.minimum((start // 128) * 128, STORE - 256), 128)
        hots = []
        for i in range(4):
            hots.append(jnp.where(offset == start - base, 1.0, 0.0).astype(BF))
            start = start + counts_ref[0, 4 * g + i]
        rows = dot_nt(jnp.concatenate(hots, axis=0), padded[:, pl.ds(base, 256)])
        for i in range(4):
            mine = rows[i * SLOT : (i + 1) * SLOT]
            rest = jnp.concatenate([mine[:HALF, 2 * PAD :], mine[HALF:, 2 * PAD :]], axis=1)
            out_ref[4 * g + i, :SLOT, :] = mine[:, : 2 * PAD].astype(BF)
            out_ref[4 * g + i, SLOT:, :] = rest.astype(BF)
        return start

    def groups(j, start):
        for u in range(UNROLL):
            start = group(j * UNROLL + u, start)
        return start

    lax.fori_loop(0, DEV // 4 // UNROLL, groups, jnp.int32(0))


def pack(moment, counts, stored_t):
    return pl.pallas_call(
        functools.partial(pack_kernel, moment),
        out_shape=pltpu.HBM((DEV, SLOT + HALF, 128), BF),
        in_specs=[pl.BlockSpec(memory_space=pltpu.SMEM), pl.BlockSpec(memory_space=pl.ANY)],
        out_specs=pl.BlockSpec(memory_space=pltpu.VMEM),
        scratch_shapes=[
            pltpu.VMEM((TRACERS * NZ + 4, STORE), BF),
            pltpu.VMEM((FEATS, STORE), BF),
            pltpu.SemaphoreType.DMA,
        ],
        compiler_params=params(8),
        name=f"pack{moment}",
    )(*(pltpu.with_memory_space_constraint(a, pltpu.HBM) for a in (counts, stored_t)))


def weights_kernel(w1_ref, b1_ref, w2_ref, b2_ref, w3t_ref, b3_ref, *refs):
    f1_ref, f2_ref, f3_ref, r3_ref, r2_ref, r1_ref, c2_ref, c3_ref, wide, tall = refs
    wide[...] = jnp.zeros_like(wide)
    for t in range(TRACERS):
        wide[t * PAD : t * PAD + NZ, :] = w1_ref[t * NZ : (t + 1) * NZ, :]
    high, low = split(wide[...])
    r1_ref[:FEATS, :] = high
    r1_ref[FEATS:, :] = low
    wide[NZ : NZ + 1, :] = b1_ref[...]
    high, low = split(wide[...].T)
    f1_ref[:HID, :] = high
    f1_ref[HID:, :] = low
    high, low = split(w2_ref[...])
    r2_ref[:HID, :] = high
    r2_ref[HID:, :] = low
    high, low = split(w2_ref[...].T)
    f2_ref[:HID, :] = high
    f2_ref[HID:, :] = low
    tall[...] = jnp.zeros_like(tall)
    tall[:NZ, :] = w3t_ref[...]
    high, low = split(tall[:PAD, :])
    f3_ref[:PAD, :] = high
    f3_ref[PAD:, :] = low
    tall[PAD : 2 * PAD, :] = tall[:PAD, :]
    tall[2 * PAD :, :] = tall[:PAD, :]
    high, low = split(tall[...].T)
    lane = lax.broadcasted_iota(jnp.int32, high.shape, 1)
    middle = (lane >= PAD) & (lane < 2 * PAD)
    r3_ref[...] = jnp.where(middle, low.astype(F32), high.astype(F32)).astype(BF)
    c2_ref[...] = jnp.broadcast_to(b2_ref[...], (8, HID)).T[:, :1]
    c3_ref[...] = jnp.zeros_like(c3_ref)
    c3_ref[:NZ, :] = jnp.broadcast_to(b3_ref[...], (8, NZ)).T[:, :1]


def weights(*args):
    shapes = ((2 * HID, FEATS), (2 * HID, HID), (2 * PAD, HID), (HID, FEATS), (2 * HID, HID), (2 * FEATS, HID))
    outs = tuple(near_shape(*shape, dtype=BF) for shape in shapes) + (near_shape(HID, 1), near_shape(PAD, 1))
    scratch = [pltpu.VMEM((FEATS, HID), F32), pltpu.VMEM((FEATS, HID), F32)]
    return call(weights_kernel, "weights", outs, args, scratch)


def edge_plane(x, plane, mask_row, fy_row, ew_ref, ee_ref):
    weighted = plane * mask_row
    lane = lax.broadcasted_iota(jnp.int32, plane.shape, 1)
    west = pltpu.roll(weighted * (flat_mix + 0.5 * fy_row), x, 1)
    east = pltpu.roll(weighted * (flat_mix - 0.5 * fy_row), x + 1, 1)
    ew_ref[...] = jnp.where(lane == x, west, ew_ref[...])
    ee_ref[...] = jnp.where(lane == x, east, ee_ref[...])


def north_edge(plane, mask_row, fx_row):
    return plane * mask_row * (flat_mix + 0.5 * fx_row)


def south_edge(plane, mask_row, fx_row):
    return plane * mask_row * (flat_mix - 0.5 * fx_row)


def edges_kernel(raw_ref, mask_ref, fx_ref, fy_ref, planes_ref, en_ref, es_ref, ew_ref, ee_ref):
    planes_ref[...] = jnp.zeros_like(planes_ref)
    ew_ref[...] = jnp.zeros_like(ew_ref)
    ee_ref[...] = jnp.zeros_like(ee_ref)
    for x in range(CX):
        for t in range(TRACERS):
            planes_ref[x, t * PAD : t * PAD + NZ, :] = raw_ref[pl.ds(t * NZ * CX + x, NZ, stride=CX), :]
        mask_row = mask_ref[x : x + 1, :].astype(F32)
        edge_plane(x, planes_ref[x], mask_row, fy_ref[x : x + 1, :], ew_ref, ee_ref)
    en_ref[...] = north_edge(planes_ref[0], mask_ref[0:1, :].astype(F32), fx_ref[0:1, :])
    es_ref[...] = south_edge(planes_ref[CX - 1], mask_ref[CX - 1 :, :].astype(F32), fx_ref[CX - 1 :, :])


EDGE = near_shape(FEATS, CY)
PLANE = near_shape(CX, FEATS, CY)


def edges(*args):
    return call(edges_kernel, "edges", (PLANE, EDGE, EDGE, EDGE, EDGE), args)


def stencil_plane(x, lam_ref, mask_ref, fx_ref, fy_ref, hn_ref, hs_ref, hw_ref, he_ref):
    def row(ref, at):
        return ref[at : at + 1, :].astype(F32)

    plane = lam_ref[x]
    weighted = plane * row(mask_ref, x)
    if x < CX - 1:
        total = north_edge(lam_ref[x + 1], row(mask_ref, x + 1), row(fx_ref, x + 1))
    else:
        total = hn_ref[...]
    if x > 0:
        total = total + south_edge(lam_ref[x - 1], row(mask_ref, x - 1), row(fx_ref, x - 1))
    else:
        total = total + hs_ref[...]
    lane = lax.broadcasted_iota(jnp.int32, plane.shape, 1)
    fy = row(fy_ref, x)
    west = pltpu.roll(weighted * (flat_mix + 0.5 * fy), CY - 1, 1)
    total = total + jnp.where(lane == CY - 1, pltpu.roll(hw_ref[...], CY - 1 - x, 1), west)
    east = pltpu.roll(weighted * (flat_mix - 0.5 * fy), 1, 1)
    from_east = he_ref[...] if x == 0 else pltpu.roll(he_ref[...], CY - x, 1)
    total = total + jnp.where(lane == 0, from_east, east)
    return plane, total - weighted


def first_kernel(lam_ref, mask_ref, fx_ref, fy_ref, hn_ref, hs_ref, hw_ref, he_ref, out_ref):
    for x in range(CX):
        plane, total = stencil_plane(x, lam_ref, mask_ref, fx_ref, fy_ref, hn_ref, hs_ref, hw_ref, he_ref)
        out_ref[x] = plane + step_size * total


def first_stencil(lam, mask, fx, fy, halos):
    return call(first_kernel, "stencil1", PLANE, (lam, mask, fx, fy, *halos))


def last_kernel(lam_ref, down_ref, mask_ref, fx_ref, fy_ref, hn_ref, hs_ref, hw_ref, he_ref, out_ref):
    for x in range(CX):
        plane, total = stencil_plane(x, lam_ref, mask_ref, fx_ref, fy_ref, hn_ref, hs_ref, hw_ref, he_ref)
        value = plane + step_size * (total + down_ref[x])
        for t in range(TRACERS):
            out_ref[pl.ds(t * NZ * CX + x, NZ, stride=CX), :] = value[t * PAD : t * PAD + NZ]


def last_stencil(lam, down, mask, fx, fy, halos):
    out = jax.ShapeDtypeStruct((TRACERS * NZ * CX, CY), F32)
    return call(last_kernel, "stencil0", out, (lam, down, mask, fx, fy, *halos))


def closure_kernel(first, *refs):
    (owner_ref, mask_ref, got_ref, lam_ref, f1_ref, f2_ref, f3_ref, r3_ref, r2_ref, r1_ref, b2_ref, b3_ref) = refs[:12]
    refs = refs[12:]
    if first:
        fx_ref, fy_ref, base_ref, out_ref, grads_ref, en_ref, es_ref, ew_ref, ee_ref = refs[:9]
        refs = refs[9:]
    else:
        before_ref, out_ref, grads_ref = refs[:3]
        refs = refs[3:]
    rows_ref, total = refs
    for half in range(2):
        for g in range(DEV // 8):
            at = half * (STORE // 2) + g * 128
            main = [got_ref[8 * g + i, half * HALF : (half + 1) * HALF, :] for i in range(8)]
            rows_ref[: 2 * PAD, at : at + 128] = jnp.concatenate(main, axis=0).T
    for g in range(DEV // 8):
        rest = [got_ref[8 * g + i, SLOT:, :] for i in range(8)]
        both = jnp.concatenate(rest, axis=0).T
        rows_ref[2 * PAD :, g * 128 : (g + 1) * 128] = both[:PAD]
        at = STORE // 2 + g * 128
        rows_ref[2 * PAD :, at : at + 128] = both[PAD:]
    if first:
        total[...] = jnp.zeros_like(total)
        ew_ref[...] = jnp.zeros_like(ew_ref)
        ee_ref[...] = jnp.zeros_like(ee_ref)
    else:
        total[...] = before_ref[...]

    def wide(ref):
        return jnp.concatenate([ref[i : i + 1, :] for i in range(CX)], axis=1)

    owner = wide(owner_ref)
    at = ((owner >> 4) & 1) * (STORE // 2) + (owner >> 5) * HALF + (owner & (HALF - 1))
    level = lax.broadcasted_iota(jnp.int32, (256, COLS), 0)
    picked = None
    for k in range(STORE // 256):
        hot = jnp.where(level == at - 256 * k, 1.0, 0.0).astype(BF)
        part = dot(rows_ref[:, 256 * k : 256 * (k + 1)], hot)
        picked = part if picked is None else picked + part
    row = lax.broadcasted_iota(jnp.int32, (FEATS, COLS), 0)
    inputs = jnp.where(row == NZ, 1.0, picked).astype(BF)

    both = dot(f1_ref[...], inputs)
    h1 = jnp.tanh(both[:HID] + both[HID:])
    h1_high, h1_low = split(h1)
    both = dot(f2_ref[...], h1_high)
    h2 = jnp.tanh(both[:HID] + both[HID:] + dot(f2_ref[:HID], h1_low) + b2_ref[...])
    h2_high, h2_low = split(h2)
    both = dot(f3_ref[...], h2_high)
    sig = jax.nn.sigmoid(both[:PAD] + both[PAD:] + dot(f3_ref[:PAD], h2_low) + b3_ref[...])
    inner = lax.broadcasted_iota(jnp.int32, (PAD, COLS), 0) < NZ - 1
    kappa = jnp.where(inner, kappa_top * sig, 0.0)

    mask_row = wide(mask_ref).astype(F32)
    slope = jnp.zeros((PAD, COLS), F32)
    direct = []
    for t in range(TRACERS):
        lo, hi = t * PAD, (t + 1) * PAD
        mu = jnp.concatenate([lam_ref[i, lo:hi, :] for i in range(CX)], axis=1) * mask_row
        gap = mu - pltpu.roll(mu, PAD - 1, 0)
        column = picked[lo:hi]
        slope = slope + gap * (pltpu.roll(column, PAD - 1, 0) - column)
        flow = kappa * gap
        direct.append(pltpu.roll(flow, 1, 0) - flow)
    d3 = slope * kappa * (1.0 - sig)
    d3_high, d3_low = split(d3)
    d2 = dot(r3_ref[...], jnp.concatenate([d3_high, d3_high, d3_low], axis=0)) * (1.0 - h2 * h2)
    d2_high, d2_low = split(d2)
    both = dot(r2_ref[...], d2_high)
    d1 = (both[:HID] + both[HID:] + dot(r2_ref[:HID], d2_low)) * (1.0 - h1 * h1)
    d1_high, d1_low = split(d1)
    both = dot(r1_ref[...], d1_high)
    d0 = both[:FEATS] + both[FEATS:] + dot(r1_ref[:FEATS], d1_low)

    ones = jnp.ones((16, COLS), BF)
    total[:FEATS, :] += dot_nt(inputs, d1_high) + dot_nt(inputs, d1_low)
    both = dot_nt(jnp.concatenate([h1_high, h1_low, ones], axis=0), d2_high)
    other = dot_nt(jnp.concatenate([h1_high, ones], axis=0), d2_low)
    total[FEATS : FEATS + HID, :] += both[:HID] + both[HID : 2 * HID] + other[:HID]
    total[NZ + 1 : NZ + 2, :] += both[2 * HID : 2 * HID + 1] + other[HID : HID + 1]
    d3_both = jnp.concatenate([d3_high, d3_low], axis=0)
    both = dot_nt(d3_both, h2_high)
    total[FEATS + HID :, :] += both[:PAD] + both[PAD:] + dot_nt(d3_high, h2_low)
    both = dot_nt(ones, d3_both)
    total[NZ + 2 : NZ + 3, :PAD] += both[:1, :PAD] + both[:1, PAD:]

    for i in range(CX):
        part = slice(i * CY, (i + 1) * CY)
        for t in range(TRACERS):
            lo, hi = t * PAD, (t + 1) * PAD
            down = d0[lo:hi, part] + direct[t][:, part]
            if first:
                out_ref[i, lo:hi, :] = base_ref[i, lo:hi, :] + step_size * down
            else:
                out_ref[i, lo:hi, :] = down
        if first:
            edge_plane(i, out_ref[i], mask_ref[i : i + 1, :].astype(F32), fy_ref[i : i + 1, :], ew_ref, ee_ref)
    if first:
        en_ref[...] = north_edge(out_ref[0], mask_ref[0:1, :].astype(F32), fx_ref[0:1, :])
        es_ref[...] = south_edge(out_ref[CX - 1], mask_ref[CX - 1 :, :].astype(F32), fx_ref[CX - 1 :, :])
        grads_ref[...] = total[...]
    else:
        grads_ref[: 2 * HID, :] = total[:, :128]
        grads_ref[2 * HID :, :] = total[:, 128:]


def closure(first, owners, mask, got, lam, split_weights, *extra):
    if first:
        out_shape = (PLANE, near_shape(2 * HID, HID), EDGE, EDGE, EDGE, EDGE)
    else:
        out_shape = (PLANE, near_shape(4 * HID, 128))
    return call(
        functools.partial(closure_kernel, first),
        "closure1" if first else "closure0",
        out_shape,
        (owners, mask, got, lam, *split_weights, *extra),
        [pltpu.VMEM((FEATS, STORE), BF), pltpu.VMEM((2 * HID, HID), F32)],
        CLOSURE_MIB,
    )


def sum_kernel(parts_ref, out_ref):
    value = parts_ref[0:8, :]
    for i in range(1, DEV):
        value = value + parts_ref[8 * i : 8 * i + 8, :]
    for i in range(DEV):
        out_ref[8 * i : 8 * i + 8, :] = value


def unpack_kernel(scale, sums_ref, w1_ref, b1_ref, w2_ref, b2_ref, w3t_ref, b3_ref):
    for part in range(2):
        lanes = slice(part * 128, (part + 1) * 128)
        top = part * 2 * HID
        for t in range(TRACERS):
            w1_ref[t * NZ : (t + 1) * NZ, lanes] = sums_ref[top + t * PAD : top + t * PAD + NZ, :] * scale
        b1_ref[:, lanes] = sums_ref[top + NZ : top + NZ + 1, :] * scale
        b2_ref[:, lanes] = sums_ref[top + NZ + 1 : top + NZ + 2, :] * scale
        w2_ref[:, lanes] = sums_ref[top + FEATS : top + FEATS + HID, :] * scale
        w3t_ref[:, lanes] = sums_ref[top + FEATS + HID : top + FEATS + HID + NZ, :] * scale
    b3_ref[...] = sums_ref[NZ + 2 : NZ + 3, :NZ] * scale


def reduce_params(packed, count, halos):
    parts = lax.all_to_all(packed, ("gx", "gy"), split_axis=0, concat_axis=0, tiled=True)
    parts, _ = lax.optimization_barrier((parts, halos))
    spread = call(sum_kernel, "sum", near_shape(*packed.shape), (parts,))
    sums = lax.all_to_all(spread, ("gx", "gy"), split_axis=0, concat_axis=0, tiled=True)
    shapes = ((TRACERS * NZ, HID), (1, HID), (HID, HID), (1, HID), (NZ, HID), (1, NZ))
    scale = step_size / float(np.sqrt(count))
    outs = tuple(jax.ShapeDtypeStruct(shape, F32) for shape in shapes)
    return call(functools.partial(unpack_kernel, scale), "unpack", outs, (sums,))


def exchange(north, south, west, east):
    gx, gy = lax.axis_size("gx"), lax.axis_size("gy")
    down_x = [(i + 1, i) for i in range(gx - 1)]
    up_x = [(i, i + 1) for i in range(gx - 1)]
    down_y = [(i + 1, i) for i in range(gy - 1)]
    up_y = [(i, i + 1) for i in range(gy - 1)]
    return (
        lax.ppermute(north, "gx", down_x),
        lax.ppermute(south, "gx", up_x),
        lax.ppermute(west, "gy", down_y),
        lax.ppermute(east, "gy", up_y),
    )


def on_device(
    stored,
    counts,
    owners,
    land_mask,
    flow_x,
    flow_y,
    costate,
    weight_in,
    bias_in,
    weight_mid,
    bias_mid,
    weight_out,
    bias_out,
):
    stored_t = stored[0].T
    late = pack(1, counts, stored_t)
    stored_t, late = lax.optimization_barrier((stored_t, late))
    late = lax.all_to_all(late, ("gx", "gy"), split_axis=0, concat_axis=0, tiled=True)
    early = pack(0, counts, stored_t)
    costate, weight_mid, early = lax.optimization_barrier((costate, weight_mid, early))
    early = lax.all_to_all(early, ("gx", "gy"), split_axis=0, concat_axis=0, tiled=True)
    split_weights = weights(
        weight_in, bias_in[None, :], weight_mid, bias_mid[None, :], weight_out.T, bias_out[None, :]
    )
    planes, *sides = edges(costate.reshape(TRACERS * NZ * CX, CY), land_mask, flow_x, flow_y)
    halos = exchange(*sides)
    base = first_stencil(planes, land_mask, flow_x, flow_y, halos)
    lam, grads, *sides = closure(True, owners, land_mask, late, planes, split_weights, flow_x, flow_y, base)
    down, packed = closure(False, owners, land_mask, early, lam, split_weights, grads)
    *sides, packed = lax.optimization_barrier((*sides, packed))
    halos = exchange(*sides)
    adjoint = last_stencil(lam, down, land_mask, flow_x, flow_y, halos)
    count = CX * CY * lax.axis_size("gx") * lax.axis_size("gy")
    g1, gb1, g2, gb2, g3, gb3 = reduce_params(packed, count, halos)
    return (adjoint.reshape(costate.shape), g1, gb1[0], g2, gb2[0], g3.T, gb3[0])


def solution(mesh):
    in_specs = (
        P(("gx", "gy"), None, None),
        P(("gx", "gy"), None),
        P("gx", "gy"),
        P("gx", "gy"),
        P("gx", "gy"),
        P("gx", "gy"),
        P(None, None, "gx", "gy"),
        P(),
        P(),
        P(),
        P(),
        P(),
        P(),
    )
    out_specs = (P(None, None, "gx", "gy"), P(), P(), P(), P(), P(), P())
    return jax.shard_map(
        on_device, mesh=mesh, in_specs=in_specs, out_specs=out_specs, check_vma=False
    )
```

```python
import functools

import jax
import jax.numpy as jnp
import numpy as np
from jax import lax
from jax.experimental import pallas as pl
from jax.experimental.pallas import tpu as pltpu
from jax.sharding import PartitionSpec as P

NZ = 60
TRACERS = 3
PAD = 64
FEATS = TRACERS * PAD
HID = 256
SLOT = 32
HALF = SLOT // 2
BLOCK = SLOT + HALF
CX = 16
CY = 128
DEV = 128
STORE = 4096
UNROLL = 8
COLS = CX * CY

CLOSURE_MIB = 24

BF = jnp.bfloat16
F32 = jnp.float32
NT = (((1,), (1,)), ((), ()))

step_size = 0.25
flat_mix = 0.25
kappa_top = 1.5


def split(value):
    high = value.astype(BF)
    return high, (value - high.astype(F32)).astype(BF)


def dot(left, right):
    return jnp.dot(left, right, preferred_element_type=F32)


def dot_nt(left, right):
    return lax.dot_general(left, right, NT, preferred_element_type=F32)


def params(mib):
    return pltpu.CompilerParams(vmem_limit_bytes=mib * 2**20)


def near_shape(*shape, dtype=F32):
    return pltpu.VMEM(shape, dtype)


def call(kernel, name, out_shape, args, scratch=(), mib=4):
    args = [pltpu.with_memory_space_constraint(a, pltpu.VMEM) for a in args]
    return pl.pallas_call(
        kernel,
        out_shape=out_shape,
        in_specs=[pl.BlockSpec(memory_space=pltpu.VMEM)] * len(args),
        scratch_shapes=list(scratch),
        compiler_params=params(mib),
        name=name,
    )(*args)


def pack_kernel(counts_ref, stored_ref, out_ref, near, padded, rows_out, in_sems, out_sem):
    cut = (FEATS - TRACERS * (PAD - NZ) + 7) // 8 * 8
    parts = (slice(0, cut), slice(cut, 2 * TRACERS * NZ))
    copies = [pltpu.make_async_copy(stored_ref.at[p, :], near.at[p, :], in_sems.at[i]) for i, p in enumerate(parts)]
    for copy in copies:
        copy.start()
    lane = lax.broadcasted_iota(jnp.int32, (SLOT, 256), 1)
    offset = lane - lax.broadcasted_iota(jnp.int32, (SLOT, 256), 0)
    for block in range(2 * TRACERS):
        padded[block * PAD + NZ : (block + 1) * PAD, :] = jnp.zeros((PAD - NZ, STORE), BF)
    for moment in range(2):
        copies[moment].wait()
        for block in range(moment * TRACERS, (moment + 1) * TRACERS):
            padded[block * PAD : block * PAD + NZ, :] = near[block * NZ : (block + 1) * NZ, :]

    def group(g, start):
        base = pl.multiple_of(jnp.minimum((start // 128) * 128, STORE - 256), 128)
        hots = []
        for i in range(4):
            hots.append(jnp.where(offset == start - base, 1.0, 0.0).astype(BF))
            start = start + counts_ref[0, 4 * g + i]
        rows = dot_nt(jnp.concatenate(hots, axis=0), padded[:, pl.ds(base, 256)])
        for i in range(4):
            for moment in range(2):
                at, first = moment * BLOCK, moment * FEATS
                mine = rows[i * SLOT : (i + 1) * SLOT, first : first + FEATS]
                rest = jnp.concatenate([mine[:HALF, 2 * PAD :], mine[HALF:, 2 * PAD :]], axis=1)
                rows_out[4 * g + i, at : at + SLOT, :] = mine[:, : 2 * PAD].astype(BF)
                rows_out[4 * g + i, at + SLOT : at + BLOCK, :] = rest.astype(BF)
        return start

    def leave(j):
        tiles = pl.ds(j * 4 * UNROLL, 4 * UNROLL)
        return pltpu.make_async_copy(rows_out.at[tiles], out_ref.at[tiles], out_sem.at[j])

    start = jnp.int32(0)
    steps = DEV // 4 // UNROLL

    def groups(j, start):
        for u in range(UNROLL):
            start = group(j * UNROLL + u, start)
        leave(j).start()
        return start

    lax.fori_loop(0, steps, groups, start)
    for j in range(steps):
        leave(j).wait()


def pack(counts, stored_t):
    anywhere = pl.BlockSpec(memory_space=pl.ANY)
    return pl.pallas_call(
        pack_kernel,
        out_shape=pltpu.HBM((DEV, 2 * BLOCK, 128), BF),
        in_specs=[pl.BlockSpec(memory_space=pltpu.SMEM), anywhere],
        out_specs=anywhere,
        scratch_shapes=[
            pltpu.VMEM((2 * TRACERS * NZ, STORE), BF),
            pltpu.VMEM((2 * FEATS, STORE), BF),
            pltpu.VMEM((DEV, 2 * BLOCK, 128), BF),
            pltpu.SemaphoreType.DMA((2,)),
            pltpu.SemaphoreType.DMA((DEV // 4 // UNROLL,)),
        ],
        compiler_params=params(24),
        name="pack",
    )(*(pltpu.with_memory_space_constraint(a, pltpu.HBM) for a in (counts, stored_t)))


def weights_kernel(w1_ref, b1_ref, w2_ref, b2_ref, w3t_ref, b3_ref, *refs):
    f1_ref, f2_ref, f3_ref, r3_ref, r2_ref, r1_ref, c2_ref, c3_ref, wide, tall = refs
    wide[...] = jnp.zeros_like(wide)
    for t in range(TRACERS):
        wide[t * PAD : t * PAD + NZ, :] = w1_ref[t * NZ : (t + 1) * NZ, :]
    high, low = split(wide[...])
    r1_ref[:FEATS, :] = high
    r1_ref[FEATS:, :] = low
    wide[NZ : NZ + 1, :] = b1_ref[...]
    high, low = split(wide[...].T)
    f1_ref[:HID, :] = high
    f1_ref[HID:, :] = low
    high, low = split(w2_ref[...])
    r2_ref[:HID, :] = high
    r2_ref[HID:, :] = low
    high, low = split(w2_ref[...].T)
    f2_ref[:HID, :] = high
    f2_ref[HID:, :] = low
    tall[...] = jnp.zeros_like(tall)
    tall[:NZ, :] = w3t_ref[...]
    high, low = split(tall[:PAD, :])
    f3_ref[:PAD, :] = high
    f3_ref[PAD:, :] = low
    tall[PAD : 2 * PAD, :] = tall[:PAD, :]
    tall[2 * PAD :, :] = tall[:PAD, :]
    high, low = split(tall[...].T)
    lane = lax.broadcasted_iota(jnp.int32, high.shape, 1)
    middle = (lane >= PAD) & (lane < 2 * PAD)
    r3_ref[...] = jnp.where(middle, low.astype(F32), high.astype(F32)).astype(BF)
    c2_ref[...] = jnp.broadcast_to(b2_ref[...], (8, HID)).T[:, :1]
    c3_ref[...] = jnp.zeros_like(c3_ref)
    c3_ref[:NZ, :] = jnp.broadcast_to(b3_ref[...], (8, NZ)).T[:, :1]


def weights(*args):
    shapes = ((2 * HID, FEATS), (2 * HID, HID), (2 * PAD, HID), (HID, FEATS), (2 * HID, HID), (2 * FEATS, HID))
    outs = tuple(near_shape(*shape, dtype=BF) for shape in shapes) + (near_shape(HID, 1), near_shape(PAD, 1))
    scratch = [pltpu.VMEM((FEATS, HID), F32), pltpu.VMEM((FEATS, HID), F32)]
    return call(weights_kernel, "weights", outs, args, scratch)


def edge_plane(x, plane, mask_row, fy_row, ew_ref, ee_ref):
    weighted = plane * mask_row
    lane = lax.broadcasted_iota(jnp.int32, plane.shape, 1)
    west = pltpu.roll(weighted * (flat_mix + 0.5 * fy_row), x, 1)
    east = pltpu.roll(weighted * (flat_mix - 0.5 * fy_row), x + 1, 1)
    ew_ref[...] = jnp.where(lane == x, west, ew_ref[...])
    ee_ref[...] = jnp.where(lane == x, east, ee_ref[...])


def north_edge(plane, mask_row, fx_row):
    return plane * mask_row * (flat_mix + 0.5 * fx_row)


def south_edge(plane, mask_row, fx_row):
    return plane * mask_row * (flat_mix - 0.5 * fx_row)


def edges_kernel(raw_ref, mask_ref, fx_ref, fy_ref, planes_ref, en_ref, es_ref, ew_ref, ee_ref):
    planes_ref[...] = jnp.zeros_like(planes_ref)
    ew_ref[...] = jnp.zeros_like(ew_ref)
    ee_ref[...] = jnp.zeros_like(ee_ref)
    for x in range(CX):
        for t in range(TRACERS):
            planes_ref[x, t * PAD : t * PAD + NZ, :] = raw_ref[pl.ds(t * NZ * CX + x, NZ, stride=CX), :]
        mask_row = mask_ref[x : x + 1, :].astype(F32)
        edge_plane(x, planes_ref[x], mask_row, fy_ref[x : x + 1, :], ew_ref, ee_ref)
    en_ref[...] = north_edge(planes_ref[0], mask_ref[0:1, :].astype(F32), fx_ref[0:1, :])
    es_ref[...] = south_edge(planes_ref[CX - 1], mask_ref[CX - 1 :, :].astype(F32), fx_ref[CX - 1 :, :])


EDGE = near_shape(FEATS, CY)
PLANE = near_shape(CX, FEATS, CY)


def edges(*args):
    return call(edges_kernel, "edges", (PLANE, EDGE, EDGE, EDGE, EDGE), args)


def stencil_plane(x, lam_ref, mask_ref, fx_ref, fy_ref, hn_ref, hs_ref, hw_ref, he_ref):
    def row(ref, at):
        return ref[at : at + 1, :].astype(F32)

    plane = lam_ref[x]
    weighted = plane * row(mask_ref, x)
    if x < CX - 1:
        total = north_edge(lam_ref[x + 1], row(mask_ref, x + 1), row(fx_ref, x + 1))
    else:
        total = hn_ref[...]
    if x > 0:
        total = total + south_edge(lam_ref[x - 1], row(mask_ref, x - 1), row(fx_ref, x - 1))
    else:
        total = total + hs_ref[...]
    lane = lax.broadcasted_iota(jnp.int32, plane.shape, 1)
    fy = row(fy_ref, x)
    west = pltpu.roll(weighted * (flat_mix + 0.5 * fy), CY - 1, 1)
    total = total + jnp.where(lane == CY - 1, pltpu.roll(hw_ref[...], CY - 1 - x, 1), west)
    east = pltpu.roll(weighted * (flat_mix - 0.5 * fy), 1, 1)
    from_east = he_ref[...] if x == 0 else pltpu.roll(he_ref[...], CY - x, 1)
    total = total + jnp.where(lane == 0, from_east, east)
    return plane, total - weighted


def first_kernel(lam_ref, mask_ref, fx_ref, fy_ref, hn_ref, hs_ref, hw_ref, he_ref, out_ref):
    for x in range(CX):
        plane, total = stencil_plane(x, lam_ref, mask_ref, fx_ref, fy_ref, hn_ref, hs_ref, hw_ref, he_ref)
        out_ref[x] = plane + step_size * total


def first_stencil(lam, mask, fx, fy, halos):
    return call(first_kernel, "stencil1", PLANE, (lam, mask, fx, fy, *halos))


def last_kernel(lam_ref, down_ref, mask_ref, fx_ref, fy_ref, hn_ref, hs_ref, hw_ref, he_ref, out_ref):
    for x in range(CX):
        plane, total = stencil_plane(x, lam_ref, mask_ref, fx_ref, fy_ref, hn_ref, hs_ref, hw_ref, he_ref)
        value = plane + step_size * (total + down_ref[x])
        for t in range(TRACERS):
            out_ref[pl.ds(t * NZ * CX + x, NZ, stride=CX), :] = value[t * PAD : t * PAD + NZ]


def last_stencil(lam, down, mask, fx, fy, halos):
    out = jax.ShapeDtypeStruct((TRACERS * NZ * CX, CY), F32)
    return call(last_kernel, "stencil0", out, (lam, down, mask, fx, fy, *halos))


def closure_step(first, got_ref, owner_ref, mask_ref, lam_ref, weight_refs, base_ref, out_ref, rows_ref, total):
    f1_ref, f2_ref, f3_ref, r3_ref, r2_ref, r1_ref, b2_ref, b3_ref = weight_refs
    for half in range(2):
        for g in range(DEV // 8):
            at = half * (STORE // 2) + g * 128
            lo = first + half * HALF
            main = [got_ref[8 * g + i, lo : lo + HALF, :] for i in range(8)]
            rows_ref[: 2 * PAD, at : at + 128] = jnp.concatenate(main, axis=0).T
    for g in range(DEV // 8):
        rest = [got_ref[8 * g + i, first + SLOT : first + BLOCK, :] for i in range(8)]
        both = jnp.concatenate(rest, axis=0).T
        rows_ref[2 * PAD :, g * 128 : (g + 1) * 128] = both[:PAD]
        at = STORE // 2 + g * 128
        rows_ref[2 * PAD :, at : at + 128] = both[PAD:]

    def wide(ref):
        return jnp.concatenate([ref[i : i + 1, :] for i in range(CX)], axis=1)

    owner = wide(owner_ref)
    at = ((owner >> 4) & 1) * (STORE // 2) + (owner >> 5) * HALF + (owner & (HALF - 1))
    level = lax.broadcasted_iota(jnp.int32, (256, COLS), 0)
    picked = None
    for k in range(STORE // 256):
        hot = jnp.where(level == at - 256 * k, 1.0, 0.0).astype(BF)
        part = dot(rows_ref[:, 256 * k : 256 * (k + 1)], hot)
        picked = part if picked is None else picked + part
    row = lax.broadcasted_iota(jnp.int32, (FEATS, COLS), 0)
    inputs = jnp.where(row == NZ, 1.0, picked).astype(BF)

    both = dot(f1_ref[...], inputs)
    h1 = jnp.tanh(both[:HID] + both[HID:])
    h1_high, h1_low = split(h1)
    both = dot(f2_ref[...], h1_high)
    h2 = jnp.tanh(both[:HID] + both[HID:] + dot(f2_ref[:HID], h1_low) + b2_ref[...])
    h2_high, h2_low = split(h2)
    both = dot(f3_ref[...], h2_high)
    sig = jax.nn.sigmoid(both[:PAD] + both[PAD:] + dot(f3_ref[:PAD], h2_low) + b3_ref[...])
    inner = lax.broadcasted_iota(jnp.int32, (PAD, COLS), 0) < NZ - 1
    kappa = jnp.where(inner, kappa_top * sig, 0.0)

    mask_row = wide(mask_ref).astype(F32)
    slope = jnp.zeros((PAD, COLS), F32)
    direct = []
    for t in range(TRACERS):
        lo, hi = t * PAD, (t + 1) * PAD
        mu = jnp.concatenate([lam_ref[i, lo:hi, :] for i in range(CX)], axis=1) * mask_row
        gap = mu - pltpu.roll(mu, PAD - 1, 0)
        column = picked[lo:hi]
        slope = slope + gap * (pltpu.roll(column, PAD - 1, 0) - column)
        flow = kappa * gap
        direct.append(pltpu.roll(flow, 1, 0) - flow)
    d3 = slope * kappa * (1.0 - sig)
    d3_high, d3_low = split(d3)
    d2 = dot(r3_ref[...], jnp.concatenate([d3_high, d3_high, d3_low], axis=0)) * (1.0 - h2 * h2)
    d2_high, d2_low = split(d2)
    both = dot(r2_ref[...], d2_high)
    d1 = (both[:HID] + both[HID:] + dot(r2_ref[:HID], d2_low)) * (1.0 - h1 * h1)
    d1_high, d1_low = split(d1)
    both = dot(r1_ref[...], d1_high)
    d0 = both[:FEATS] + both[FEATS:] + dot(r1_ref[:FEATS], d1_low)

    ones = jnp.ones((16, COLS), BF)
    total[:FEATS, :] += dot_nt(inputs, d1_high) + dot_nt(inputs, d1_low)
    both = dot_nt(jnp.concatenate([h1_high, h1_low, ones], axis=0), d2_high)
    other = dot_nt(jnp.concatenate([h1_high, ones], axis=0), d2_low)
    total[FEATS : FEATS + HID, :] += both[:HID] + both[HID : 2 * HID] + other[:HID]
    total[NZ + 1 : NZ + 2, :] += both[2 * HID : 2 * HID + 1] + other[HID : HID + 1]
    d3_both = jnp.concatenate([d3_high, d3_low], axis=0)
    both = dot_nt(d3_both, h2_high)
    total[FEATS + HID :, :] += both[:PAD] + both[PAD:] + dot_nt(d3_high, h2_low)
    both = dot_nt(ones, d3_both)
    total[NZ + 2 : NZ + 3, :PAD] += both[:1, :PAD] + both[:1, PAD:]

    for i in range(CX):
        part = slice(i * CY, (i + 1) * CY)
        for t in range(TRACERS):
            lo, hi = t * PAD, (t + 1) * PAD
            down = d0[lo:hi, part] + direct[t][:, part]
            if base_ref is not None:
                out_ref[i, lo:hi, :] = base_ref[i, lo:hi, :] + step_size * down
            else:
                out_ref[i, lo:hi, :] = down


def closure_kernel(got_ref, owner_ref, mask_ref, fx_ref, fy_ref, planes_ref, base_ref, *refs):
    weight_refs, refs = refs[:8], refs[8:]
    lam_ref, down_ref, grads_ref, en_ref, es_ref, ew_ref, ee_ref, late_ref, early_ref, total = refs
    total[...] = jnp.zeros_like(total)
    ew_ref[...] = jnp.zeros_like(ew_ref)
    ee_ref[...] = jnp.zeros_like(ee_ref)
    step = functools.partial(closure_step, got_ref=got_ref, owner_ref=owner_ref, mask_ref=mask_ref, total=total)
    step(BLOCK, lam_ref=planes_ref, weight_refs=weight_refs, base_ref=base_ref, out_ref=lam_ref, rows_ref=late_ref)
    for x in range(CX):
        edge_plane(x, lam_ref[x], mask_ref[x : x + 1, :].astype(F32), fy_ref[x : x + 1, :], ew_ref, ee_ref)
    en_ref[...] = north_edge(lam_ref[0], mask_ref[0:1, :].astype(F32), fx_ref[0:1, :])
    es_ref[...] = south_edge(lam_ref[CX - 1], mask_ref[CX - 1 :, :].astype(F32), fx_ref[CX - 1 :, :])
    step(0, lam_ref=lam_ref, weight_refs=weight_refs, base_ref=None, out_ref=down_ref, rows_ref=early_ref)
    grads_ref[: 2 * HID, :] = total[:, :128]
    grads_ref[2 * HID :, :] = total[:, 128:]


def closure(*args):
    outs = (PLANE, PLANE, near_shape(4 * HID, 128), EDGE, EDGE, EDGE, EDGE)
    rows = pltpu.VMEM((FEATS, STORE), BF)
    scratch = [rows, rows, pltpu.VMEM((2 * HID, HID), F32)]
    return call(closure_kernel, "closure", outs, args, scratch, CLOSURE_MIB)


def sum_kernel(parts_ref, out_ref):
    value = parts_ref[0:8, :]
    for i in range(1, DEV):
        value = value + parts_ref[8 * i : 8 * i + 8, :]
    for i in range(DEV):
        out_ref[8 * i : 8 * i + 8, :] = value


def unpack_kernel(scale, sums_ref, w1_ref, b1_ref, w2_ref, b2_ref, w3t_ref, b3_ref):
    for part in range(2):
        lanes = slice(part * 128, (part + 1) * 128)
        top = part * 2 * HID
        for t in range(TRACERS):
            w1_ref[t * NZ : (t + 1) * NZ, lanes] = sums_ref[top + t * PAD : top + t * PAD + NZ, :] * scale
        b1_ref[:, lanes] = sums_ref[top + NZ : top + NZ + 1, :] * scale
        b2_ref[:, lanes] = sums_ref[top + NZ + 1 : top + NZ + 2, :] * scale
        w2_ref[:, lanes] = sums_ref[top + FEATS : top + FEATS + HID, :] * scale
        w3t_ref[:, lanes] = sums_ref[top + FEATS + HID : top + FEATS + HID + NZ, :] * scale
    b3_ref[...] = sums_ref[NZ + 2 : NZ + 3, :NZ] * scale


def reduce_params(packed, tied):
    parts = lax.all_to_all(packed, ("gx", "gy"), split_axis=0, concat_axis=0, tiled=True)
    parts, _ = lax.optimization_barrier((parts, tied))
    spread = call(sum_kernel, "sum", near_shape(*packed.shape), (parts,))
    return spread


def finish_params(spread, count):
    sums = lax.all_to_all(spread, ("gx", "gy"), split_axis=0, concat_axis=0, tiled=True)
    shapes = ((TRACERS * NZ, HID), (1, HID), (HID, HID), (1, HID), (NZ, HID), (1, NZ))
    scale = step_size / float(np.sqrt(count))
    outs = tuple(jax.ShapeDtypeStruct(shape, F32) for shape in shapes)
    return call(functools.partial(unpack_kernel, scale), "unpack", outs, (sums,))


def exchange(axis, before, after):
    up = [(i, i + 1) for i in range(lax.axis_size(axis) - 1)]
    down = [(j, i) for i, j in up]
    return lax.ppermute(before, axis, down), lax.ppermute(after, axis, up)


def on_device(
    stored,
    counts,
    owners,
    land_mask,
    flow_x,
    flow_y,
    costate,
    weight_in,
    bias_in,
    weight_mid,
    bias_mid,
    weight_out,
    bias_out,
):
    payload = pack(counts, stored[0].T)
    costate, weight_mid, payload = lax.optimization_barrier((costate, weight_mid, payload))
    got = lax.all_to_all(payload, ("gx", "gy"), split_axis=0, concat_axis=0, tiled=True)
    split_weights = weights(
        weight_in, bias_in[None, :], weight_mid, bias_mid[None, :], weight_out.T, bias_out[None, :]
    )
    planes, north, south, west, east = edges(
        costate.reshape(TRACERS * NZ * CX, CY), land_mask, flow_x, flow_y
    )
    halos = exchange("gx", north, south) + exchange("gy", west, east)
    base = first_stencil(planes, land_mask, flow_x, flow_y, halos)
    lam, down, packed, north, south, west, east = closure(
        got, owners, land_mask, flow_x, flow_y, planes, base, *split_weights
    )
    halos_x = exchange("gx", north, south)
    spread = reduce_params(packed, halos_x)
    west, east, spread = lax.optimization_barrier((west, east, spread))
    halos_y = exchange("gy", west, east)
    adjoint = last_stencil(lam, down, land_mask, flow_x, flow_y, halos_x + halos_y)
    count = CX * CY * lax.axis_size("gx") * lax.axis_size("gy")
    g1, gb1, g2, gb2, g3, gb3 = finish_params(spread, count)
    return (adjoint.reshape(costate.shape), g1, gb1[0], g2, gb2[0], g3.T, gb3[0])


def solution(mesh):
    in_specs = (
        P(("gx", "gy"), None, None),
        P(("gx", "gy"), None),
        P("gx", "gy"),
        P("gx", "gy"),
        P("gx", "gy"),
        P("gx", "gy"),
        P(None, None, "gx", "gy"),
        P(),
        P(),
        P(),
        P(),
        P(),
        P(),
    )
    out_specs = (P(None, None, "gx", "gy"), P(), P(), P(), P(), P(), P())
    return jax.shard_map(
        on_device, mesh=mesh, in_specs=in_specs, out_specs=out_specs, check_vma=False
    )
```

```python
import functools

import jax
import jax.numpy as jnp
import numpy as np
from jax import lax
from jax.experimental import pallas as pl
from jax.experimental.pallas import tpu as pltpu
from jax.sharding import PartitionSpec as P

NZ = 60
TRACERS = 3
PAD = 64
FEATS = TRACERS * PAD
HID = 256
SLOT = 32
HALF = SLOT // 2
BLOCK = SLOT + HALF
CX = 16
CY = 128
DEV = 128
STORE = 4096
UNROLL = 8
COLS = CX * CY

CLOSURE_MIB = 24

BF = jnp.bfloat16
F32 = jnp.float32
NT = (((1,), (1,)), ((), ()))

step_size = 0.25
flat_mix = 0.25
kappa_top = 1.5


def split(value):
    high = value.astype(BF)
    return high, (value - high.astype(F32)).astype(BF)


def dot(left, right):
    return jnp.dot(left, right, preferred_element_type=F32)


def dot_nt(left, right):
    return lax.dot_general(left, right, NT, preferred_element_type=F32)


def params(mib):
    return pltpu.CompilerParams(vmem_limit_bytes=mib * 2**20)


def near(*shape, dtype=F32):
    return pltpu.VMEM(shape, dtype)


def far(*shape, dtype=F32):
    return pltpu.HBM(shape, dtype)


def call(kernel, name, outs, args, copied=(), scratch=(), mib=4):
    args = [pltpu.with_memory_space_constraint(a, pltpu.VMEM) for a in args]
    copied = [pltpu.with_memory_space_constraint(a, pltpu.HBM) for a in copied]
    inside = pl.BlockSpec(memory_space=pltpu.VMEM)
    anywhere = pl.BlockSpec(memory_space=pl.ANY)
    return pl.pallas_call(
        kernel,
        out_shape=tuple(out[0] if isinstance(out, list) else out for out in outs),
        in_specs=[inside] * len(args) + [anywhere] * len(copied),
        out_specs=tuple(anywhere if isinstance(out, list) else inside for out in outs),
        scratch_shapes=list(scratch),
        compiler_params=params(mib),
        name=name,
    )(*args, *copied)


def pack_kernel(counts_ref, stored_ref, out_ref, near, padded, rows_out, in_sems, out_sem):
    cut = (FEATS - TRACERS * (PAD - NZ) + 7) // 8 * 8
    parts = (slice(0, cut), slice(cut, 2 * TRACERS * NZ))
    copies = [pltpu.make_async_copy(stored_ref.at[p, :], near.at[p, :], in_sems.at[i]) for i, p in enumerate(parts)]
    for copy in copies:
        copy.start()
    lane = lax.broadcasted_iota(jnp.int32, (SLOT, 256), 1)
    offset = lane - lax.broadcasted_iota(jnp.int32, (SLOT, 256), 0)
    for block in range(2 * TRACERS):
        padded[block * PAD + NZ : (block + 1) * PAD, :] = jnp.zeros((PAD - NZ, STORE), BF)
    for moment in range(2):
        copies[moment].wait()
        for block in range(moment * TRACERS, (moment + 1) * TRACERS):
            padded[block * PAD : block * PAD + NZ, :] = near[block * NZ : (block + 1) * NZ, :]

    def group(g, start):
        base = pl.multiple_of(jnp.minimum((start // 128) * 128, STORE - 256), 128)
        hots = []
        for i in range(4):
            hots.append(jnp.where(offset == start - base, 1.0, 0.0).astype(BF))
            start = start + counts_ref[0, 4 * g + i]
        rows = dot_nt(jnp.concatenate(hots, axis=0), padded[:, pl.ds(base, 256)])
        for i in range(4):
            for moment in range(2):
                at, first = moment * BLOCK, moment * FEATS
                mine = rows[i * SLOT : (i + 1) * SLOT, first : first + FEATS]
                rest = jnp.concatenate([mine[:HALF, 2 * PAD :], mine[HALF:, 2 * PAD :]], axis=1)
                rows_out[4 * g + i, at : at + SLOT, :] = mine[:, : 2 * PAD].astype(BF)
                rows_out[4 * g + i, at + SLOT : at + BLOCK, :] = rest.astype(BF)
        return start

    def leave(j):
        tiles = pl.ds(j * 4 * UNROLL, 4 * UNROLL)
        return pltpu.make_async_copy(rows_out.at[tiles], out_ref.at[tiles], out_sem.at[j])

    start = jnp.int32(0)
    steps = DEV // 4 // UNROLL

    def groups(j, start):
        for u in range(UNROLL):
            start = group(j * UNROLL + u, start)
        leave(j).start()
        return start

    lax.fori_loop(0, steps, groups, start)
    for j in range(steps):
        leave(j).wait()


def pack(counts, stored_t):
    anywhere = pl.BlockSpec(memory_space=pl.ANY)
    return pl.pallas_call(
        pack_kernel,
        out_shape=pltpu.HBM((DEV, 2 * BLOCK, 128), BF),
        in_specs=[pl.BlockSpec(memory_space=pltpu.SMEM), anywhere],
        out_specs=anywhere,
        scratch_shapes=[
            pltpu.VMEM((2 * TRACERS * NZ, STORE), BF),
            pltpu.VMEM((2 * FEATS, STORE), BF),
            pltpu.VMEM((DEV, 2 * BLOCK, 128), BF),
            pltpu.SemaphoreType.DMA((2,)),
            pltpu.SemaphoreType.DMA((DEV // 4 // UNROLL,)),
        ],
        compiler_params=params(24),
        name="pack",
    )(*(pltpu.with_memory_space_constraint(a, pltpu.HBM) for a in (counts, stored_t)))


def weights_kernel(w1_ref, b1_ref, w2_ref, b2_ref, w3t_ref, b3_ref, *refs):
    f1_ref, f2_ref, f3_ref, r3_ref, r2_ref, r1_ref, c2_ref, c3_ref, wide, tall = refs
    wide[...] = jnp.zeros_like(wide)
    for t in range(TRACERS):
        wide[t * PAD : t * PAD + NZ, :] = w1_ref[t * NZ : (t + 1) * NZ, :]
    high, low = split(wide[...])
    r1_ref[:FEATS, :] = high
    r1_ref[FEATS:, :] = low
    wide[NZ : NZ + 1, :] = b1_ref[...]
    high, low = split(wide[...].T)
    f1_ref[:HID, :] = high
    f1_ref[HID:, :] = low
    high, low = split(w2_ref[...])
    r2_ref[:HID, :] = high
    r2_ref[HID:, :] = low
    high, low = split(w2_ref[...].T)
    f2_ref[:HID, :] = high
    f2_ref[HID:, :] = low
    tall[...] = jnp.zeros_like(tall)
    tall[:NZ, :] = w3t_ref[...]
    high, low = split(tall[:PAD, :])
    f3_ref[:PAD, :] = high
    f3_ref[PAD:, :] = low
    tall[PAD : 2 * PAD, :] = tall[:PAD, :]
    tall[2 * PAD :, :] = tall[:PAD, :]
    high, low = split(tall[...].T)
    lane = lax.broadcasted_iota(jnp.int32, high.shape, 1)
    middle = (lane >= PAD) & (lane < 2 * PAD)
    r3_ref[...] = jnp.where(middle, low.astype(F32), high.astype(F32)).astype(BF)
    c2_ref[...] = jnp.broadcast_to(b2_ref[...], (8, HID)).T[:, :1]
    c3_ref[...] = jnp.zeros_like(c3_ref)
    c3_ref[:NZ, :] = jnp.broadcast_to(b3_ref[...], (8, NZ)).T[:, :1]


WEIGHTS = ((2 * HID, FEATS), (2 * HID, HID), (2 * PAD, HID), (HID, FEATS), (2 * HID, HID), (2 * FEATS, HID))


def weights(*args):
    outs = tuple(far(*shape, dtype=BF) for shape in WEIGHTS) + (far(HID, 1), far(PAD, 1))
    return call(weights_kernel, "weights", outs, args, scratch=[near(FEATS, HID), near(FEATS, HID)])


def edge_plane(x, plane, mask_row, fy_row, ew_ref, ee_ref):
    weighted = plane * mask_row
    lane = lax.broadcasted_iota(jnp.int32, plane.shape, 1)
    west = pltpu.roll(weighted * (flat_mix + 0.5 * fy_row), x, 1)
    east = pltpu.roll(weighted * (flat_mix - 0.5 * fy_row), x + 1, 1)
    ew_ref[...] = jnp.where(lane == x, west, ew_ref[...])
    ee_ref[...] = jnp.where(lane == x, east, ee_ref[...])


def north_edge(plane, mask_row, fx_row):
    return plane * mask_row * (flat_mix + 0.5 * fx_row)


def south_edge(plane, mask_row, fx_row):
    return plane * mask_row * (flat_mix - 0.5 * fx_row)


def row(ref, x):
    return ref[x : x + 1, :].astype(F32)


def local_plane(x, lam_ref, mask_ref, fx_ref, fy_ref):
    weighted = lam_ref[x] * row(mask_ref, x)
    lane = lax.broadcasted_iota(jnp.int32, weighted.shape, 1)
    fy = row(fy_ref, x)
    west = pltpu.roll(weighted * (flat_mix + 0.5 * fy), CY - 1, 1)
    east = pltpu.roll(weighted * (flat_mix - 0.5 * fy), 1, 1)
    total = jnp.where(lane == CY - 1, 0.0, west) + jnp.where(lane == 0, 0.0, east) - weighted
    if x < CX - 1:
        total = total + north_edge(lam_ref[x + 1], row(mask_ref, x + 1), row(fx_ref, x + 1))
    if x > 0:
        total = total + south_edge(lam_ref[x - 1], row(mask_ref, x - 1), row(fx_ref, x - 1))
    return total


def halo_plane(x, hn_ref, hs_ref, hw_ref, he_ref):
    lane = lax.broadcasted_iota(jnp.int32, hn_ref.shape, 1)
    total = jnp.where(lane == CY - 1, pltpu.roll(hw_ref[...], CY - 1 - x, 1), 0.0)
    east = he_ref[...] if x == 0 else pltpu.roll(he_ref[...], CY - x, 1)
    total = total + jnp.where(lane == 0, east, 0.0)
    if x == 0:
        total = total + hs_ref[...]
    if x == CX - 1:
        total = total + hn_ref[...]
    return total


def put_edges(lam_ref, mask_ref, fx_ref, fy_ref, en_ref, es_ref, ew_ref, ee_ref):
    ew_ref[...] = jnp.zeros_like(ew_ref)
    ee_ref[...] = jnp.zeros_like(ee_ref)
    for x in range(CX):
        edge_plane(x, lam_ref[x], row(mask_ref, x), row(fy_ref, x), ew_ref, ee_ref)
    en_ref[...] = north_edge(lam_ref[0], row(mask_ref, 0), row(fx_ref, 0))
    es_ref[...] = south_edge(lam_ref[CX - 1], row(mask_ref, CX - 1), row(fx_ref, CX - 1))


def edges_kernel(raw_ref, mask_ref, fx_ref, fy_ref, planes_ref, base_ref, en_ref, es_ref, ew_ref, ee_ref):
    planes_ref[...] = jnp.zeros_like(planes_ref)
    for x in range(CX):
        for t in range(TRACERS):
            planes_ref[x, t * PAD : t * PAD + NZ, :] = raw_ref[pl.ds(t * NZ * CX + x, NZ, stride=CX), :]
    put_edges(planes_ref, mask_ref, fx_ref, fy_ref, en_ref, es_ref, ew_ref, ee_ref)
    for x in range(CX):
        base_ref[x] = planes_ref[x] + step_size * local_plane(x, planes_ref, mask_ref, fx_ref, fy_ref)


EDGE = far(FEATS, CY)
PLANE = (CX, FEATS, CY)


def edges(*args):
    return call(edges_kernel, "edges", (far(*PLANE), far(*PLANE), EDGE, EDGE, EDGE, EDGE), args)


def last_kernel(mask_ref, fx_ref, fy_ref, hn_ref, hs_ref, hw_ref, he_ref, lam_far, down_far, out_ref, lam, down, sems):
    copies = [
        pltpu.make_async_copy(lam_far, lam, sems.at[0]),
        pltpu.make_async_copy(down_far, down, sems.at[1]),
    ]
    for copy in copies:
        copy.start()
    for copy in copies:
        copy.wait()
    for x in range(CX):
        total = local_plane(x, lam, mask_ref, fx_ref, fy_ref) + halo_plane(x, hn_ref, hs_ref, hw_ref, he_ref)
        value = lam[x] + step_size * (total + down[x])
        for t in range(TRACERS):
            out_ref[pl.ds(t * NZ * CX + x, NZ, stride=CX), :] = value[t * PAD : t * PAD + NZ]


def last_stencil(lam, down, *args):
    scratch = [near(*PLANE), near(*PLANE), pltpu.SemaphoreType.DMA((2,))]
    (out,) = call(last_kernel, "stencil0", (far(TRACERS * NZ * CX, CY),), args, (lam, down), scratch, mib=8)
    return out


def closure_step(first, got_ref, owner_ref, mask_ref, lam_ref, weight_refs, out_ref, rows_ref, total, wait):
    f1_ref, f2_ref, f3_ref, r3_ref, r2_ref, r1_ref, b2_ref, b3_ref = weight_refs
    for half in range(2):
        for g in range(DEV // 8):
            at = half * (STORE // 2) + g * 128
            lo = first + half * HALF
            main = [got_ref[8 * g + i, lo : lo + HALF, :] for i in range(8)]
            rows_ref[: 2 * PAD, at : at + 128] = jnp.concatenate(main, axis=0).T
    for g in range(DEV // 8):
        rest = [got_ref[8 * g + i, first + SLOT : first + BLOCK, :] for i in range(8)]
        both = jnp.concatenate(rest, axis=0).T
        rows_ref[2 * PAD :, g * 128 : (g + 1) * 128] = both[:PAD]
        at = STORE // 2 + g * 128
        rows_ref[2 * PAD :, at : at + 128] = both[PAD:]

    def wide(ref):
        return jnp.concatenate([ref[i : i + 1, :] for i in range(CX)], axis=1)

    owner = wide(owner_ref)
    at = ((owner >> 4) & 1) * (STORE // 2) + (owner >> 5) * HALF + (owner & (HALF - 1))
    level = lax.broadcasted_iota(jnp.int32, (256, COLS), 0)
    picked = None
    for k in range(STORE // 256):
        hot = jnp.where(level == at - 256 * k, 1.0, 0.0).astype(BF)
        part = dot(rows_ref[:, 256 * k : 256 * (k + 1)], hot)
        picked = part if picked is None else picked + part
    row = lax.broadcasted_iota(jnp.int32, (FEATS, COLS), 0)
    inputs = jnp.where(row == NZ, 1.0, picked).astype(BF)

    wait("weights")
    both = dot(f1_ref[...], inputs)
    h1 = jnp.tanh(both[:HID] + both[HID:])
    h1_high, h1_low = split(h1)
    both = dot(f2_ref[...], h1_high)
    h2 = jnp.tanh(both[:HID] + both[HID:] + dot(f2_ref[:HID], h1_low) + b2_ref[...])
    h2_high, h2_low = split(h2)
    both = dot(f3_ref[...], h2_high)
    sig = jax.nn.sigmoid(both[:PAD] + both[PAD:] + dot(f3_ref[:PAD], h2_low) + b3_ref[...])
    inner = lax.broadcasted_iota(jnp.int32, (PAD, COLS), 0) < NZ - 1
    kappa = jnp.where(inner, kappa_top * sig, 0.0)

    wait("lam")
    mask_row = wide(mask_ref).astype(F32)
    slope = jnp.zeros((PAD, COLS), F32)
    direct = []
    for t in range(TRACERS):
        lo, hi = t * PAD, (t + 1) * PAD
        mu = jnp.concatenate([lam_ref[i, lo:hi, :] for i in range(CX)], axis=1) * mask_row
        gap = mu - pltpu.roll(mu, PAD - 1, 0)
        column = picked[lo:hi]
        slope = slope + gap * (pltpu.roll(column, PAD - 1, 0) - column)
        flow = kappa * gap
        direct.append(pltpu.roll(flow, 1, 0) - flow)
    d3 = slope * kappa * (1.0 - sig)
    d3_high, d3_low = split(d3)
    d2 = dot(r3_ref[...], jnp.concatenate([d3_high, d3_high, d3_low], axis=0)) * (1.0 - h2 * h2)
    d2_high, d2_low = split(d2)
    both = dot(r2_ref[...], d2_high)
    d1 = (both[:HID] + both[HID:] + dot(r2_ref[:HID], d2_low)) * (1.0 - h1 * h1)
    d1_high, d1_low = split(d1)
    both = dot(r1_ref[...], d1_high)
    d0 = both[:FEATS] + both[FEATS:] + dot(r1_ref[:FEATS], d1_low)

    for i in range(CX):
        part = slice(i * CY, (i + 1) * CY)
        for t in range(TRACERS):
            lo, hi = t * PAD, (t + 1) * PAD
            out_ref[i, lo:hi, :] = d0[lo:hi, part] + direct[t][:, part]
    wait("out")

    ones = jnp.ones((16, COLS), BF)
    total[:FEATS, :] += dot_nt(inputs, d1_high) + dot_nt(inputs, d1_low)
    both = dot_nt(jnp.concatenate([h1_high, h1_low, ones], axis=0), d2_high)
    other = dot_nt(jnp.concatenate([h1_high, ones], axis=0), d2_low)
    total[FEATS : FEATS + HID, :] += both[:HID] + both[HID : 2 * HID] + other[:HID]
    total[NZ + 1 : NZ + 2, :] += both[2 * HID : 2 * HID + 1] + other[HID : HID + 1]
    d3_both = jnp.concatenate([d3_high, d3_low], axis=0)
    both = dot_nt(d3_both, h2_high)
    total[FEATS + HID :, :] += both[:PAD] + both[PAD:] + dot_nt(d3_high, h2_low)
    both = dot_nt(ones, d3_both)
    total[NZ + 2 : NZ + 3, :PAD] += both[:1, :PAD] + both[:1, PAD:]


def bring(refs, copies, sems):
    started = {}
    for i, (name, source, target) in enumerate(copies):
        started.setdefault(name, []).append(pltpu.make_async_copy(source, target, sems.at[i]))
        started[name][-1].start()

    def wait(name):
        for copy in started.pop(name, ()):
            copy.wait()

    return wait


def late_kernel(got_ref, owner_ref, mask_ref, *refs):
    sources, (out_ref, total), refs = refs[:10], refs[10:12], refs[12:]
    targets, (rows_ref, down, sems) = refs[:10], refs[10:]
    names = ("weights",) * 8 + ("lam", "base")
    wait = bring(refs, zip(names, sources, targets), sems)
    planes, base = targets[8:]
    total[...] = jnp.zeros_like(total)

    def then(name):
        wait(name)
        if name == "out":
            wait("base")
            for x in range(CX):
                out_ref[x] = base[x] + step_size * down[x]

    closure_step(BLOCK, got_ref, owner_ref, mask_ref, planes, targets[:8], down, rows_ref, total, then)


def early_kernel(got_ref, owner_ref, mask_ref, fx_ref, fy_ref, part_ref, before_ref, *refs):
    halos, sources, refs = refs[:4], refs[4:12], refs[12:]
    (lam_far, down_far, grads_ref), sides, refs = refs[:3], refs[3:7], refs[7:]
    targets, (rows_ref, lam, down, total, sems, out_sems) = refs[:8], refs[8:]
    wait = bring(refs, zip(("weights",) * 8, sources, targets), sems)
    for x in range(CX):
        lam[x] = part_ref[x] + step_size * halo_plane(x, *halos)
    lam_copy = pltpu.make_async_copy(lam, lam_far, out_sems.at[0])
    lam_copy.start()
    down_copy = pltpu.make_async_copy(down, down_far, out_sems.at[1])
    put_edges(lam, mask_ref, fx_ref, fy_ref, *sides)
    total[...] = before_ref[...]

    def then(name):
        wait(name)
        if name == "out":
            down_copy.start()

    closure_step(0, got_ref, owner_ref, mask_ref, lam, targets, down, rows_ref, total, then)
    grads_ref[: 2 * HID, :] = total[:, :128]
    grads_ref[2 * HID :, :] = total[:, 128:]
    lam_copy.wait()
    down_copy.wait()


WEIGHT_SCRATCH = [near(*shape, dtype=BF) for shape in WEIGHTS] + [near(HID, 1), near(PAD, 1)]
ROWS = near(FEATS, STORE, dtype=BF)
TOTAL = near(2 * HID, HID)


def late_closure(got, owners, mask, split_weights, planes, base):
    scratch = WEIGHT_SCRATCH + [near(*PLANE), near(*PLANE), ROWS, near(*PLANE), pltpu.SemaphoreType.DMA((10,))]
    copied = (*split_weights, planes, base)
    return call(late_kernel, "closure1", (near(*PLANE), TOTAL), (got, owners, mask), copied, scratch, CLOSURE_MIB)


def early_closure(got, owners, mask, fx, fy, part, before, halos, split_weights):
    outs = ([far(*PLANE)], [far(*PLANE)], far(4 * HID, 128), EDGE, EDGE, EDGE, EDGE)
    scratch = WEIGHT_SCRATCH + [ROWS, near(*PLANE), near(*PLANE), TOTAL]
    scratch += [pltpu.SemaphoreType.DMA((8,)), pltpu.SemaphoreType.DMA((2,))]
    args = (got, owners, mask, fx, fy, part, before, *halos)
    return call(early_kernel, "closure0", outs, args, split_weights, scratch, CLOSURE_MIB)


def sum_kernel(parts_ref, out_ref):
    value = parts_ref[0:8, :]
    for i in range(1, DEV):
        value = value + parts_ref[8 * i : 8 * i + 8, :]
    for i in range(DEV):
        out_ref[8 * i : 8 * i + 8, :] = value


def unpack_kernel(scale, sums_ref, w1_ref, b1_ref, w2_ref, b2_ref, w3t_ref, b3_ref):
    for part in range(2):
        lanes = slice(part * 128, (part + 1) * 128)
        top = part * 2 * HID
        for t in range(TRACERS):
            w1_ref[t * NZ : (t + 1) * NZ, lanes] = sums_ref[top + t * PAD : top + t * PAD + NZ, :] * scale
        b1_ref[:, lanes] = sums_ref[top + NZ : top + NZ + 1, :] * scale
        b2_ref[:, lanes] = sums_ref[top + NZ + 1 : top + NZ + 2, :] * scale
        w2_ref[:, lanes] = sums_ref[top + FEATS : top + FEATS + HID, :] * scale
        w3t_ref[:, lanes] = sums_ref[top + FEATS + HID : top + FEATS + HID + NZ, :] * scale
    b3_ref[...] = sums_ref[NZ + 2 : NZ + 3, :NZ] * scale


def reduce_params(packed, tied):
    parts = lax.all_to_all(packed, ("gx", "gy"), split_axis=0, concat_axis=0, tiled=True)
    parts, _ = lax.optimization_barrier((parts, tied))
    (spread,) = call(sum_kernel, "sum", (far(*packed.shape),), (parts,))
    return spread


def finish_params(spread, count):
    sums = lax.all_to_all(spread, ("gx", "gy"), split_axis=0, concat_axis=0, tiled=True)
    shapes = ((TRACERS * NZ, HID), (1, HID), (HID, HID), (1, HID), (NZ, HID), (1, NZ))
    scale = step_size / float(np.sqrt(count))
    outs = tuple(far(*shape) for shape in shapes)
    return call(functools.partial(unpack_kernel, scale), "unpack", outs, (sums,))


def exchange(axis, before, after):
    up = [(i, i + 1) for i in range(lax.axis_size(axis) - 1)]
    down = [(j, i) for i, j in up]
    return lax.ppermute(before, axis, down), lax.ppermute(after, axis, up)


def on_device(
    stored,
    counts,
    owners,
    land_mask,
    flow_x,
    flow_y,
    costate,
    weight_in,
    bias_in,
    weight_mid,
    bias_mid,
    weight_out,
    bias_out,
):
    payload = pack(counts, stored[0].T)
    costate, weight_mid, payload = lax.optimization_barrier((costate, weight_mid, payload))
    got = lax.all_to_all(payload, ("gx", "gy"), split_axis=0, concat_axis=0, tiled=True)
    split_weights = weights(
        weight_in, bias_in[None, :], weight_mid, bias_mid[None, :], weight_out.T, bias_out[None, :]
    )
    planes, base, north, south, west, east = edges(
        costate.reshape(TRACERS * NZ * CX, CY), land_mask, flow_x, flow_y
    )
    halos = exchange("gx", north, south) + exchange("gy", west, east)
    part, grads = late_closure(got, owners, land_mask, split_weights, planes, base)
    lam, down, packed, north, south, west, east = early_closure(
        got, owners, land_mask, flow_x, flow_y, part, grads, halos, split_weights
    )
    halos_x = exchange("gx", north, south)
    spread = reduce_params(packed, halos_x)
    west, east, spread = lax.optimization_barrier((west, east, spread))
    halos_y = exchange("gy", west, east)
    adjoint = last_stencil(lam, down, land_mask, flow_x, flow_y, *halos_x, *halos_y)
    count = CX * CY * lax.axis_size("gx") * lax.axis_size("gy")
    g1, gb1, g2, gb2, g3, gb3 = finish_params(spread, count)
    return (adjoint.reshape(costate.shape), g1, gb1[0], g2, gb2[0], g3.T, gb3[0])


def solution(mesh):
    in_specs = (
        P(("gx", "gy"), None, None),
        P(("gx", "gy"), None),
        P("gx", "gy"),
        P("gx", "gy"),
        P("gx", "gy"),
        P("gx", "gy"),
        P(None, None, "gx", "gy"),
        P(),
        P(),
        P(),
        P(),
        P(),
        P(),
    )
    out_specs = (P(None, None, "gx", "gy"), P(), P(), P(), P(), P(), P())
    return jax.shard_map(
        on_device, mesh=mesh, in_specs=in_specs, out_specs=out_specs, check_vma=False
    )
```

```python
import functools

import jax
import jax.numpy as jnp
import numpy as np
from jax import lax
from jax.experimental import pallas as pl
from jax.experimental.pallas import tpu as pltpu
from jax.sharding import PartitionSpec as P

NZ = 60
TRACERS = 3
PAD = 64
FEATS = TRACERS * PAD
HID = 256
SLOT = 32
HALF = SLOT // 2
BLOCK = SLOT + HALF
CX = 16
CY = 128
DEV = 128
STORE = 4096
UNROLL = 16
COLS = CX * CY

CLOSURE_MIB = 24

BF = jnp.bfloat16
F32 = jnp.float32
NT = (((1,), (1,)), ((), ()))

step_size = 0.25
flat_mix = 0.25
kappa_top = 1.5


def split(value):
    high = value.astype(BF)
    return high, (value - high.astype(F32)).astype(BF)


def dot(left, right):
    return jnp.dot(left, right, preferred_element_type=F32)


def dot_nt(left, right):
    return lax.dot_general(left, right, NT, preferred_element_type=F32)


def params(mib):
    return pltpu.CompilerParams(vmem_limit_bytes=mib * 2**20)


def bring(copies, sems):
    started = {}
    for i, (name, source, target) in enumerate(copies):
        started.setdefault(name, []).append(pltpu.make_async_copy(source, target, sems.at[i]))
        started[name][-1].start()

    def wait(name):
        for copy in started.pop(name, ()):
            copy.wait()

    return wait


def near(*shape, dtype=F32):
    return pltpu.VMEM(shape, dtype)


def far(*shape, dtype=F32):
    return pltpu.HBM(shape, dtype)


def call(kernel, name, outs, args, copied=(), scratch=(), mib=4, aliases={}):
    args = [pltpu.with_memory_space_constraint(a, pltpu.VMEM) for a in args]
    copied = [pltpu.with_memory_space_constraint(a, pltpu.HBM) for a in copied]
    inside = pl.BlockSpec(memory_space=pltpu.VMEM)
    anywhere = pl.BlockSpec(memory_space=pl.ANY)
    return pl.pallas_call(
        kernel,
        out_shape=tuple(out[0] if isinstance(out, list) else out for out in outs),
        in_specs=[inside] * len(args) + [anywhere] * len(copied),
        out_specs=tuple(anywhere if isinstance(out, list) else inside for out in outs),
        scratch_shapes=list(scratch),
        input_output_aliases=aliases,
        compiler_params=params(mib),
        name=name,
    )(*args, *copied)


def pack_kernel(counts_ref, stored_ref, out_ref, near, padded, rows_out, in_sems, out_sem):
    cut = (FEATS - TRACERS * (PAD - NZ) + 7) // 8 * 8
    parts = (slice(0, cut), slice(cut, 2 * TRACERS * NZ))
    copies = [pltpu.make_async_copy(stored_ref.at[p, :], near.at[p, :], in_sems.at[i]) for i, p in enumerate(parts)]
    for copy in copies:
        copy.start()
    lane = lax.broadcasted_iota(jnp.int32, (SLOT, 256), 1)
    offset = lane - lax.broadcasted_iota(jnp.int32, (SLOT, 256), 0)
    for block in range(2 * TRACERS):
        padded[block * PAD + NZ : (block + 1) * PAD, :] = jnp.zeros((PAD - NZ, STORE), BF)
    for moment in range(2):
        copies[moment].wait()
        for block in range(moment * TRACERS, (moment + 1) * TRACERS):
            padded[block * PAD : block * PAD + NZ, :] = near[block * NZ : (block + 1) * NZ, :]

    def group(g, start):
        base = pl.multiple_of(jnp.minimum((start // 128) * 128, STORE - 256), 128)
        hots = []
        for i in range(4):
            hots.append(jnp.where(offset == start - base, 1.0, 0.0).astype(BF))
            start = start + counts_ref[0, 4 * g + i]
        rows = dot_nt(jnp.concatenate(hots, axis=0), padded[:, pl.ds(base, 256)])
        for i in range(4):
            for moment in range(2):
                at, first = moment * BLOCK, moment * FEATS
                mine = rows[i * SLOT : (i + 1) * SLOT, first : first + FEATS]
                rest = jnp.concatenate([mine[:HALF, 2 * PAD :], mine[HALF:, 2 * PAD :]], axis=1)
                rows_out[4 * g + i, at : at + SLOT, :] = mine[:, : 2 * PAD].astype(BF)
                rows_out[4 * g + i, at + SLOT : at + BLOCK, :] = rest.astype(BF)
        return start

    def leave(j):
        tiles = pl.ds(j * 4 * UNROLL, 4 * UNROLL)
        return pltpu.make_async_copy(rows_out.at[tiles], out_ref.at[tiles], out_sem.at[j])

    start = jnp.int32(0)
    steps = DEV // 4 // UNROLL

    def groups(j, start):
        for u in range(UNROLL):
            start = group(j * UNROLL + u, start)
        leave(j).start()
        return start

    lax.fori_loop(0, steps, groups, start)
    for j in range(steps):
        leave(j).wait()


def pack(counts, stored_t):
    anywhere = pl.BlockSpec(memory_space=pl.ANY)
    return pl.pallas_call(
        pack_kernel,
        out_shape=pltpu.HBM((DEV, 2 * BLOCK, 128), BF),
        in_specs=[pl.BlockSpec(memory_space=pltpu.SMEM), anywhere],
        out_specs=anywhere,
        scratch_shapes=[
            pltpu.VMEM((2 * TRACERS * NZ, STORE), BF),
            pltpu.VMEM((2 * FEATS, STORE), BF),
            pltpu.VMEM((DEV, 2 * BLOCK, 128), BF),
            pltpu.SemaphoreType.DMA((2,)),
            pltpu.SemaphoreType.DMA((DEV // 4 // UNROLL,)),
        ],
        compiler_params=params(24),
        name="pack",
    )(*(pltpu.with_memory_space_constraint(a, pltpu.HBM) for a in (counts, stored_t)))


def weights_kernel(w1_ref, b1_ref, w2_ref, b2_ref, w3t_ref, b3_ref, *refs):
    f1_ref, f2_ref, f3_ref, r3_ref, r2_ref, r1_ref, c2_ref, c3_ref, wide, tall = refs
    wide[...] = jnp.zeros_like(wide)
    for t in range(TRACERS):
        wide[t * PAD : t * PAD + NZ, :] = w1_ref[t * NZ : (t + 1) * NZ, :]
    high, low = split(wide[...])
    r1_ref[:FEATS, :] = high
    r1_ref[FEATS:, :] = low
    wide[NZ : NZ + 1, :] = b1_ref[...]
    high, low = split(wide[...].T)
    f1_ref[:HID, :] = high
    f1_ref[HID:, :] = low
    high, low = split(w2_ref[...])
    r2_ref[:HID, :] = high
    r2_ref[HID:, :] = low
    high, low = split(w2_ref[...].T)
    f2_ref[:HID, :] = high
    f2_ref[HID:, :] = low
    tall[...] = jnp.zeros_like(tall)
    tall[:NZ, :] = w3t_ref[...]
    high, low = split(tall[:PAD, :])
    f3_ref[:PAD, :] = high
    f3_ref[PAD:, :] = low
    tall[PAD : 2 * PAD, :] = tall[:PAD, :]
    tall[2 * PAD :, :] = tall[:PAD, :]
    high, low = split(tall[...].T)
    lane = lax.broadcasted_iota(jnp.int32, high.shape, 1)
    middle = (lane >= PAD) & (lane < 2 * PAD)
    r3_ref[...] = jnp.where(middle, low.astype(F32), high.astype(F32)).astype(BF)
    c2_ref[...] = jnp.broadcast_to(b2_ref[...], (8, HID)).T[:, :1]
    c3_ref[...] = jnp.zeros_like(c3_ref)
    c3_ref[:NZ, :] = jnp.broadcast_to(b3_ref[...], (8, NZ)).T[:, :1]


WEIGHTS = ((2 * HID, FEATS), (2 * HID, HID), (2 * PAD, HID), (HID, FEATS), (2 * HID, HID), (2 * FEATS, HID))


def weights(*args):
    outs = tuple(far(*shape, dtype=BF) for shape in WEIGHTS) + (far(HID, 1), far(PAD, 1))
    return call(weights_kernel, "weights", outs, args, scratch=[near(FEATS, HID), near(FEATS, HID)])


def edge_plane(x, plane, mask_row, fy_row, ew_ref, ee_ref):
    weighted = plane * mask_row
    lane = lax.broadcasted_iota(jnp.int32, plane.shape, 1)
    west = pltpu.roll(weighted * (flat_mix + 0.5 * fy_row), x, 1)
    east = pltpu.roll(weighted * (flat_mix - 0.5 * fy_row), x + 1, 1)
    ew_ref[...] = jnp.where(lane == x, west, ew_ref[...])
    ee_ref[...] = jnp.where(lane == x, east, ee_ref[...])


def north_edge(plane, mask_row, fx_row):
    return plane * mask_row * (flat_mix + 0.5 * fx_row)


def south_edge(plane, mask_row, fx_row):
    return plane * mask_row * (flat_mix - 0.5 * fx_row)


def row(ref, x):
    return ref[x : x + 1, :].astype(F32)


def local_plane(x, lam_ref, mask_ref, fx_ref, fy_ref):
    weighted = lam_ref[x] * row(mask_ref, x)
    lane = lax.broadcasted_iota(jnp.int32, weighted.shape, 1)
    fy = row(fy_ref, x)
    west = pltpu.roll(weighted * (flat_mix + 0.5 * fy), CY - 1, 1)
    east = pltpu.roll(weighted * (flat_mix - 0.5 * fy), 1, 1)
    total = jnp.where(lane == CY - 1, 0.0, west) + jnp.where(lane == 0, 0.0, east) - weighted
    if x < CX - 1:
        total = total + north_edge(lam_ref[x + 1], row(mask_ref, x + 1), row(fx_ref, x + 1))
    if x > 0:
        total = total + south_edge(lam_ref[x - 1], row(mask_ref, x - 1), row(fx_ref, x - 1))
    return total


def halo_lanes(x, hw_ref, he_ref):
    lane = lax.broadcasted_iota(jnp.int32, hw_ref.shape, 1)
    east = he_ref[...] if x == 0 else pltpu.roll(he_ref[...], CY - x, 1)
    west = pltpu.roll(hw_ref[...], CY - 1 - x, 1)
    return jnp.where(lane == CY - 1, west, 0.0) + jnp.where(lane == 0, east, 0.0)


def put_edges(lam_ref, mask_ref, fx_ref, fy_ref, en_ref, es_ref, ew_ref, ee_ref):
    ew_ref[...] = jnp.zeros_like(ew_ref)
    ee_ref[...] = jnp.zeros_like(ee_ref)
    for x in range(CX):
        edge_plane(x, lam_ref[x], row(mask_ref, x), row(fy_ref, x), ew_ref, ee_ref)
    en_ref[...] = north_edge(lam_ref[0], row(mask_ref, 0), row(fx_ref, 0))
    es_ref[...] = south_edge(lam_ref[CX - 1], row(mask_ref, CX - 1), row(fx_ref, CX - 1))


def edges_kernel(raw_ref, mask_ref, fx_ref, fy_ref, planes_ref, base_ref, en_ref, es_ref, ew_ref, ee_ref):
    planes_ref[...] = jnp.zeros_like(planes_ref)
    for x in range(CX):
        for t in range(TRACERS):
            planes_ref[x, t * PAD : t * PAD + NZ, :] = raw_ref[pl.ds(t * NZ * CX + x, NZ, stride=CX), :]
    put_edges(planes_ref, mask_ref, fx_ref, fy_ref, en_ref, es_ref, ew_ref, ee_ref)
    for x in range(CX):
        base_ref[x] = planes_ref[x] + step_size * local_plane(x, planes_ref, mask_ref, fx_ref, fy_ref)


EDGE = far(FEATS, CY)
PLANE = (CX, FEATS, CY)


def edges(*args):
    return call(edges_kernel, "edges", (far(*PLANE), far(*PLANE), EDGE, EDGE, EDGE, EDGE), args)


def last_kernel(mask_ref, fx_ref, fy_ref, hw_ref, he_ref, lam_far, down_far, out_ref, lam, down, sems):
    wait = bring(((0, lam_far, lam), (0, down_far, down)), sems)
    wait(0)
    for x in range(CX):
        total = local_plane(x, lam, mask_ref, fx_ref, fy_ref) + halo_lanes(x, hw_ref, he_ref)
        value = lam[x] + step_size * (total + down[x])
        for t in range(TRACERS):
            out_ref[pl.ds(t * NZ * CX + x, NZ, stride=CX), :] = value[t * PAD : t * PAD + NZ]


def last_stencil(lam, down, *args):
    scratch = [near(*PLANE), near(*PLANE), pltpu.SemaphoreType.DMA((2,))]
    (out,) = call(last_kernel, "stencil0", (near(TRACERS * NZ * CX, CY),), args, (lam, down), scratch, mib=8)
    return out


def rows_kernel(part_ref, hn_ref, hs_ref, out_ref):
    for x, halo_ref in ((0, hs_ref), (CX - 1, hn_ref)):
        for t in range(TRACERS):
            rows = pl.ds(t * NZ * CX + x, NZ, stride=CX)
            out_ref[rows, :] = part_ref[rows, :] + step_size * halo_ref[t * PAD : t * PAD + NZ, :]


def add_rows(part, hn, hs):
    (out,) = call(rows_kernel, "rows0", (near(*part.shape),), (part, hn, hs), aliases={0: 0})
    return out


def closure_step(first, got_ref, owner_ref, mask_ref, lam_ref, weight_refs, out_ref, rows_ref, total, wait):
    f1_ref, f2_ref, f3_ref, r3_ref, r2_ref, r1_ref, b2_ref, b3_ref = weight_refs
    for half in range(2):
        for g in range(DEV // 8):
            at = half * (STORE // 2) + g * 128
            lo = first + half * HALF
            main = [got_ref[8 * g + i, lo : lo + HALF, :] for i in range(8)]
            rows_ref[: 2 * PAD, at : at + 128] = jnp.concatenate(main, axis=0).T
    for g in range(DEV // 8):
        rest = [got_ref[8 * g + i, first + SLOT : first + BLOCK, :] for i in range(8)]
        both = jnp.concatenate(rest, axis=0).T
        rows_ref[2 * PAD :, g * 128 : (g + 1) * 128] = both[:PAD]
        at = STORE // 2 + g * 128
        rows_ref[2 * PAD :, at : at + 128] = both[PAD:]

    def wide(ref):
        return jnp.concatenate([ref[i : i + 1, :] for i in range(CX)], axis=1)

    wait("tile")
    owner = wide(owner_ref)
    at = ((owner >> 4) & 1) * (STORE // 2) + (owner >> 5) * HALF + (owner & (HALF - 1))
    level = lax.broadcasted_iota(jnp.int32, (256, COLS), 0)
    picked = None
    for k in range(STORE // 256):
        hot = jnp.where(level == at - 256 * k, 1.0, 0.0).astype(BF)
        part = dot(rows_ref[:, 256 * k : 256 * (k + 1)], hot)
        picked = part if picked is None else picked + part
    row = lax.broadcasted_iota(jnp.int32, (FEATS, COLS), 0)
    inputs = jnp.where(row == NZ, 1.0, picked).astype(BF)

    wait("weights")
    both = dot(f1_ref[...], inputs)
    h1 = jnp.tanh(both[:HID] + both[HID:])
    h1_high, h1_low = split(h1)
    both = dot(f2_ref[...], h1_high)
    h2 = jnp.tanh(both[:HID] + both[HID:] + dot(f2_ref[:HID], h1_low) + b2_ref[...])
    h2_high, h2_low = split(h2)
    both = dot(f3_ref[...], h2_high)
    sig = jax.nn.sigmoid(both[:PAD] + both[PAD:] + dot(f3_ref[:PAD], h2_low) + b3_ref[...])
    inner = lax.broadcasted_iota(jnp.int32, (PAD, COLS), 0) < NZ - 1
    kappa = jnp.where(inner, kappa_top * sig, 0.0)

    wait("lam")
    mask_row = wide(mask_ref).astype(F32)
    slope = jnp.zeros((PAD, COLS), F32)
    direct = []
    for t in range(TRACERS):
        lo, hi = t * PAD, (t + 1) * PAD
        mu = jnp.concatenate([lam_ref[i, lo:hi, :] for i in range(CX)], axis=1) * mask_row
        gap = mu - pltpu.roll(mu, PAD - 1, 0)
        column = picked[lo:hi]
        slope = slope + gap * (pltpu.roll(column, PAD - 1, 0) - column)
        flow = kappa * gap
        direct.append(pltpu.roll(flow, 1, 0) - flow)
    d3 = slope * kappa * (1.0 - sig)
    d3_high, d3_low = split(d3)
    d2 = dot(r3_ref[...], jnp.concatenate([d3_high, d3_high, d3_low], axis=0)) * (1.0 - h2 * h2)
    d2_high, d2_low = split(d2)
    both = dot(r2_ref[...], d2_high)
    d1 = (both[:HID] + both[HID:] + dot(r2_ref[:HID], d2_low)) * (1.0 - h1 * h1)
    d1_high, d1_low = split(d1)
    both = dot(r1_ref[...], d1_high)
    d0 = both[:FEATS] + both[FEATS:] + dot(r1_ref[:FEATS], d1_low)

    for i in range(CX):
        part = slice(i * CY, (i + 1) * CY)
        for t in range(TRACERS):
            lo, hi = t * PAD, (t + 1) * PAD
            out_ref[i, lo:hi, :] = d0[lo:hi, part] + direct[t][:, part]
    wait("out")

    ones = jnp.ones((16, COLS), BF)
    total[:FEATS, :] += dot_nt(inputs, d1_high) + dot_nt(inputs, d1_low)
    both = dot_nt(jnp.concatenate([h1_high, h1_low, ones], axis=0), d2_high)
    other = dot_nt(jnp.concatenate([h1_high, ones], axis=0), d2_low)
    total[FEATS : FEATS + HID, :] += both[:HID] + both[HID : 2 * HID] + other[:HID]
    total[NZ + 1 : NZ + 2, :] += both[2 * HID : 2 * HID + 1] + other[HID : HID + 1]
    d3_both = jnp.concatenate([d3_high, d3_low], axis=0)
    both = dot_nt(d3_both, h2_high)
    total[FEATS + HID :, :] += both[:PAD] + both[PAD:] + dot_nt(d3_high, h2_low)
    both = dot_nt(ones, d3_both)
    total[NZ + 2 : NZ + 3, :PAD] += both[:1, :PAD] + both[:1, PAD:]


def late_kernel(got_ref, *refs):
    sources, (out_ref, total), refs = refs[:12], refs[12:14], refs[14:]
    targets, (rows_ref, down, sems) = refs[:12], refs[12:]
    names = ("tile", "tile") + ("weights",) * 8 + ("lam", "base")
    wait = bring(zip(names, sources, targets), sems)
    owner, mask, *split_weights = targets[:10]
    planes, base = targets[10:]
    total[...] = jnp.zeros_like(total)

    def then(name):
        wait(name)
        if name == "out":
            wait("base")
            for x in range(CX):
                out_ref[x] = base[x] + step_size * down[x]

    closure_step(BLOCK, got_ref, owner, mask, planes, split_weights, down, rows_ref, total, then)


def early_kernel(got_ref, owner_ref, mask_ref, fx_ref, fy_ref, part_ref, before_ref, *refs):
    halos, sources, refs = refs[:4], refs[4:12], refs[12:]
    (lam_far, down_far, grads_ref), sides, refs = refs[:3], refs[3:7], refs[7:]
    targets, (rows_ref, lam, down, total, sems, out_sems) = refs[:8], refs[8:]
    wait = bring(zip(("weights",) * 8, sources, targets), sems)
    hn_ref, hs_ref, hw_ref, he_ref = halos
    for x in range(CX):
        halo = halo_lanes(x, hw_ref, he_ref)
        if x == 0:
            halo = halo + hs_ref[...]
        if x == CX - 1:
            halo = halo + hn_ref[...]
        lam[x] = part_ref[x] + step_size * halo
    lam_copy = pltpu.make_async_copy(lam, lam_far, out_sems.at[0])
    lam_copy.start()
    down_copy = pltpu.make_async_copy(down, down_far, out_sems.at[1])
    put_edges(lam, mask_ref, fx_ref, fy_ref, *sides)
    total[...] = before_ref[...]

    def then(name):
        wait(name)
        if name == "out":
            down_copy.start()

    closure_step(0, got_ref, owner_ref, mask_ref, lam, targets, down, rows_ref, total, then)
    grads_ref[: 2 * HID, :] = total[:, :128]
    grads_ref[2 * HID :, :] = total[:, 128:]
    lam_copy.wait()
    down_copy.wait()


WEIGHT_SCRATCH = [near(*shape, dtype=BF) for shape in WEIGHTS] + [near(HID, 1), near(PAD, 1)]
ROWS = near(FEATS, STORE, dtype=BF)
TOTAL = near(2 * HID, HID)


def late_closure(got, *copied):
    scratch = [near(CX, CY, dtype=jnp.int32)] * 2 + WEIGHT_SCRATCH
    scratch += [near(*PLANE), near(*PLANE), ROWS, near(*PLANE), pltpu.SemaphoreType.DMA((12,))]
    return call(late_kernel, "closure1", (near(*PLANE), TOTAL), (got,), copied, scratch, CLOSURE_MIB)


def early_closure(got, owners, mask, fx, fy, part, before, halos, split_weights):
    outs = ([far(*PLANE)], [far(*PLANE)], far(4 * HID, 128), EDGE, EDGE, EDGE, EDGE)
    scratch = WEIGHT_SCRATCH + [ROWS, near(*PLANE), near(*PLANE), TOTAL]
    scratch += [pltpu.SemaphoreType.DMA((8,)), pltpu.SemaphoreType.DMA((2,))]
    args = (got, owners, mask, fx, fy, part, before, *halos)
    return call(early_kernel, "closure0", outs, args, split_weights, scratch, CLOSURE_MIB)


def sum_kernel(parts_ref, out_ref):
    value = parts_ref[0:8, :]
    for i in range(1, DEV):
        value = value + parts_ref[8 * i : 8 * i + 8, :]
    for i in range(DEV):
        out_ref[8 * i : 8 * i + 8, :] = value


def unpack_kernel(scale, sums_ref, w1_ref, b1_ref, w2_ref, b2_ref, w3t_ref, b3_ref):
    for part in range(2):
        lanes = slice(part * 128, (part + 1) * 128)
        top = part * 2 * HID
        for t in range(TRACERS):
            w1_ref[t * NZ : (t + 1) * NZ, lanes] = sums_ref[top + t * PAD : top + t * PAD + NZ, :] * scale
        b1_ref[:, lanes] = sums_ref[top + NZ : top + NZ + 1, :] * scale
        b2_ref[:, lanes] = sums_ref[top + NZ + 1 : top + NZ + 2, :] * scale
        w2_ref[:, lanes] = sums_ref[top + FEATS : top + FEATS + HID, :] * scale
        w3t_ref[:, lanes] = sums_ref[top + FEATS + HID : top + FEATS + HID + NZ, :] * scale
    b3_ref[...] = sums_ref[NZ + 2 : NZ + 3, :NZ] * scale


def reduce_params(packed, tied):
    parts = lax.all_to_all(packed, ("gx", "gy"), split_axis=0, concat_axis=0, tiled=True)
    parts, _ = lax.optimization_barrier((parts, tied))
    (spread,) = call(sum_kernel, "sum", (far(*packed.shape),), (parts,))
    return spread


def finish_params(spread, count):
    sums = lax.all_to_all(spread, ("gx", "gy"), split_axis=0, concat_axis=0, tiled=True)
    shapes = ((TRACERS * NZ, HID), (1, HID), (HID, HID), (1, HID), (NZ, HID), (1, NZ))
    scale = step_size / float(np.sqrt(count))
    outs = tuple(far(*shape) for shape in shapes)
    return call(functools.partial(unpack_kernel, scale), "unpack", outs, (sums,))


def exchange(axis, before, after):
    up = [(i, i + 1) for i in range(lax.axis_size(axis) - 1)]
    down = [(j, i) for i, j in up]
    return lax.ppermute(before, axis, down), lax.ppermute(after, axis, up)


def on_device(
    stored,
    counts,
    owners,
    land_mask,
    flow_x,
    flow_y,
    costate,
    weight_in,
    bias_in,
    weight_mid,
    bias_mid,
    weight_out,
    bias_out,
):
    payload = pack(counts, stored[0].T)
    costate, weight_mid, payload = lax.optimization_barrier((costate, weight_mid, payload))
    got = lax.all_to_all(payload, ("gx", "gy"), split_axis=0, concat_axis=0, tiled=True)
    split_weights = weights(
        weight_in, bias_in[None, :], weight_mid, bias_mid[None, :], weight_out.T, bias_out[None, :]
    )
    planes, base, north, south, west, east = edges(
        costate.reshape(TRACERS * NZ * CX, CY), land_mask, flow_x, flow_y
    )
    halos = exchange("gx", north, south) + exchange("gy", west, east)
    part, grads = late_closure(got, owners, land_mask, *split_weights, planes, base)
    lam, down, packed, north, south, west, east = early_closure(
        got, owners, land_mask, flow_x, flow_y, part, grads, halos, split_weights
    )
    halos_y = exchange("gy", west, east)
    spread = reduce_params(packed, halos_y)
    north, south, spread = lax.optimization_barrier((north, south, spread))
    halos_x = exchange("gx", north, south)
    lam, down, spread = lax.optimization_barrier((lam, down, spread))
    adjoint = last_stencil(lam, down, land_mask, flow_x, flow_y, *halos_y)
    adjoint = add_rows(adjoint, *halos_x)
    count = CX * CY * lax.axis_size("gx") * lax.axis_size("gy")
    g1, gb1, g2, gb2, g3, gb3 = finish_params(spread, count)
    return (adjoint.reshape(costate.shape), g1, gb1[0], g2, gb2[0], g3.T, gb3[0])


def solution(mesh):
    in_specs = (
        P(("gx", "gy"), None, None),
        P(("gx", "gy"), None),
        P("gx", "gy"),
        P("gx", "gy"),
        P("gx", "gy"),
        P("gx", "gy"),
        P(None, None, "gx", "gy"),
        P(),
        P(),
        P(),
        P(),
        P(),
        P(),
    )
    out_specs = (P(None, None, "gx", "gy"), P(), P(), P(), P(), P(), P())
    return jax.shard_map(
        on_device, mesh=mesh, in_specs=in_specs, out_specs=out_specs, check_vma=False
    )
```

```python
import functools

import jax
import jax.numpy as jnp
import numpy as np
from jax import lax
from jax.experimental import pallas as pl
from jax.experimental.pallas import tpu as pltpu
from jax.sharding import PartitionSpec as P

NZ = 60
TRACERS = 3
PAD = 64
FEATS = TRACERS * PAD
HID = 256
SLOT = 32
HALF = SLOT // 2
BLOCK = SLOT + HALF
CX = 16
CY = 128
DEV = 128
STORE = 4096
UNROLL = 16
COLS = CX * CY

CLOSURE_MIB = 24

BF = jnp.bfloat16
F32 = jnp.float32
NT = (((1,), (1,)), ((), ()))

step_size = 0.25
flat_mix = 0.25
kappa_top = 1.5


def split(value):
    high = value.astype(BF)
    return high, (value - high.astype(F32)).astype(BF)


def dot(left, right):
    return jnp.dot(left, right, preferred_element_type=F32)


def dot_nt(left, right):
    return lax.dot_general(left, right, NT, preferred_element_type=F32)


def params(mib):
    return pltpu.CompilerParams(vmem_limit_bytes=mib * 2**20)


def bring(copies, sems):
    started = {}
    for i, (name, source, target) in enumerate(copies):
        started.setdefault(name, []).append(pltpu.make_async_copy(source, target, sems.at[i]))
        started[name][-1].start()

    def wait(name):
        for copy in started.pop(name, ()):
            copy.wait()

    return wait


def near(*shape, dtype=F32):
    return pltpu.VMEM(shape, dtype)


def far(*shape, dtype=F32):
    return pltpu.HBM(shape, dtype)


def call(kernel, name, outs, args, copied=(), scratch=(), mib=4, aliases={}):
    args = [pltpu.with_memory_space_constraint(a, pltpu.VMEM) for a in args]
    copied = [pltpu.with_memory_space_constraint(a, pltpu.HBM) for a in copied]
    inside = pl.BlockSpec(memory_space=pltpu.VMEM)
    anywhere = pl.BlockSpec(memory_space=pl.ANY)
    return pl.pallas_call(
        kernel,
        out_shape=tuple(out[0] if isinstance(out, list) else out for out in outs),
        in_specs=[inside] * len(args) + [anywhere] * len(copied),
        out_specs=tuple(anywhere if isinstance(out, list) else inside for out in outs),
        scratch_shapes=list(scratch),
        input_output_aliases=aliases,
        compiler_params=params(mib),
        name=name,
    )(*args, *copied)


def pack_kernel(counts_ref, stored_ref, out_ref, near, padded, rows_out, in_sems, out_sem):
    cut = (FEATS - TRACERS * (PAD - NZ) + 7) // 8 * 8
    parts = (slice(0, cut), slice(cut, 2 * TRACERS * NZ))
    copies = [pltpu.make_async_copy(stored_ref.at[p, :], near.at[p, :], in_sems.at[i]) for i, p in enumerate(parts)]
    for copy in copies:
        copy.start()
    lane = lax.broadcasted_iota(jnp.int32, (SLOT, 256), 1)
    offset = lane - lax.broadcasted_iota(jnp.int32, (SLOT, 256), 0)
    for block in range(2 * TRACERS):
        padded[block * PAD + NZ : (block + 1) * PAD, :] = jnp.zeros((PAD - NZ, STORE), BF)
    for moment in range(2):
        copies[moment].wait()
        for block in range(moment * TRACERS, (moment + 1) * TRACERS):
            padded[block * PAD : block * PAD + NZ, :] = near[block * NZ : (block + 1) * NZ, :]

    def group(g, start):
        base = pl.multiple_of(jnp.minimum((start // 128) * 128, STORE - 256), 128)
        hots = []
        for i in range(4):
            hots.append(jnp.where(offset == start - base, 1.0, 0.0).astype(BF))
            start = start + counts_ref[0, 4 * g + i]
        rows = dot_nt(jnp.concatenate(hots, axis=0), padded[:, pl.ds(base, 256)])
        for i in range(4):
            for moment in range(2):
                at, first = moment * BLOCK, moment * FEATS
                mine = rows[i * SLOT : (i + 1) * SLOT, first : first + FEATS]
                rest = jnp.concatenate([mine[:HALF, 2 * PAD :], mine[HALF:, 2 * PAD :]], axis=1)
                rows_out[4 * g + i, at : at + SLOT, :] = mine[:, : 2 * PAD].astype(BF)
                rows_out[4 * g + i, at + SLOT : at + BLOCK, :] = rest.astype(BF)
        return start

    def leave(j):
        tiles = pl.ds(j * 4 * UNROLL, 4 * UNROLL)
        return pltpu.make_async_copy(rows_out.at[tiles], out_ref.at[tiles], out_sem.at[j])

    start = jnp.int32(0)
    steps = DEV // 4 // UNROLL

    def groups(j, start):
        for u in range(UNROLL):
            start = group(j * UNROLL + u, start)
        leave(j).start()
        return start

    lax.fori_loop(0, steps, groups, start)
    for j in range(steps):
        leave(j).wait()


def pack(counts, stored_t):
    anywhere = pl.BlockSpec(memory_space=pl.ANY)
    return pl.pallas_call(
        pack_kernel,
        out_shape=pltpu.HBM((DEV, 2 * BLOCK, 128), BF),
        in_specs=[pl.BlockSpec(memory_space=pltpu.SMEM), anywhere],
        out_specs=anywhere,
        scratch_shapes=[
            pltpu.VMEM((2 * TRACERS * NZ, STORE), BF),
            pltpu.VMEM((2 * FEATS, STORE), BF),
            pltpu.VMEM((DEV, 2 * BLOCK, 128), BF),
            pltpu.SemaphoreType.DMA((2,)),
            pltpu.SemaphoreType.DMA((DEV // 4 // UNROLL,)),
        ],
        compiler_params=params(24),
        name="pack",
    )(*(pltpu.with_memory_space_constraint(a, pltpu.HBM) for a in (counts, stored_t)))


def weights_kernel(w1_ref, b1_ref, w2_ref, b2_ref, w3t_ref, b3_ref, *refs):
    f1_ref, f2_ref, f3_ref, r3_ref, r2_ref, r1_ref, c2_ref, c3_ref, wide, tall = refs
    wide[...] = jnp.zeros_like(wide)
    for t in range(TRACERS):
        wide[t * PAD : t * PAD + NZ, :] = w1_ref[t * NZ : (t + 1) * NZ, :]
    high, low = split(wide[...])
    r1_ref[:FEATS, :] = high
    r1_ref[FEATS:, :] = low
    wide[NZ : NZ + 1, :] = b1_ref[...]
    high, low = split(wide[...].T)
    f1_ref[:HID, :] = high
    f1_ref[HID:, :] = low
    high, low = split(w2_ref[...])
    r2_ref[:HID, :] = high
    r2_ref[HID:, :] = low
    high, low = split(w2_ref[...].T)
    f2_ref[:HID, :] = high
    f2_ref[HID:, :] = low
    tall[...] = jnp.zeros_like(tall)
    tall[:NZ, :] = w3t_ref[...]
    high, low = split(tall[:PAD, :])
    f3_ref[:PAD, :] = high
    f3_ref[PAD:, :] = low
    tall[PAD : 2 * PAD, :] = tall[:PAD, :]
    tall[2 * PAD :, :] = tall[:PAD, :]
    high, low = split(tall[...].T)
    lane = lax.broadcasted_iota(jnp.int32, high.shape, 1)
    middle = (lane >= PAD) & (lane < 2 * PAD)
    r3_ref[...] = jnp.where(middle, low.astype(F32), high.astype(F32)).astype(BF)
    c2_ref[...] = jnp.broadcast_to(b2_ref[...], (8, HID)).T[:, :1]
    c3_ref[...] = jnp.zeros_like(c3_ref)
    c3_ref[:NZ, :] = jnp.broadcast_to(b3_ref[...], (8, NZ)).T[:, :1]


WEIGHTS = ((2 * HID, FEATS), (2 * HID, HID), (2 * PAD, HID), (HID, FEATS), (2 * HID, HID), (2 * FEATS, HID))


def weights(*args):
    outs = tuple(far(*shape, dtype=BF) for shape in WEIGHTS) + (far(HID, 1), far(PAD, 1))
    return call(weights_kernel, "weights", outs, args, scratch=[near(FEATS, HID), near(FEATS, HID)])


def edge_plane(x, plane, mask_row, fy_row, ew_ref, ee_ref):
    weighted = plane * mask_row
    lane = lax.broadcasted_iota(jnp.int32, plane.shape, 1)
    west = pltpu.roll(weighted * (flat_mix + 0.5 * fy_row), x, 1)
    east = pltpu.roll(weighted * (flat_mix - 0.5 * fy_row), x + 1, 1)
    ew_ref[...] = jnp.where(lane == x, west, ew_ref[...])
    ee_ref[...] = jnp.where(lane == x, east, ee_ref[...])


def north_edge(plane, mask_row, fx_row):
    return plane * mask_row * (flat_mix + 0.5 * fx_row)


def south_edge(plane, mask_row, fx_row):
    return plane * mask_row * (flat_mix - 0.5 * fx_row)


def row(ref, x):
    return ref[x : x + 1, :].astype(F32)


def local_plane(x, lam_ref, mask_ref, fx_ref, fy_ref):
    weighted = lam_ref[x] * row(mask_ref, x)
    lane = lax.broadcasted_iota(jnp.int32, weighted.shape, 1)
    fy = row(fy_ref, x)
    west = pltpu.roll(weighted * (flat_mix + 0.5 * fy), CY - 1, 1)
    east = pltpu.roll(weighted * (flat_mix - 0.5 * fy), 1, 1)
    total = jnp.where(lane == CY - 1, 0.0, west) + jnp.where(lane == 0, 0.0, east) - weighted
    if x < CX - 1:
        total = total + north_edge(lam_ref[x + 1], row(mask_ref, x + 1), row(fx_ref, x + 1))
    if x > 0:
        total = total + south_edge(lam_ref[x - 1], row(mask_ref, x - 1), row(fx_ref, x - 1))
    return total


def halo_lanes(x, hw_ref, he_ref):
    lane = lax.broadcasted_iota(jnp.int32, hw_ref.shape, 1)
    east = he_ref[...] if x == 0 else pltpu.roll(he_ref[...], CY - x, 1)
    west = pltpu.roll(hw_ref[...], CY - 1 - x, 1)
    return jnp.where(lane == CY - 1, west, 0.0) + jnp.where(lane == 0, east, 0.0)


def put_edges(lam_ref, mask_ref, fx_ref, fy_ref, en_ref, es_ref, ew_ref, ee_ref):
    ew_ref[...] = jnp.zeros_like(ew_ref)
    ee_ref[...] = jnp.zeros_like(ee_ref)
    for x in range(CX):
        edge_plane(x, lam_ref[x], row(mask_ref, x), row(fy_ref, x), ew_ref, ee_ref)
    en_ref[...] = north_edge(lam_ref[0], row(mask_ref, 0), row(fx_ref, 0))
    es_ref[...] = south_edge(lam_ref[CX - 1], row(mask_ref, CX - 1), row(fx_ref, CX - 1))


def edges_kernel(raw_ref, mask_ref, fx_ref, fy_ref, planes_ref, base_ref, en_ref, es_ref, ew_ref, ee_ref):
    planes_ref[...] = jnp.zeros_like(planes_ref)
    for x in range(CX):
        for t in range(TRACERS):
            planes_ref[x, t * PAD : t * PAD + NZ, :] = raw_ref[pl.ds(t * NZ * CX + x, NZ, stride=CX), :]
    put_edges(planes_ref, mask_ref, fx_ref, fy_ref, en_ref, es_ref, ew_ref, ee_ref)
    for x in range(CX):
        base_ref[x] = planes_ref[x] + step_size * local_plane(x, planes_ref, mask_ref, fx_ref, fy_ref)


EDGE = far(FEATS, CY)
PLANE = (CX, FEATS, CY)


def edges(*args):
    return call(edges_kernel, "edges", (far(*PLANE), far(*PLANE), EDGE, EDGE, EDGE, EDGE), args)


def last_kernel(mask_ref, fx_ref, fy_ref, hw_ref, he_ref, lam_far, down_far, out_ref, lam, down, sems):
    wait = bring(((0, lam_far, lam), (0, down_far, down)), sems)
    wait(0)
    for x in range(CX):
        total = local_plane(x, lam, mask_ref, fx_ref, fy_ref) + halo_lanes(x, hw_ref, he_ref)
        value = lam[x] + step_size * (total + down[x])
        for t in range(TRACERS):
            out_ref[pl.ds(t * NZ * CX + x, NZ, stride=CX), :] = value[t * PAD : t * PAD + NZ]


def last_stencil(lam, down, *args):
    scratch = [near(*PLANE), near(*PLANE), pltpu.SemaphoreType.DMA((2,))]
    (out,) = call(last_kernel, "stencil0", (near(TRACERS * NZ * CX, CY),), args, (lam, down), scratch, mib=8)
    return out


def rows_kernel(part_ref, hn_ref, hs_ref, out_ref):
    for x, halo_ref in ((0, hs_ref), (CX - 1, hn_ref)):
        for t in range(TRACERS):
            rows = pl.ds(t * NZ * CX + x, NZ, stride=CX)
            out_ref[rows, :] = part_ref[rows, :] + step_size * halo_ref[t * PAD : t * PAD + NZ, :]


def add_rows(part, hn, hs):
    (out,) = call(rows_kernel, "rows0", (near(*part.shape),), (part, hn, hs), aliases={0: 0})
    return out


def closure_step(first, got_ref, owner_ref, mask_ref, lam_ref, weight_refs, out_ref, rows_ref, total, wait):
    f1_ref, f2_ref, f3_ref, r3_ref, r2_ref, r1_ref, b2_ref, b3_ref = weight_refs
    for half in range(2):
        for g in range(DEV // 8):
            at = half * (STORE // 2) + g * 128
            lo = first + half * HALF
            main = [got_ref[8 * g + i, lo : lo + HALF, :] for i in range(8)]
            rows_ref[: 2 * PAD, at : at + 128] = jnp.concatenate(main, axis=0).T
    for g in range(DEV // 8):
        rest = [got_ref[8 * g + i, first + SLOT : first + BLOCK, :] for i in range(8)]
        both = jnp.concatenate(rest, axis=0).T
        rows_ref[2 * PAD :, g * 128 : (g + 1) * 128] = both[:PAD]
        at = STORE // 2 + g * 128
        rows_ref[2 * PAD :, at : at + 128] = both[PAD:]

    def wide(ref):
        return jnp.concatenate([ref[i : i + 1, :] for i in range(CX)], axis=1)

    wait("tile")
    owner = wide(owner_ref)
    at = ((owner >> 4) & 1) * (STORE // 2) + (owner >> 5) * HALF + (owner & (HALF - 1))
    level = lax.broadcasted_iota(jnp.int32, (256, COLS), 0)
    picked = None
    for k in range(STORE // 256):
        hot = jnp.where(level == at - 256 * k, 1.0, 0.0).astype(BF)
        part = dot(rows_ref[:, 256 * k : 256 * (k + 1)], hot)
        picked = part if picked is None else picked + part
    row = lax.broadcasted_iota(jnp.int32, (FEATS, COLS), 0)
    inputs = jnp.where(row == NZ, 1.0, picked).astype(BF)

    wait("weights")
    both = dot(f1_ref[...], inputs)
    h1 = jnp.tanh(both[:HID] + both[HID:])
    h1_high, h1_low = split(h1)
    both = dot(f2_ref[...], h1_high)
    h2 = jnp.tanh(both[:HID] + both[HID:] + dot(f2_ref[:HID], h1_low) + b2_ref[...])
    h2_high, h2_low = split(h2)
    both = dot(f3_ref[...], h2_high)
    sig = jax.nn.sigmoid(both[:PAD] + both[PAD:] + dot(f3_ref[:PAD], h2_low) + b3_ref[...])
    inner = lax.broadcasted_iota(jnp.int32, (PAD, COLS), 0) < NZ - 1
    kappa = jnp.where(inner, kappa_top * sig, 0.0)

    wait("lam")
    mask_row = wide(mask_ref).astype(F32)
    slope = jnp.zeros((PAD, COLS), F32)
    direct = []
    for t in range(TRACERS):
        lo, hi = t * PAD, (t + 1) * PAD
        mu = jnp.concatenate([lam_ref[i, lo:hi, :] for i in range(CX)], axis=1) * mask_row
        gap = mu - pltpu.roll(mu, PAD - 1, 0)
        column = picked[lo:hi]
        slope = slope + gap * (pltpu.roll(column, PAD - 1, 0) - column)
        flow = kappa * gap
        direct.append(pltpu.roll(flow, 1, 0) - flow)
    d3 = slope * kappa * (1.0 - sig)
    d3_high, d3_low = split(d3)
    d2 = dot(r3_ref[...], jnp.concatenate([d3_high, d3_high, d3_low], axis=0)) * (1.0 - h2 * h2)
    d2_high, d2_low = split(d2)
    both = dot(r2_ref[...], d2_high)
    d1 = (both[:HID] + both[HID:] + dot(r2_ref[:HID], d2_low)) * (1.0 - h1 * h1)
    d1_high, d1_low = split(d1)
    both = dot(r1_ref[...], d1_high)
    d0 = both[:FEATS] + both[FEATS:] + dot(r1_ref[:FEATS], d1_low)

    for i in range(CX):
        part = slice(i * CY, (i + 1) * CY)
        for t in range(TRACERS):
            lo, hi = t * PAD, (t + 1) * PAD
            out_ref[i, lo:hi, :] = d0[lo:hi, part] + direct[t][:, part]
    wait("out")

    ones = jnp.ones((16, COLS), BF)
    total[:FEATS, :] += dot_nt(inputs, d1_high) + dot_nt(inputs, d1_low)
    both = dot_nt(jnp.concatenate([h1_high, h1_low, ones], axis=0), d2_high)
    other = dot_nt(jnp.concatenate([h1_high, ones], axis=0), d2_low)
    total[FEATS : FEATS + HID, :] += both[:HID] + both[HID : 2 * HID] + other[:HID]
    total[NZ + 1 : NZ + 2, :] += both[2 * HID : 2 * HID + 1] + other[HID : HID + 1]
    d3_both = jnp.concatenate([d3_high, d3_low], axis=0)
    both = dot_nt(d3_both, h2_high)
    total[FEATS + HID :, :] += both[:PAD] + both[PAD:] + dot_nt(d3_high, h2_low)
    both = dot_nt(ones, d3_both)
    total[NZ + 2 : NZ + 3, :PAD] += both[:1, :PAD] + both[:1, PAD:]


def late_kernel(got_ref, *refs):
    sources, (out_ref, total), refs = refs[:12], refs[12:14], refs[14:]
    targets, (rows_ref, down, sems) = refs[:12], refs[12:]
    names = ("tile", "tile") + ("weights",) * 8 + ("lam", "base")
    wait = bring(zip(names, sources, targets), sems)
    owner, mask, *split_weights = targets[:10]
    planes, base = targets[10:]
    total[...] = jnp.zeros_like(total)

    def then(name):
        wait(name)
        if name == "out":
            wait("base")
            for x in range(CX):
                out_ref[x] = base[x] + step_size * down[x]

    closure_step(BLOCK, got_ref, owner, mask, planes, split_weights, down, rows_ref, total, then)


def early_kernel(got_ref, fx_ref, fy_ref, part_ref, before_ref, owner_ref, mask_ref, *refs):
    split_weights, halos, refs = refs[:8], refs[8:12], refs[12:]
    (lam_far, down_far, grads_ref), sides, (rows_ref, lam, down, total, out_sems) = refs[:3], refs[3:7], refs[7:]
    hn_ref, hs_ref, hw_ref, he_ref = halos
    for x in range(CX):
        halo = halo_lanes(x, hw_ref, he_ref)
        if x == 0:
            halo = halo + hs_ref[...]
        if x == CX - 1:
            halo = halo + hn_ref[...]
        lam[x] = part_ref[x] + step_size * halo
    lam_copy = pltpu.make_async_copy(lam, lam_far, out_sems.at[0])
    lam_copy.start()
    down_copy = pltpu.make_async_copy(down, down_far, out_sems.at[1])
    put_edges(lam, mask_ref, fx_ref, fy_ref, *sides)
    total[...] = before_ref[...]

    def then(name):
        if name == "out":
            down_copy.start()

    closure_step(0, got_ref, owner_ref, mask_ref, lam, split_weights, down, rows_ref, total, then)
    grads_ref[: 2 * HID, :] = total[:, :128]
    grads_ref[2 * HID :, :] = total[:, 128:]
    lam_copy.wait()
    down_copy.wait()


TILE_WEIGHTS = [near(CX, CY, dtype=jnp.int32)] * 2
TILE_WEIGHTS += [near(*shape, dtype=BF) for shape in WEIGHTS] + [near(HID, 1), near(PAD, 1)]
ROWS = near(FEATS, STORE, dtype=BF)


def late_closure(got, *copied):
    outs = (near(*PLANE), near(2 * HID, HID), *TILE_WEIGHTS)
    scratch = [near(*PLANE), near(*PLANE), ROWS, near(*PLANE), pltpu.SemaphoreType.DMA((12,))]
    return call(late_kernel, "closure1", outs, (got,), copied, scratch, CLOSURE_MIB)


def early_closure(got, fx, fy, part, before, brought, halos):
    outs = ([far(*PLANE)], [far(*PLANE)], far(4 * HID, 128), EDGE, EDGE, EDGE, EDGE)
    scratch = [ROWS, near(*PLANE), near(*PLANE), near(2 * HID, HID), pltpu.SemaphoreType.DMA((2,))]
    args = (got, fx, fy, part, before, *brought, *halos)
    return call(early_kernel, "closure0", outs, args, (), scratch, CLOSURE_MIB)


def sum_kernel(parts_ref, out_ref):
    value = parts_ref[0:8, :]
    for i in range(1, DEV):
        value = value + parts_ref[8 * i : 8 * i + 8, :]
    for i in range(DEV):
        out_ref[8 * i : 8 * i + 8, :] = value


def unpack_kernel(scale, sums_ref, w1_ref, b1_ref, w2_ref, b2_ref, w3t_ref, b3_ref):
    for part in range(2):
        lanes = slice(part * 128, (part + 1) * 128)
        top = part * 2 * HID
        for t in range(TRACERS):
            w1_ref[t * NZ : (t + 1) * NZ, lanes] = sums_ref[top + t * PAD : top + t * PAD + NZ, :] * scale
        b1_ref[:, lanes] = sums_ref[top + NZ : top + NZ + 1, :] * scale
        b2_ref[:, lanes] = sums_ref[top + NZ + 1 : top + NZ + 2, :] * scale
        w2_ref[:, lanes] = sums_ref[top + FEATS : top + FEATS + HID, :] * scale
        w3t_ref[:, lanes] = sums_ref[top + FEATS + HID : top + FEATS + HID + NZ, :] * scale
    b3_ref[...] = sums_ref[NZ + 2 : NZ + 3, :NZ] * scale


def reduce_params(packed, tied):
    parts = lax.all_to_all(packed, ("gx", "gy"), split_axis=0, concat_axis=0, tiled=True)
    parts, _ = lax.optimization_barrier((parts, tied))
    (spread,) = call(sum_kernel, "sum", (far(*packed.shape),), (parts,))
    return spread


def finish_params(spread, count):
    sums = lax.all_to_all(spread, ("gx", "gy"), split_axis=0, concat_axis=0, tiled=True)
    shapes = ((TRACERS * NZ, HID), (1, HID), (HID, HID), (1, HID), (NZ, HID), (1, NZ))
    scale = step_size / float(np.sqrt(count))
    outs = tuple(far(*shape) for shape in shapes)
    return call(functools.partial(unpack_kernel, scale), "unpack", outs, (sums,))


def exchange(axis, before, after):
    up = [(i, i + 1) for i in range(lax.axis_size(axis) - 1)]
    down = [(j, i) for i, j in up]
    return lax.ppermute(before, axis, down), lax.ppermute(after, axis, up)


def on_device(
    stored,
    counts,
    owners,
    land_mask,
    flow_x,
    flow_y,
    costate,
    weight_in,
    bias_in,
    weight_mid,
    bias_mid,
    weight_out,
    bias_out,
):
    payload = pack(counts, stored[0].T)
    costate, weight_mid, payload = lax.optimization_barrier((costate, weight_mid, payload))
    got = lax.all_to_all(payload, ("gx", "gy"), split_axis=0, concat_axis=0, tiled=True)
    split_weights = weights(
        weight_in, bias_in[None, :], weight_mid, bias_mid[None, :], weight_out.T, bias_out[None, :]
    )
    planes, base, north, south, west, east = edges(
        costate.reshape(TRACERS * NZ * CX, CY), land_mask, flow_x, flow_y
    )
    halos = exchange("gx", north, south) + exchange("gy", west, east)
    part, grads, *brought = late_closure(got, owners, land_mask, *split_weights, planes, base)
    lam, down, packed, north, south, west, east = early_closure(got, flow_x, flow_y, part, grads, brought, halos)
    halos_y = exchange("gy", west, east)
    spread = reduce_params(packed, halos_y)
    north, south, spread = lax.optimization_barrier((north, south, spread))
    halos_x = exchange("gx", north, south)
    lam, down, spread = lax.optimization_barrier((lam, down, spread))
    adjoint = last_stencil(lam, down, land_mask, flow_x, flow_y, *halos_y)
    adjoint = add_rows(adjoint, *halos_x)
    count = CX * CY * lax.axis_size("gx") * lax.axis_size("gy")
    g1, gb1, g2, gb2, g3, gb3 = finish_params(spread, count)
    return (adjoint.reshape(costate.shape), g1, gb1[0], g2, gb2[0], g3.T, gb3[0])


def solution(mesh):
    in_specs = (
        P(("gx", "gy"), None, None),
        P(("gx", "gy"), None),
        P("gx", "gy"),
        P("gx", "gy"),
        P("gx", "gy"),
        P("gx", "gy"),
        P(None, None, "gx", "gy"),
        P(),
        P(),
        P(),
        P(),
        P(),
        P(),
    )
    out_specs = (P(None, None, "gx", "gy"), P(), P(), P(), P(), P(), P())
    return jax.shard_map(
        on_device, mesh=mesh, in_specs=in_specs, out_specs=out_specs, check_vma=False
    )
```

```python
import functools

import jax
import jax.numpy as jnp
import numpy as np
from jax import lax
from jax.experimental import pallas as pl
from jax.experimental.pallas import tpu as pltpu
from jax.sharding import PartitionSpec as P

NZ = 60
TRACERS = 3
PAD = 64
FEATS = TRACERS * PAD
HID = 256
SLOT = 32
HALF = SLOT // 2
BLOCK = SLOT + HALF
CX = 16
CY = 128
DEV = 128
STORE = 4096
UNROLL = DEV // 8
BATCH = 4
COLS = CX * CY

CLOSURE_MIB = 24

BF = jnp.bfloat16
F32 = jnp.float32
NT = (((1,), (1,)), ((), ()))

step_size = 0.25
flat_mix = 0.25
kappa_top = 1.5


def split(value):
    high = value.astype(BF)
    return high, (value - high.astype(F32)).astype(BF)


def dot(left, right):
    return jnp.dot(left, right, preferred_element_type=F32)


def dot_nt(left, right):
    return lax.dot_general(left, right, NT, preferred_element_type=F32)


def params(mib):
    return pltpu.CompilerParams(vmem_limit_bytes=mib * 2**20)


def bring(copies, sems):
    started = {}
    for i, (name, source, target) in enumerate(copies):
        started.setdefault(name, []).append(pltpu.make_async_copy(source, target, sems.at[i]))
        started[name][-1].start()

    def wait(name):
        for copy in started.pop(name, ()):
            copy.wait()

    return wait


def near(*shape, dtype=F32):
    return pltpu.VMEM(shape, dtype)


def far(*shape, dtype=F32):
    return pltpu.HBM(shape, dtype)


def call(kernel, name, outs, args, copied=(), scratch=(), mib=4, aliases={}):
    args = [pltpu.with_memory_space_constraint(a, pltpu.VMEM) for a in args]
    copied = [pltpu.with_memory_space_constraint(a, pltpu.HBM) for a in copied]
    inside = pl.BlockSpec(memory_space=pltpu.VMEM)
    anywhere = pl.BlockSpec(memory_space=pl.ANY)
    return pl.pallas_call(
        kernel,
        out_shape=tuple(out[0] if isinstance(out, list) else out for out in outs),
        in_specs=[inside] * len(args) + [anywhere] * len(copied),
        out_specs=tuple(anywhere if isinstance(out, list) else inside for out in outs),
        scratch_shapes=list(scratch),
        input_output_aliases=aliases,
        compiler_params=params(mib),
        name=name,
    )(*args, *copied)


def pack_kernel(counts_ref, stored_ref, out_ref, near, padded, rows_out, in_sems, out_sem):
    cut = STORE // 2 + 128
    parts = (slice(0, cut), slice(cut, STORE))
    copies = [pltpu.make_async_copy(stored_ref.at[:, p], near.at[:, p], in_sems.at[i]) for i, p in enumerate(parts)]
    for copy in copies:
        copy.start()
    lane = lax.broadcasted_iota(jnp.int32, (SLOT, 256), 1)
    offset = lane - lax.broadcasted_iota(jnp.int32, (SLOT, 256), 0)
    for block in range(2 * TRACERS):
        padded[block * PAD + NZ : (block + 1) * PAD, :] = jnp.zeros((PAD - NZ, STORE), BF)

    def arrive(half):
        copies[half].wait()
        for block in range(2 * TRACERS):
            padded[block * PAD : block * PAD + NZ, parts[half]] = near[block * NZ : (block + 1) * NZ, parts[half]]

    def group(g, start):
        base = pl.multiple_of(jnp.minimum((start // 128) * 128, STORE - 256), 128)
        hots = []
        for i in range(4):
            hots.append(jnp.where(offset == start - base, 1.0, 0.0).astype(BF))
            start = start + counts_ref[0, 4 * g + i]
        rows = dot_nt(jnp.concatenate(hots, axis=0), padded[:, pl.ds(base, 256)])
        for i in range(4):
            for moment in range(2):
                at, first = moment * BLOCK, moment * FEATS
                mine = rows[i * SLOT : (i + 1) * SLOT, first : first + FEATS]
                rest = jnp.concatenate([mine[:HALF, 2 * PAD :], mine[HALF:, 2 * PAD :]], axis=1)
                rows_out[4 * g + i, at : at + SLOT, :] = mine[:, : 2 * PAD].astype(BF)
                rows_out[4 * g + i, at + SLOT : at + BLOCK, :] = rest.astype(BF)
        return start

    def leave(j):
        tiles = pl.ds(j * 4 * BATCH, 4 * BATCH)
        return pltpu.make_async_copy(rows_out.at[tiles], out_ref.at[tiles], out_sem.at[j])

    def groups(half, start):
        pl.when(half == 0)(functools.partial(arrive, 0))
        pl.when(half == 1)(functools.partial(arrive, 1))
        for u in range(UNROLL):
            start = group(half * UNROLL + u, start)
            if u % BATCH == BATCH - 1:
                leave(half * (UNROLL // BATCH) + u // BATCH).start()
        return start

    lax.fori_loop(0, 2, groups, jnp.int32(0))
    for j in range(DEV // 4 // BATCH):
        leave(j).wait()


def pack(counts, stored_t):
    anywhere = pl.BlockSpec(memory_space=pl.ANY)
    return pl.pallas_call(
        pack_kernel,
        out_shape=pltpu.HBM((DEV, 2 * BLOCK, 128), BF),
        in_specs=[pl.BlockSpec(memory_space=pltpu.SMEM), anywhere],
        out_specs=anywhere,
        scratch_shapes=[
            pltpu.VMEM((2 * TRACERS * NZ, STORE), BF),
            pltpu.VMEM((2 * FEATS, STORE), BF),
            pltpu.VMEM((DEV, 2 * BLOCK, 128), BF),
            pltpu.SemaphoreType.DMA((2,)),
            pltpu.SemaphoreType.DMA((DEV // 4 // BATCH,)),
        ],
        compiler_params=params(24),
        name="pack",
    )(*(pltpu.with_memory_space_constraint(a, pltpu.HBM) for a in (counts, stored_t)))


def weights_kernel(w1_ref, b1_ref, w2_ref, b2_ref, w3t_ref, b3_ref, *refs):
    f1_ref, f2_ref, f3_ref, r3_ref, r2_ref, r1_ref, c2_ref, c3_ref, wide, tall = refs
    wide[...] = jnp.zeros_like(wide)
    for t in range(TRACERS):
        wide[t * PAD : t * PAD + NZ, :] = w1_ref[t * NZ : (t + 1) * NZ, :]
    high, low = split(wide[...])
    r1_ref[:FEATS, :] = high
    r1_ref[FEATS:, :] = low
    wide[NZ : NZ + 1, :] = b1_ref[...]
    high, low = split(wide[...].T)
    f1_ref[:HID, :] = high
    f1_ref[HID:, :] = low
    high, low = split(w2_ref[...])
    r2_ref[:HID, :] = high
    r2_ref[HID:, :] = low
    high, low = split(w2_ref[...].T)
    f2_ref[:HID, :] = high
    f2_ref[HID:, :] = low
    tall[...] = jnp.zeros_like(tall)
    tall[:NZ, :] = w3t_ref[...]
    high, low = split(tall[:PAD, :])
    f3_ref[:PAD, :] = high
    f3_ref[PAD:, :] = low
    tall[PAD : 2 * PAD, :] = tall[:PAD, :]
    tall[2 * PAD :, :] = tall[:PAD, :]
    high, low = split(tall[...].T)
    lane = lax.broadcasted_iota(jnp.int32, high.shape, 1)
    middle = (lane >= PAD) & (lane < 2 * PAD)
    r3_ref[...] = jnp.where(middle, low.astype(F32), high.astype(F32)).astype(BF)
    c2_ref[...] = jnp.broadcast_to(b2_ref[...], (8, HID)).T[:, :1]
    c3_ref[...] = jnp.zeros_like(c3_ref)
    c3_ref[:NZ, :] = jnp.broadcast_to(b3_ref[...], (8, NZ)).T[:, :1]


WEIGHTS = ((2 * HID, FEATS), (2 * HID, HID), (2 * PAD, HID), (HID, FEATS), (2 * HID, HID), (2 * FEATS, HID))


def weights(*args):
    outs = tuple(far(*shape, dtype=BF) for shape in WEIGHTS) + (far(HID, 1), far(PAD, 1))
    return call(weights_kernel, "weights", outs, args, scratch=[near(FEATS, HID), near(FEATS, HID)])


def edge_plane(x, plane, mask_row, fy_row, ew_ref, ee_ref):
    weighted = plane * mask_row
    lane = lax.broadcasted_iota(jnp.int32, plane.shape, 1)
    west = pltpu.roll(weighted * (flat_mix + 0.5 * fy_row), x, 1)
    east = pltpu.roll(weighted * (flat_mix - 0.5 * fy_row), x + 1, 1)
    ew_ref[...] = jnp.where(lane == x, west, ew_ref[...])
    ee_ref[...] = jnp.where(lane == x, east, ee_ref[...])


def north_edge(plane, mask_row, fx_row):
    return plane * mask_row * (flat_mix + 0.5 * fx_row)


def south_edge(plane, mask_row, fx_row):
    return plane * mask_row * (flat_mix - 0.5 * fx_row)


def row(ref, x):
    return ref[x : x + 1, :].astype(F32)


def local_plane(x, lam_ref, mask_ref, fx_ref, fy_ref):
    weighted = lam_ref[x] * row(mask_ref, x)
    lane = lax.broadcasted_iota(jnp.int32, weighted.shape, 1)
    fy = row(fy_ref, x)
    west = pltpu.roll(weighted * (flat_mix + 0.5 * fy), CY - 1, 1)
    east = pltpu.roll(weighted * (flat_mix - 0.5 * fy), 1, 1)
    total = jnp.where(lane == CY - 1, 0.0, west) + jnp.where(lane == 0, 0.0, east) - weighted
    if x < CX - 1:
        total = total + north_edge(lam_ref[x + 1], row(mask_ref, x + 1), row(fx_ref, x + 1))
    if x > 0:
        total = total + south_edge(lam_ref[x - 1], row(mask_ref, x - 1), row(fx_ref, x - 1))
    return total


def halo_lanes(x, hw_ref, he_ref):
    lane = lax.broadcasted_iota(jnp.int32, hw_ref.shape, 1)
    east = he_ref[...] if x == 0 else pltpu.roll(he_ref[...], CY - x, 1)
    west = pltpu.roll(hw_ref[...], CY - 1 - x, 1)
    return jnp.where(lane == CY - 1, west, 0.0) + jnp.where(lane == 0, east, 0.0)


def put_edges(lam_ref, mask_ref, fx_ref, fy_ref, en_ref, es_ref, ew_ref, ee_ref):
    ew_ref[...] = jnp.zeros_like(ew_ref)
    ee_ref[...] = jnp.zeros_like(ee_ref)
    for x in range(CX):
        edge_plane(x, lam_ref[x], row(mask_ref, x), row(fy_ref, x), ew_ref, ee_ref)
    en_ref[...] = north_edge(lam_ref[0], row(mask_ref, 0), row(fx_ref, 0))
    es_ref[...] = south_edge(lam_ref[CX - 1], row(mask_ref, CX - 1), row(fx_ref, CX - 1))


def edges_kernel(raw_ref, mask_ref, fx_ref, fy_ref, planes_ref, base_ref, en_ref, es_ref, ew_ref, ee_ref):
    planes_ref[...] = jnp.zeros_like(planes_ref)
    for x in range(CX):
        for t in range(TRACERS):
            planes_ref[x, t * PAD : t * PAD + NZ, :] = raw_ref[pl.ds(t * NZ * CX + x, NZ, stride=CX), :]
    put_edges(planes_ref, mask_ref, fx_ref, fy_ref, en_ref, es_ref, ew_ref, ee_ref)
    for x in range(CX):
        base_ref[x] = planes_ref[x] + step_size * local_plane(x, planes_ref, mask_ref, fx_ref, fy_ref)


EDGE = far(FEATS, CY)
PLANE = (CX, FEATS, CY)


def edges(*args):
    return call(edges_kernel, "edges", (far(*PLANE), far(*PLANE), EDGE, EDGE, EDGE, EDGE), args)


def last_kernel(mask_ref, fx_ref, fy_ref, hw_ref, he_ref, lam_far, down_far, out_ref, lam, down, sems):
    wait = bring(((0, lam_far, lam), (0, down_far, down)), sems)
    wait(0)
    for x in range(CX):
        total = local_plane(x, lam, mask_ref, fx_ref, fy_ref) + halo_lanes(x, hw_ref, he_ref)
        value = lam[x] + step_size * (total + down[x])
        for t in range(TRACERS):
            out_ref[pl.ds(t * NZ * CX + x, NZ, stride=CX), :] = value[t * PAD : t * PAD + NZ]


def last_stencil(lam, down, *args):
    scratch = [near(*PLANE), near(*PLANE), pltpu.SemaphoreType.DMA((2,))]
    (out,) = call(last_kernel, "stencil0", (near(TRACERS * NZ * CX, CY),), args, (lam, down), scratch, mib=8)
    return out


def rows_kernel(part_ref, hn_ref, hs_ref, out_ref):
    for x, halo_ref in ((0, hs_ref), (CX - 1, hn_ref)):
        for t in range(TRACERS):
            rows = pl.ds(t * NZ * CX + x, NZ, stride=CX)
            out_ref[rows, :] = part_ref[rows, :] + step_size * halo_ref[t * PAD : t * PAD + NZ, :]


def add_rows(part, hn, hs):
    (out,) = call(rows_kernel, "rows0", (near(*part.shape),), (part, hn, hs), aliases={0: 0})
    return out


def closure_step(first, got_ref, owner_ref, mask_ref, lam_ref, weight_refs, out_ref, rows_ref, total, wait):
    f1_ref, f2_ref, f3_ref, r3_ref, r2_ref, r1_ref, b2_ref, b3_ref = weight_refs
    for half in range(2):
        for g in range(DEV // 8):
            at = half * (STORE // 2) + g * 128
            lo = first + half * HALF
            main = [got_ref[8 * g + i, lo : lo + HALF, :] for i in range(8)]
            rows_ref[: 2 * PAD, at : at + 128] = jnp.concatenate(main, axis=0).T
    for g in range(DEV // 8):
        rest = [got_ref[8 * g + i, first + SLOT : first + BLOCK, :] for i in range(8)]
        both = jnp.concatenate(rest, axis=0).T
        rows_ref[2 * PAD :, g * 128 : (g + 1) * 128] = both[:PAD]
        at = STORE // 2 + g * 128
        rows_ref[2 * PAD :, at : at + 128] = both[PAD:]

    def wide(ref):
        return jnp.concatenate([ref[i : i + 1, :] for i in range(CX)], axis=1)

    wait("tile")
    owner = wide(owner_ref)
    at = ((owner >> 4) & 1) * (STORE // 2) + (owner >> 5) * HALF + (owner & (HALF - 1))
    level = lax.broadcasted_iota(jnp.int32, (256, COLS), 0)
    picked = None
    for k in range(STORE // 256):
        hot = jnp.where(level == at - 256 * k, 1.0, 0.0).astype(BF)
        part = dot(rows_ref[:, 256 * k : 256 * (k + 1)], hot)
        picked = part if picked is None else picked + part
    row = lax.broadcasted_iota(jnp.int32, (FEATS, COLS), 0)
    inputs = jnp.where(row == NZ, 1.0, picked).astype(BF)

    wait("weights")
    both = dot(f1_ref[...], inputs)
    h1 = jnp.tanh(both[:HID] + both[HID:])
    h1_high, h1_low = split(h1)
    both = dot(f2_ref[...], h1_high)
    h2 = jnp.tanh(both[:HID] + both[HID:] + dot(f2_ref[:HID], h1_low) + b2_ref[...])
    h2_high, h2_low = split(h2)
    both = dot(f3_ref[...], h2_high)
    sig = jax.nn.sigmoid(both[:PAD] + both[PAD:] + dot(f3_ref[:PAD], h2_low) + b3_ref[...])
    inner = lax.broadcasted_iota(jnp.int32, (PAD, COLS), 0) < NZ - 1
    kappa = jnp.where(inner, kappa_top * sig, 0.0)

    wait("lam")
    mask_row = wide(mask_ref).astype(F32)
    slope = jnp.zeros((PAD, COLS), F32)
    direct = []
    for t in range(TRACERS):
        lo, hi = t * PAD, (t + 1) * PAD
        mu = jnp.concatenate([lam_ref[i, lo:hi, :] for i in range(CX)], axis=1) * mask_row
        gap = mu - pltpu.roll(mu, PAD - 1, 0)
        column = picked[lo:hi]
        slope = slope + gap * (pltpu.roll(column, PAD - 1, 0) - column)
        flow = kappa * gap
        direct.append(pltpu.roll(flow, 1, 0) - flow)
    d3 = slope * kappa * (1.0 - sig)
    d3_high, d3_low = split(d3)
    d2 = dot(r3_ref[...], jnp.concatenate([d3_high, d3_high, d3_low], axis=0)) * (1.0 - h2 * h2)
    d2_high, d2_low = split(d2)
    both = dot(r2_ref[...], d2_high)
    d1 = (both[:HID] + both[HID:] + dot(r2_ref[:HID], d2_low)) * (1.0 - h1 * h1)
    d1_high, d1_low = split(d1)
    both = dot(r1_ref[...], d1_high)
    d0 = both[:FEATS] + both[FEATS:] + dot(r1_ref[:FEATS], d1_low)

    for i in range(CX):
        part = slice(i * CY, (i + 1) * CY)
        for t in range(TRACERS):
            lo, hi = t * PAD, (t + 1) * PAD
            out_ref[i, lo:hi, :] = d0[lo:hi, part] + direct[t][:, part]
    wait("out")

    ones = jnp.ones((16, COLS), BF)
    total[:FEATS, :] += dot_nt(inputs, d1_high) + dot_nt(inputs, d1_low)
    both = dot_nt(jnp.concatenate([h1_high, h1_low, ones], axis=0), d2_high)
    other = dot_nt(jnp.concatenate([h1_high, ones], axis=0), d2_low)
    total[FEATS : FEATS + HID, :] += both[:HID] + both[HID : 2 * HID] + other[:HID]
    total[NZ + 1 : NZ + 2, :] += both[2 * HID : 2 * HID + 1] + other[HID : HID + 1]
    d3_both = jnp.concatenate([d3_high, d3_low], axis=0)
    both = dot_nt(d3_both, h2_high)
    total[FEATS + HID :, :] += both[:PAD] + both[PAD:] + dot_nt(d3_high, h2_low)
    both = dot_nt(ones, d3_both)
    total[NZ + 2 : NZ + 3, :PAD] += both[:1, :PAD] + both[:1, PAD:]


def late_kernel(got_ref, *refs):
    sources, (out_ref, total), refs = refs[:12], refs[12:14], refs[14:]
    targets, (rows_ref, down, sems) = refs[:12], refs[12:]
    names = ("tile", "tile") + ("weights",) * 8 + ("lam", "base")
    wait = bring(zip(names, sources, targets), sems)
    owner, mask, *split_weights = targets[:10]
    planes, base = targets[10:]
    total[...] = jnp.zeros_like(total)

    def then(name):
        wait(name)
        if name == "out":
            wait("base")
            for x in range(CX):
                out_ref[x] = base[x] + step_size * down[x]

    closure_step(BLOCK, got_ref, owner, mask, planes, split_weights, down, rows_ref, total, then)


def early_kernel(got_ref, fx_ref, fy_ref, part_ref, before_ref, owner_ref, mask_ref, *refs):
    split_weights, halos, refs = refs[:8], refs[8:12], refs[12:]
    (lam_far, down_far, grads_ref), sides, (rows_ref, lam, down, total, out_sems) = refs[:3], refs[3:7], refs[7:]
    hn_ref, hs_ref, hw_ref, he_ref = halos
    for x in range(CX):
        halo = halo_lanes(x, hw_ref, he_ref)
        if x == 0:
            halo = halo + hs_ref[...]
        if x == CX - 1:
            halo = halo + hn_ref[...]
        lam[x] = part_ref[x] + step_size * halo
    lam_copy = pltpu.make_async_copy(lam, lam_far, out_sems.at[0])
    lam_copy.start()
    down_copy = pltpu.make_async_copy(down, down_far, out_sems.at[1])
    put_edges(lam, mask_ref, fx_ref, fy_ref, *sides)
    total[...] = before_ref[...]

    def then(name):
        if name == "out":
            down_copy.start()

    closure_step(0, got_ref, owner_ref, mask_ref, lam, split_weights, down, rows_ref, total, then)
    grads_ref[: 2 * HID, :] = total[:, :128]
    grads_ref[2 * HID :, :] = total[:, 128:]
    lam_copy.wait()
    down_copy.wait()


TILE_WEIGHTS = [near(CX, CY, dtype=jnp.int32)] * 2
TILE_WEIGHTS += [near(*shape, dtype=BF) for shape in WEIGHTS] + [near(HID, 1), near(PAD, 1)]
ROWS = near(FEATS, STORE, dtype=BF)


def late_closure(got, *copied):
    outs = (near(*PLANE), near(2 * HID, HID), *TILE_WEIGHTS)
    scratch = [near(*PLANE), near(*PLANE), ROWS, near(*PLANE), pltpu.SemaphoreType.DMA((12,))]
    return call(late_kernel, "closure1", outs, (got,), copied, scratch, CLOSURE_MIB)


def early_closure(got, fx, fy, part, before, brought, halos):
    outs = ([far(*PLANE)], [far(*PLANE)], far(4 * HID, 128), EDGE, EDGE, EDGE, EDGE)
    scratch = [ROWS, near(*PLANE), near(*PLANE), near(2 * HID, HID), pltpu.SemaphoreType.DMA((2,))]
    args = (got, fx, fy, part, before, *brought, *halos)
    return call(early_kernel, "closure0", outs, args, (), scratch, CLOSURE_MIB)


def sum_kernel(parts_ref, out_ref):
    value = parts_ref[0:8, :]
    for i in range(1, DEV):
        value = value + parts_ref[8 * i : 8 * i + 8, :]
    for i in range(DEV):
        out_ref[8 * i : 8 * i + 8, :] = value


def unpack_kernel(scale, sums_ref, w1_ref, b1_ref, w2_ref, b2_ref, w3t_ref, b3_ref):
    for part in range(2):
        lanes = slice(part * 128, (part + 1) * 128)
        top = part * 2 * HID
        for t in range(TRACERS):
            w1_ref[t * NZ : (t + 1) * NZ, lanes] = sums_ref[top + t * PAD : top + t * PAD + NZ, :] * scale
        b1_ref[:, lanes] = sums_ref[top + NZ : top + NZ + 1, :] * scale
        b2_ref[:, lanes] = sums_ref[top + NZ + 1 : top + NZ + 2, :] * scale
        w2_ref[:, lanes] = sums_ref[top + FEATS : top + FEATS + HID, :] * scale
        w3t_ref[:, lanes] = sums_ref[top + FEATS + HID : top + FEATS + HID + NZ, :] * scale
    b3_ref[...] = sums_ref[NZ + 2 : NZ + 3, :NZ] * scale


def reduce_params(packed):
    parts = lax.all_to_all(packed, ("gx", "gy"), split_axis=0, concat_axis=0, tiled=True)
    (spread,) = call(sum_kernel, "sum", (far(*packed.shape),), (parts,))
    return spread


def finish_params(spread, count):
    sums = lax.all_to_all(spread, ("gx", "gy"), split_axis=0, concat_axis=0, tiled=True)
    shapes = ((TRACERS * NZ, HID), (1, HID), (HID, HID), (1, HID), (NZ, HID), (1, NZ))
    scale = step_size / float(np.sqrt(count))
    outs = tuple(far(*shape) for shape in shapes)
    return call(functools.partial(unpack_kernel, scale), "unpack", outs, (sums,))


def exchange(axis, before, after):
    up = [(i, i + 1) for i in range(lax.axis_size(axis) - 1)]
    down = [(j, i) for i, j in up]
    return lax.ppermute(before, axis, down), lax.ppermute(after, axis, up)


def on_device(
    stored,
    counts,
    owners,
    land_mask,
    flow_x,
    flow_y,
    costate,
    weight_in,
    bias_in,
    weight_mid,
    bias_mid,
    weight_out,
    bias_out,
):
    payload = pack(counts, stored[0].T)
    costate, weight_mid, payload = lax.optimization_barrier((costate, weight_mid, payload))
    got = lax.all_to_all(payload, ("gx", "gy"), split_axis=0, concat_axis=0, tiled=True)
    split_weights = weights(
        weight_in, bias_in[None, :], weight_mid, bias_mid[None, :], weight_out.T, bias_out[None, :]
    )
    planes, base, north, south, west, east = edges(
        costate.reshape(TRACERS * NZ * CX, CY), land_mask, flow_x, flow_y
    )
    halos = exchange("gx", north, south) + exchange("gy", west, east)
    part, grads, *brought = late_closure(got, owners, land_mask, *split_weights, planes, base)
    lam, down, packed, north, south, west, east = early_closure(got, flow_x, flow_y, part, grads, brought, halos)
    halos_y = exchange("gy", west, east)
    spread = reduce_params(packed)
    north, south, spread, halos_y = lax.optimization_barrier((north, south, spread, halos_y))
    halos_x = exchange("gx", north, south)
    lam, down, spread = lax.optimization_barrier((lam, down, spread))
    adjoint = last_stencil(lam, down, land_mask, flow_x, flow_y, *halos_y)
    adjoint = add_rows(adjoint, *halos_x)
    count = CX * CY * lax.axis_size("gx") * lax.axis_size("gy")
    g1, gb1, g2, gb2, g3, gb3 = finish_params(spread, count)
    return (adjoint.reshape(costate.shape), g1, gb1[0], g2, gb2[0], g3.T, gb3[0])


def solution(mesh):
    in_specs = (
        P(("gx", "gy"), None, None),
        P(("gx", "gy"), None),
        P("gx", "gy"),
        P("gx", "gy"),
        P("gx", "gy"),
        P("gx", "gy"),
        P(None, None, "gx", "gy"),
        P(),
        P(),
        P(),
        P(),
        P(),
        P(),
    )
    out_specs = (P(None, None, "gx", "gy"), P(), P(), P(), P(), P(), P())
    return jax.shard_map(
        on_device, mesh=mesh, in_specs=in_specs, out_specs=out_specs, check_vma=False
    )
```

```python
import functools

import jax
import jax.numpy as jnp
import numpy as np
from jax import lax
from jax.experimental import pallas as pl
from jax.experimental.pallas import tpu as pltpu
from jax.sharding import PartitionSpec as P

NZ = 60
TRACERS = 3
PAD = 64
FEATS = TRACERS * PAD
HID = 256
SLOT = 32
HALF = SLOT // 2
BLOCK = SLOT + HALF
CX = 16
CY = 128
APART = 8
DEV = 128
STORE = 4096
UNROLL = DEV // 8
BATCH = 4
COLS = CX * CY

CLOSURE_MIB = 24

BF = jnp.bfloat16
F32 = jnp.float32
NT = (((1,), (1,)), ((), ()))

step_size = 0.25
flat_mix = 0.25
kappa_top = 1.5


def split(value):
    high = value.astype(BF)
    return high, (value - high.astype(F32)).astype(BF)


def dot(left, right):
    return jnp.dot(left, right, preferred_element_type=F32)


def dot_nt(left, right):
    return lax.dot_general(left, right, NT, preferred_element_type=F32)


def params(mib):
    return pltpu.CompilerParams(vmem_limit_bytes=mib * 2**20)


def bring(copies, sems):
    started = {}
    for i, (name, source, target) in enumerate(copies):
        started.setdefault(name, []).append(pltpu.make_async_copy(source, target, sems.at[i]))
        started[name][-1].start()

    def wait(name):
        for copy in started.pop(name, ()):
            copy.wait()

    return wait


def near(*shape, dtype=F32):
    return pltpu.VMEM(shape, dtype)


def far(*shape, dtype=F32):
    return pltpu.HBM(shape, dtype)


def call(kernel, name, outs, args, copied=(), scratch=(), mib=4, aliases={}):
    args = [pltpu.with_memory_space_constraint(a, pltpu.VMEM) for a in args]
    copied = [pltpu.with_memory_space_constraint(a, pltpu.HBM) for a in copied]
    inside = pl.BlockSpec(memory_space=pltpu.VMEM)
    anywhere = pl.BlockSpec(memory_space=pl.ANY)
    return pl.pallas_call(
        kernel,
        out_shape=tuple(out[0] if isinstance(out, list) else out for out in outs),
        in_specs=[inside] * len(args) + [anywhere] * len(copied),
        out_specs=tuple(anywhere if isinstance(out, list) else inside for out in outs),
        scratch_shapes=list(scratch),
        input_output_aliases=aliases,
        compiler_params=params(mib),
        name=name,
    )(*args, *copied)


def pack_kernel(counts_ref, stored_ref, out_ref, near, padded, rows_out, in_sems, out_sem):
    cut = STORE // 2 + 128
    parts = (slice(0, cut), slice(cut, STORE))
    copies = [pltpu.make_async_copy(stored_ref.at[:, p], near.at[:, p], in_sems.at[i]) for i, p in enumerate(parts)]
    for copy in copies:
        copy.start()
    lane = lax.broadcasted_iota(jnp.int32, (SLOT, 256), 1)
    offset = lane - lax.broadcasted_iota(jnp.int32, (SLOT, 256), 0)
    for block in range(2 * TRACERS):
        padded[block * PAD + NZ : (block + 1) * PAD, :] = jnp.zeros((PAD - NZ, STORE), BF)

    def arrive(half):
        copies[half].wait()
        for block in range(2 * TRACERS):
            padded[block * PAD : block * PAD + NZ, parts[half]] = near[block * NZ : (block + 1) * NZ, parts[half]]

    def group(g, start):
        base = pl.multiple_of(jnp.minimum((start // 128) * 128, STORE - 256), 128)
        hots = []
        for i in range(4):
            hots.append(jnp.where(offset == start - base, 1.0, 0.0).astype(BF))
            start = start + counts_ref[0, 4 * g + i]
        rows = dot_nt(jnp.concatenate(hots, axis=0), padded[:, pl.ds(base, 256)])
        for i in range(4):
            for moment in range(2):
                at, first = moment * BLOCK, moment * FEATS
                mine = rows[i * SLOT : (i + 1) * SLOT, first : first + FEATS]
                rest = jnp.concatenate([mine[:HALF, 2 * PAD :], mine[HALF:, 2 * PAD :]], axis=1)
                rows_out[4 * g + i, at : at + SLOT, :] = mine[:, : 2 * PAD].astype(BF)
                rows_out[4 * g + i, at + SLOT : at + BLOCK, :] = rest.astype(BF)
        return start

    def leave(j):
        tiles = pl.ds(j * 4 * BATCH, 4 * BATCH)
        return pltpu.make_async_copy(rows_out.at[tiles], out_ref.at[tiles], out_sem.at[j])

    def groups(half, start):
        pl.when(half == 0)(functools.partial(arrive, 0))
        pl.when(half == 1)(functools.partial(arrive, 1))
        for u in range(UNROLL):
            start = group(half * UNROLL + u, start)
            if u % BATCH == BATCH - 1:
                leave(half * (UNROLL // BATCH) + u // BATCH).start()
        return start

    lax.fori_loop(0, 2, groups, jnp.int32(0))
    for j in range(DEV // 4 // BATCH):
        leave(j).wait()


def pack(counts, stored_t):
    anywhere = pl.BlockSpec(memory_space=pl.ANY)
    return pl.pallas_call(
        pack_kernel,
        out_shape=pltpu.HBM((DEV, 2 * BLOCK, 128), BF),
        in_specs=[pl.BlockSpec(memory_space=pltpu.SMEM), anywhere],
        out_specs=anywhere,
        scratch_shapes=[
            pltpu.VMEM((2 * TRACERS * NZ, STORE), BF),
            pltpu.VMEM((2 * FEATS, STORE), BF),
            pltpu.VMEM((DEV, 2 * BLOCK, 128), BF),
            pltpu.SemaphoreType.DMA((2,)),
            pltpu.SemaphoreType.DMA((DEV // 4 // BATCH,)),
        ],
        compiler_params=params(24),
        name="pack",
    )(*(pltpu.with_memory_space_constraint(a, pltpu.HBM) for a in (counts, stored_t)))


def weights_kernel(w1_ref, b1_ref, w2_ref, b2_ref, w3t_ref, b3_ref, *refs):
    f1_ref, f2_ref, f3_ref, r3_ref, r2_ref, r1_ref, c2_ref, c3_ref, wide, tall = refs
    wide[...] = jnp.zeros_like(wide)
    for t in range(TRACERS):
        wide[t * PAD : t * PAD + NZ, :] = w1_ref[t * NZ : (t + 1) * NZ, :]
    high, low = split(wide[...])
    r1_ref[:FEATS, :] = high
    r1_ref[FEATS:, :] = low
    wide[NZ : NZ + 1, :] = b1_ref[...]
    high, low = split(wide[...].T)
    f1_ref[:HID, :] = high
    f1_ref[HID:, :] = low
    high, low = split(w2_ref[...])
    r2_ref[:HID, :] = high
    r2_ref[HID:, :] = low
    high, low = split(w2_ref[...].T)
    f2_ref[:HID, :] = high
    f2_ref[HID:, :] = low
    tall[...] = jnp.zeros_like(tall)
    tall[:NZ, :] = w3t_ref[...]
    high, low = split(tall[:PAD, :])
    f3_ref[:PAD, :] = high
    f3_ref[PAD:, :] = low
    tall[PAD : 2 * PAD, :] = tall[:PAD, :]
    tall[2 * PAD :, :] = tall[:PAD, :]
    high, low = split(tall[...].T)
    lane = lax.broadcasted_iota(jnp.int32, high.shape, 1)
    middle = (lane >= PAD) & (lane < 2 * PAD)
    r3_ref[...] = jnp.where(middle, low.astype(F32), high.astype(F32)).astype(BF)
    c2_ref[...] = jnp.broadcast_to(b2_ref[...], (8, HID)).T[:, :1]
    c3_ref[...] = jnp.zeros_like(c3_ref)
    c3_ref[:NZ, :] = jnp.broadcast_to(b3_ref[...], (8, NZ)).T[:, :1]


WEIGHTS = ((2 * HID, FEATS), (2 * HID, HID), (2 * PAD, HID), (HID, FEATS), (2 * HID, HID), (2 * FEATS, HID))


def weights(*args):
    outs = tuple(far(*shape, dtype=BF) for shape in WEIGHTS) + (far(HID, 1), far(PAD, 1))
    return call(weights_kernel, "weights", outs, args, scratch=[near(FEATS, HID), near(FEATS, HID)])


def north_edge(plane, mask_row, fx_row):
    return plane * mask_row * (flat_mix + 0.5 * fx_row)


def south_edge(plane, mask_row, fx_row):
    return plane * mask_row * (flat_mix - 0.5 * fx_row)


def row(ref, x):
    return ref[x : x + 1, :].astype(F32)


def local_plane(x, lam_ref, mask_ref, fx_ref, fy_ref):
    weighted = lam_ref[x] * row(mask_ref, x)
    lane = lax.broadcasted_iota(jnp.int32, weighted.shape, 1)
    fy = row(fy_ref, x)
    west = pltpu.roll(weighted * (flat_mix + 0.5 * fy), CY - 1, 1)
    east = pltpu.roll(weighted * (flat_mix - 0.5 * fy), 1, 1)
    total = jnp.where(lane == CY - 1, 0.0, west) + jnp.where(lane == 0, 0.0, east) - weighted
    if x < CX - 1:
        total = total + north_edge(lam_ref[x + 1], row(mask_ref, x + 1), row(fx_ref, x + 1))
    if x > 0:
        total = total + south_edge(lam_ref[x - 1], row(mask_ref, x - 1), row(fx_ref, x - 1))
    return total


def join_lanes(hw_ref, he_ref):
    lane = lax.broadcasted_iota(jnp.int32, hw_ref.shape, 1)
    return jnp.where(lane % APART == APART - 1, pltpu.roll(hw_ref[...], CY - 1, 1), he_ref[...])


def halo_lanes(x, joined):
    lane = lax.broadcasted_iota(jnp.int32, joined.shape, 1)
    here = joined if x == 0 else pltpu.roll(joined, CY - APART * x, 1)
    return jnp.where((lane == 0) | (lane == CY - 1), here, 0.0)


def put_edges(lam_ref, mask_ref, fx_ref, fy_ref, en_ref, es_ref, ew_ref, ee_ref):
    lane = lax.broadcasted_iota(jnp.int32, (PAD, CY), 1)
    for t in range(TRACERS):
        levels = slice(t * PAD, (t + 1) * PAD)
        west = east = jnp.zeros((PAD, CY), F32)
        for x in range(CX):
            weighted = lam_ref[x, levels, :] * row(mask_ref, x)
            fy = row(fy_ref, x)
            at = APART * x
            west = jnp.where(lane == at, pltpu.roll(weighted * (flat_mix + 0.5 * fy), at, 1), west)
            east = jnp.where(lane == at, pltpu.roll(weighted * (flat_mix - 0.5 * fy), at + 1, 1), east)
        ew_ref[levels, :] = west
        ee_ref[levels, :] = east
    en_ref[...] = north_edge(lam_ref[0], row(mask_ref, 0), row(fx_ref, 0))
    es_ref[...] = south_edge(lam_ref[CX - 1], row(mask_ref, CX - 1), row(fx_ref, CX - 1))


def edges_kernel(raw_ref, mask_ref, fx_ref, fy_ref, planes_ref, base_ref, en_ref, es_ref, ew_ref, ee_ref):
    planes_ref[...] = jnp.zeros_like(planes_ref)
    for x in range(CX):
        for t in range(TRACERS):
            planes_ref[x, t * PAD : t * PAD + NZ, :] = raw_ref[pl.ds(t * NZ * CX + x, NZ, stride=CX), :]
    put_edges(planes_ref, mask_ref, fx_ref, fy_ref, en_ref, es_ref, ew_ref, ee_ref)
    for x in range(CX):
        base_ref[x] = planes_ref[x] + step_size * local_plane(x, planes_ref, mask_ref, fx_ref, fy_ref)


EDGE = far(FEATS, CY)
PLANE = (CX, FEATS, CY)


def edges(*args):
    return call(edges_kernel, "edges", (far(*PLANE), far(*PLANE), EDGE, EDGE, EDGE, EDGE), args, mib=8)


def last_kernel(mask_ref, fx_ref, fy_ref, hw_ref, he_ref, lam_far, down_far, out_ref, lam, down, sems):
    wait = bring(((0, lam_far, lam), (0, down_far, down)), sems)
    joined = join_lanes(hw_ref, he_ref)
    wait(0)
    for x in range(CX):
        total = local_plane(x, lam, mask_ref, fx_ref, fy_ref) + halo_lanes(x, joined)
        value = lam[x] + step_size * (total + down[x])
        for t in range(TRACERS):
            out_ref[pl.ds(t * NZ * CX + x, NZ, stride=CX), :] = value[t * PAD : t * PAD + NZ]


def last_stencil(lam, down, *args):
    scratch = [near(*PLANE), near(*PLANE), pltpu.SemaphoreType.DMA((2,))]
    (out,) = call(last_kernel, "stencil0", (near(TRACERS * NZ * CX, CY),), args, (lam, down), scratch, mib=8)
    return out


def rows_kernel(part_ref, hn_ref, hs_ref, out_ref):
    for x, halo_ref in ((0, hs_ref), (CX - 1, hn_ref)):
        for t in range(TRACERS):
            rows = pl.ds(t * NZ * CX + x, NZ, stride=CX)
            out_ref[rows, :] = part_ref[rows, :] + step_size * halo_ref[t * PAD : t * PAD + NZ, :]


def add_rows(part, hn, hs):
    (out,) = call(rows_kernel, "rows0", (near(*part.shape),), (part, hn, hs), aliases={0: 0})
    return out


def closure_step(first, got_ref, owner_ref, mask_ref, lam_ref, weight_refs, out_ref, rows_ref, total, wait):
    f1_ref, f2_ref, f3_ref, r3_ref, r2_ref, r1_ref, b2_ref, b3_ref = weight_refs
    for half in range(2):
        for g in range(DEV // 8):
            at = half * (STORE // 2) + g * 128
            lo = first + half * HALF
            main = [got_ref[8 * g + i, lo : lo + HALF, :] for i in range(8)]
            rows_ref[: 2 * PAD, at : at + 128] = jnp.concatenate(main, axis=0).T
    for g in range(DEV // 8):
        rest = [got_ref[8 * g + i, first + SLOT : first + BLOCK, :] for i in range(8)]
        both = jnp.concatenate(rest, axis=0).T
        rows_ref[2 * PAD :, g * 128 : (g + 1) * 128] = both[:PAD]
        at = STORE // 2 + g * 128
        rows_ref[2 * PAD :, at : at + 128] = both[PAD:]

    def wide(ref):
        return jnp.concatenate([ref[i : i + 1, :] for i in range(CX)], axis=1)

    wait("tile")
    owner = wide(owner_ref)
    at = ((owner >> 4) & 1) * (STORE // 2) + (owner >> 5) * HALF + (owner & (HALF - 1))
    level = lax.broadcasted_iota(jnp.int32, (256, COLS), 0)
    picked = None
    for k in range(STORE // 256):
        hot = jnp.where(level == at - 256 * k, 1.0, 0.0).astype(BF)
        part = dot(rows_ref[:, 256 * k : 256 * (k + 1)], hot)
        picked = part if picked is None else picked + part
    row = lax.broadcasted_iota(jnp.int32, (FEATS, COLS), 0)
    inputs = jnp.where(row == NZ, 1.0, picked).astype(BF)

    wait("weights")
    both = dot(f1_ref[...], inputs)
    h1 = jnp.tanh(both[:HID] + both[HID:])
    h1_high, h1_low = split(h1)
    both = dot(f2_ref[...], h1_high)
    h2 = jnp.tanh(both[:HID] + both[HID:] + dot(f2_ref[:HID], h1_low) + b2_ref[...])
    h2_high, h2_low = split(h2)
    both = dot(f3_ref[...], h2_high)
    sig = jax.nn.sigmoid(both[:PAD] + both[PAD:] + dot(f3_ref[:PAD], h2_low) + b3_ref[...])
    inner = lax.broadcasted_iota(jnp.int32, (PAD, COLS), 0) < NZ - 1
    kappa = jnp.where(inner, kappa_top * sig, 0.0)

    wait("lam")
    mask_row = wide(mask_ref).astype(F32)
    slope = jnp.zeros((PAD, COLS), F32)
    direct = []
    for t in range(TRACERS):
        lo, hi = t * PAD, (t + 1) * PAD
        mu = jnp.concatenate([lam_ref[i, lo:hi, :] for i in range(CX)], axis=1) * mask_row
        gap = mu - pltpu.roll(mu, PAD - 1, 0)
        column = picked[lo:hi]
        slope = slope + gap * (pltpu.roll(column, PAD - 1, 0) - column)
        flow = kappa * gap
        direct.append(pltpu.roll(flow, 1, 0) - flow)
    d3 = slope * kappa * (1.0 - sig)
    d3_high, d3_low = split(d3)
    d2 = dot(r3_ref[...], jnp.concatenate([d3_high, d3_high, d3_low], axis=0)) * (1.0 - h2 * h2)
    d2_high, d2_low = split(d2)
    both = dot(r2_ref[...], d2_high)
    d1 = (both[:HID] + both[HID:] + dot(r2_ref[:HID], d2_low)) * (1.0 - h1 * h1)
    d1_high, d1_low = split(d1)
    both = dot(r1_ref[...], d1_high)
    d0 = both[:FEATS] + both[FEATS:] + dot(r1_ref[:FEATS], d1_low)

    for i in range(CX):
        part = slice(i * CY, (i + 1) * CY)
        for t in range(TRACERS):
            lo, hi = t * PAD, (t + 1) * PAD
            out_ref[i, lo:hi, :] = d0[lo:hi, part] + direct[t][:, part]
    wait("out")

    ones = jnp.ones((16, COLS), BF)
    total[:FEATS, :] += dot_nt(inputs, d1_high) + dot_nt(inputs, d1_low)
    both = dot_nt(jnp.concatenate([h1_high, h1_low, ones], axis=0), d2_high)
    other = dot_nt(jnp.concatenate([h1_high, ones], axis=0), d2_low)
    total[FEATS : FEATS + HID, :] += both[:HID] + both[HID : 2 * HID] + other[:HID]
    total[NZ + 1 : NZ + 2, :] += both[2 * HID : 2 * HID + 1] + other[HID : HID + 1]
    d3_both = jnp.concatenate([d3_high, d3_low], axis=0)
    both = dot_nt(d3_both, h2_high)
    total[FEATS + HID :, :] += both[:PAD] + both[PAD:] + dot_nt(d3_high, h2_low)
    both = dot_nt(ones, d3_both)
    total[NZ + 2 : NZ + 3, :PAD] += both[:1, :PAD] + both[:1, PAD:]


def late_kernel(got_ref, *refs):
    sources, (out_ref, total), refs = refs[:12], refs[12:14], refs[14:]
    targets, (rows_ref, down, sems) = refs[:12], refs[12:]
    names = ("tile", "tile") + ("weights",) * 8 + ("lam", "base")
    wait = bring(zip(names, sources, targets), sems)
    owner, mask, *split_weights = targets[:10]
    planes, base = targets[10:]
    total[...] = jnp.zeros_like(total)

    def then(name):
        wait(name)
        if name == "out":
            wait("base")
            for x in range(CX):
                out_ref[x] = base[x] + step_size * down[x]

    closure_step(BLOCK, got_ref, owner, mask, planes, split_weights, down, rows_ref, total, then)


def early_kernel(got_ref, fx_ref, fy_ref, part_ref, before_ref, owner_ref, mask_ref, *refs):
    split_weights, halos, refs = refs[:8], refs[8:12], refs[12:]
    (lam_far, down_far, grads_ref), sides, (rows_ref, lam, down, total, out_sems) = refs[:3], refs[3:7], refs[7:]
    hn_ref, hs_ref, hw_ref, he_ref = halos
    joined = join_lanes(hw_ref, he_ref)
    for x in range(CX):
        halo = halo_lanes(x, joined)
        if x == 0:
            halo = halo + hs_ref[...]
        if x == CX - 1:
            halo = halo + hn_ref[...]
        lam[x] = part_ref[x] + step_size * halo
    lam_copy = pltpu.make_async_copy(lam, lam_far, out_sems.at[0])
    lam_copy.start()
    down_copy = pltpu.make_async_copy(down, down_far, out_sems.at[1])
    put_edges(lam, mask_ref, fx_ref, fy_ref, *sides)
    total[...] = before_ref[...]

    def then(name):
        if name == "out":
            down_copy.start()

    closure_step(0, got_ref, owner_ref, mask_ref, lam, split_weights, down, rows_ref, total, then)
    grads_ref[: 2 * HID, :] = total[:, :128]
    grads_ref[2 * HID :, :] = total[:, 128:]
    lam_copy.wait()
    down_copy.wait()


TILE_WEIGHTS = [near(CX, CY, dtype=jnp.int32)] * 2
TILE_WEIGHTS += [near(*shape, dtype=BF) for shape in WEIGHTS] + [near(HID, 1), near(PAD, 1)]
ROWS = near(FEATS, STORE, dtype=BF)


def late_closure(got, *copied):
    outs = (near(*PLANE), near(2 * HID, HID), *TILE_WEIGHTS)
    scratch = [near(*PLANE), near(*PLANE), ROWS, near(*PLANE), pltpu.SemaphoreType.DMA((12,))]
    return call(late_kernel, "closure1", outs, (got,), copied, scratch, CLOSURE_MIB)


def early_closure(got, fx, fy, part, before, brought, halos):
    outs = ([far(*PLANE)], [far(*PLANE)], far(4 * HID, 128), EDGE, EDGE, EDGE, EDGE)
    scratch = [ROWS, near(*PLANE), near(*PLANE), near(2 * HID, HID), pltpu.SemaphoreType.DMA((2,))]
    args = (got, fx, fy, part, before, *brought, *halos)
    return call(early_kernel, "closure0", outs, args, (), scratch, CLOSURE_MIB)


def sum_kernel(parts_ref, out_ref):
    value = parts_ref[0:8, :]
    for i in range(1, DEV):
        value = value + parts_ref[8 * i : 8 * i + 8, :]
    for i in range(DEV):
        out_ref[8 * i : 8 * i + 8, :] = value


def unpack_kernel(scale, sums_ref, w1_ref, b1_ref, w2_ref, b2_ref, w3t_ref, b3_ref):
    for part in range(2):
        lanes = slice(part * 128, (part + 1) * 128)
        top = part * 2 * HID
        for t in range(TRACERS):
            w1_ref[t * NZ : (t + 1) * NZ, lanes] = sums_ref[top + t * PAD : top + t * PAD + NZ, :] * scale
        b1_ref[:, lanes] = sums_ref[top + NZ : top + NZ + 1, :] * scale
        b2_ref[:, lanes] = sums_ref[top + NZ + 1 : top + NZ + 2, :] * scale
        w2_ref[:, lanes] = sums_ref[top + FEATS : top + FEATS + HID, :] * scale
        w3t_ref[:, lanes] = sums_ref[top + FEATS + HID : top + FEATS + HID + NZ, :] * scale
    b3_ref[...] = sums_ref[NZ + 2 : NZ + 3, :NZ] * scale


def reduce_params(packed):
    parts = lax.all_to_all(packed, ("gx", "gy"), split_axis=0, concat_axis=0, tiled=True)
    (spread,) = call(sum_kernel, "sum", (far(*packed.shape),), (parts,))
    return spread


def finish_params(spread, count):
    sums = lax.all_to_all(spread, ("gx", "gy"), split_axis=0, concat_axis=0, tiled=True)
    shapes = ((TRACERS * NZ, HID), (1, HID), (HID, HID), (1, HID), (NZ, HID), (1, NZ))
    scale = step_size / float(np.sqrt(count))
    outs = tuple(far(*shape) for shape in shapes)
    return call(functools.partial(unpack_kernel, scale), "unpack", outs, (sums,))


def exchange(axis, before, after):
    up = [(i, i + 1) for i in range(lax.axis_size(axis) - 1)]
    down = [(j, i) for i, j in up]
    return lax.ppermute(before, axis, down), lax.ppermute(after, axis, up)


def on_device(
    stored,
    counts,
    owners,
    land_mask,
    flow_x,
    flow_y,
    costate,
    weight_in,
    bias_in,
    weight_mid,
    bias_mid,
    weight_out,
    bias_out,
):
    payload = pack(counts, stored[0].T)
    costate, weight_mid, payload = lax.optimization_barrier((costate, weight_mid, payload))
    got = lax.all_to_all(payload, ("gx", "gy"), split_axis=0, concat_axis=0, tiled=True)
    split_weights = weights(
        weight_in, bias_in[None, :], weight_mid, bias_mid[None, :], weight_out.T, bias_out[None, :]
    )
    planes, base, north, south, west, east = edges(
        costate.reshape(TRACERS * NZ * CX, CY), land_mask, flow_x, flow_y
    )
    halos = exchange("gx", north, south) + exchange("gy", west, east)
    part, grads, *brought = late_closure(got, owners, land_mask, *split_weights, planes, base)
    lam, down, packed, north, south, west, east = early_closure(got, flow_x, flow_y, part, grads, brought, halos)
    halos_y = exchange("gy", west, east)
    spread = reduce_params(packed)
    north, south, spread, halos_y = lax.optimization_barrier((north, south, spread, halos_y))
    halos_x = exchange("gx", north, south)
    lam, down, spread = lax.optimization_barrier((lam, down, spread))
    adjoint = last_stencil(lam, down, land_mask, flow_x, flow_y, *halos_y)
    adjoint = add_rows(adjoint, *halos_x)
    count = CX * CY * lax.axis_size("gx") * lax.axis_size("gy")
    g1, gb1, g2, gb2, g3, gb3 = finish_params(spread, count)
    return (adjoint.reshape(costate.shape), g1, gb1[0], g2, gb2[0], g3.T, gb3[0])


def solution(mesh):
    in_specs = (
        P(("gx", "gy"), None, None),
        P(("gx", "gy"), None),
        P("gx", "gy"),
        P("gx", "gy"),
        P("gx", "gy"),
        P("gx", "gy"),
        P(None, None, "gx", "gy"),
        P(),
        P(),
        P(),
        P(),
        P(),
        P(),
    )
    out_specs = (P(None, None, "gx", "gy"), P(), P(), P(), P(), P(), P())
    return jax.shard_map(
        on_device, mesh=mesh, in_specs=in_specs, out_specs=out_specs, check_vma=False
    )
```

```python
import functools

import jax
import jax.numpy as jnp
import numpy as np
from jax import lax
from jax.experimental import pallas as pl
from jax.experimental.pallas import tpu as pltpu
from jax.sharding import PartitionSpec as P

NZ = 60
TRACERS = 3
PAD = 64
FEATS = TRACERS * PAD
HID = 256
SLOT = 32
HALF = SLOT // 2
BLOCK = SLOT + HALF
CX = 16
CY = 128
APART = 8
DEV = 128
STORE = 4096
UNROLL = DEV // 8
BATCH = 4
COLS = CX * CY

CLOSURE_MIB = 24

BF = jnp.bfloat16
F32 = jnp.float32
NT = (((1,), (1,)), ((), ()))

step_size = 0.25
flat_mix = 0.25
kappa_top = 1.5


def split(value):
    high = value.astype(BF)
    return high, (value - high.astype(F32)).astype(BF)


def dot(left, right):
    return jnp.dot(left, right, preferred_element_type=F32)


def dot_nt(left, right):
    return lax.dot_general(left, right, NT, preferred_element_type=F32)


def params(mib):
    return pltpu.CompilerParams(vmem_limit_bytes=mib * 2**20)


def bring(copies, sems):
    started = {}
    for i, (name, source, target) in enumerate(copies):
        started.setdefault(name, []).append(pltpu.make_async_copy(source, target, sems.at[i]))
        started[name][-1].start()

    def wait(name):
        for copy in started.pop(name, ()):
            copy.wait()

    return wait


def near(*shape, dtype=F32):
    return pltpu.VMEM(shape, dtype)


def far(*shape, dtype=F32):
    return pltpu.HBM(shape, dtype)


def call(kernel, name, outs, args, copied=(), scratch=(), mib=4, aliases={}):
    args = [pltpu.with_memory_space_constraint(a, pltpu.VMEM) for a in args]
    copied = [pltpu.with_memory_space_constraint(a, pltpu.HBM) for a in copied]
    inside = pl.BlockSpec(memory_space=pltpu.VMEM)
    anywhere = pl.BlockSpec(memory_space=pl.ANY)
    return pl.pallas_call(
        kernel,
        out_shape=tuple(out[0] if isinstance(out, list) else out for out in outs),
        in_specs=[inside] * len(args) + [anywhere] * len(copied),
        out_specs=tuple(anywhere if isinstance(out, list) else inside for out in outs),
        scratch_shapes=list(scratch),
        input_output_aliases=aliases,
        compiler_params=params(mib),
        name=name,
    )(*args, *copied)


def pack_kernel(counts_ref, stored_ref, out_ref, near, padded, rows_out, in_sems, out_sem):
    cut = STORE // 2 + 128
    parts = (slice(0, cut), slice(cut, STORE))
    copies = [pltpu.make_async_copy(stored_ref.at[:, p], near.at[:, p], in_sems.at[i]) for i, p in enumerate(parts)]
    for copy in copies:
        copy.start()
    lane = lax.broadcasted_iota(jnp.int32, (SLOT, 256), 1)
    offset = lane - lax.broadcasted_iota(jnp.int32, (SLOT, 256), 0)
    for block in range(2 * TRACERS):
        padded[block * PAD + NZ : (block + 1) * PAD, :] = jnp.zeros((PAD - NZ, STORE), BF)

    def arrive(half):
        copies[half].wait()
        for block in range(2 * TRACERS):
            padded[block * PAD : block * PAD + NZ, parts[half]] = near[block * NZ : (block + 1) * NZ, parts[half]]

    def group(g, start):
        base = pl.multiple_of(jnp.minimum((start // 128) * 128, STORE - 256), 128)
        hots = []
        for i in range(4):
            hots.append(jnp.where(offset == start - base, 1.0, 0.0).astype(BF))
            start = start + counts_ref[0, 4 * g + i]
        rows = dot_nt(jnp.concatenate(hots, axis=0), padded[:, pl.ds(base, 256)])
        for i in range(4):
            for moment in range(2):
                at, first = moment * BLOCK, moment * FEATS
                mine = rows[i * SLOT : (i + 1) * SLOT, first : first + FEATS]
                rest = jnp.concatenate([mine[:HALF, 2 * PAD :], mine[HALF:, 2 * PAD :]], axis=1)
                rows_out[4 * g + i, at : at + SLOT, :] = mine[:, : 2 * PAD].astype(BF)
                rows_out[4 * g + i, at + SLOT : at + BLOCK, :] = rest.astype(BF)
        return start

    def leave(j):
        tiles = pl.ds(j * 4 * BATCH, 4 * BATCH)
        return pltpu.make_async_copy(rows_out.at[tiles], out_ref.at[tiles], out_sem.at[j])

    def groups(half, start):
        pl.when(half == 0)(functools.partial(arrive, 0))
        pl.when(half == 1)(functools.partial(arrive, 1))
        for u in range(UNROLL):
            start = group(half * UNROLL + u, start)
            if u % BATCH == BATCH - 1:
                leave(half * (UNROLL // BATCH) + u // BATCH).start()
        return start

    lax.fori_loop(0, 2, groups, jnp.int32(0))
    for j in range(DEV // 4 // BATCH):
        leave(j).wait()


def pack(counts, stored_t):
    anywhere = pl.BlockSpec(memory_space=pl.ANY)
    return pl.pallas_call(
        pack_kernel,
        out_shape=pltpu.HBM((DEV, 2 * BLOCK, 128), BF),
        in_specs=[pl.BlockSpec(memory_space=pltpu.SMEM), anywhere],
        out_specs=anywhere,
        scratch_shapes=[
            pltpu.VMEM((2 * TRACERS * NZ, STORE), BF),
            pltpu.VMEM((2 * FEATS, STORE), BF),
            pltpu.VMEM((DEV, 2 * BLOCK, 128), BF),
            pltpu.SemaphoreType.DMA((2,)),
            pltpu.SemaphoreType.DMA((DEV // 4 // BATCH,)),
        ],
        compiler_params=params(24),
        name="pack",
    )(*(pltpu.with_memory_space_constraint(a, pltpu.HBM) for a in (counts, stored_t)))


def weights_kernel(w1_ref, b1_ref, w2_ref, b2_ref, w3t_ref, b3_ref, *refs):
    f1_ref, f2_ref, f3_ref, r3_ref, r2_ref, r1_ref, c2_ref, c3_ref, wide, tall = refs
    wide[...] = jnp.zeros_like(wide)
    for t in range(TRACERS):
        wide[t * PAD : t * PAD + NZ, :] = w1_ref[t * NZ : (t + 1) * NZ, :]
    high, low = split(wide[...])
    r1_ref[:FEATS, :] = high
    r1_ref[FEATS:, :] = low
    wide[NZ : NZ + 1, :] = b1_ref[...]
    high, low = split(wide[...].T)
    f1_ref[:HID, :] = high
    f1_ref[HID:, :] = low
    high, low = split(w2_ref[...])
    r2_ref[:HID, :] = high
    r2_ref[HID:, :] = low
    high, low = split(w2_ref[...].T)
    f2_ref[:HID, :] = high
    f2_ref[HID:, :] = low
    tall[...] = jnp.zeros_like(tall)
    tall[:NZ, :] = w3t_ref[...]
    high, low = split(tall[:PAD, :])
    f3_ref[:PAD, :] = high
    f3_ref[PAD:, :] = low
    tall[PAD : 2 * PAD, :] = tall[:PAD, :]
    tall[2 * PAD :, :] = tall[:PAD, :]
    high, low = split(tall[...].T)
    lane = lax.broadcasted_iota(jnp.int32, high.shape, 1)
    middle = (lane >= PAD) & (lane < 2 * PAD)
    r3_ref[...] = jnp.where(middle, low.astype(F32), high.astype(F32)).astype(BF)
    c2_ref[...] = jnp.broadcast_to(b2_ref[...], (8, HID)).T[:, :1]
    c3_ref[...] = jnp.zeros_like(c3_ref)
    c3_ref[:NZ, :] = jnp.broadcast_to(b3_ref[...], (8, NZ)).T[:, :1]


WEIGHTS = ((2 * HID, FEATS), (2 * HID, HID), (2 * PAD, HID), (HID, FEATS), (2 * HID, HID), (2 * FEATS, HID))


def weights(*args):
    outs = tuple(far(*shape, dtype=BF) for shape in WEIGHTS) + (far(HID, 1), far(PAD, 1))
    return call(weights_kernel, "weights", outs, args, scratch=[near(FEATS, HID), near(FEATS, HID)])


def north_edge(plane, mask_row, fx_row):
    return plane * mask_row * (flat_mix + 0.5 * fx_row)


def south_edge(plane, mask_row, fx_row):
    return plane * mask_row * (flat_mix - 0.5 * fx_row)


def row(ref, x):
    return ref[x : x + 1, :].astype(F32)


def local_plane(x, lam_ref, mask_ref, fx_ref, fy_ref):
    weighted = lam_ref[x] * row(mask_ref, x)
    lane = lax.broadcasted_iota(jnp.int32, weighted.shape, 1)
    fy = row(fy_ref, x)
    west = pltpu.roll(weighted * (flat_mix + 0.5 * fy), CY - 1, 1)
    east = pltpu.roll(weighted * (flat_mix - 0.5 * fy), 1, 1)
    total = jnp.where(lane == CY - 1, 0.0, west) + jnp.where(lane == 0, 0.0, east) - weighted
    if x < CX - 1:
        total = total + north_edge(lam_ref[x + 1], row(mask_ref, x + 1), row(fx_ref, x + 1))
    if x > 0:
        total = total + south_edge(lam_ref[x - 1], row(mask_ref, x - 1), row(fx_ref, x - 1))
    return total


def join_lanes(hw_ref, he_ref):
    lane = lax.broadcasted_iota(jnp.int32, hw_ref.shape, 1)
    return jnp.where(lane % APART == APART - 1, pltpu.roll(hw_ref[...], CY - 1, 1), he_ref[...])


def halo_lanes(x, joined):
    lane = lax.broadcasted_iota(jnp.int32, joined.shape, 1)
    here = joined if x == 0 else pltpu.roll(joined, CY - APART * x, 1)
    return jnp.where((lane == 0) | (lane == CY - 1), here, 0.0)


def put_edges(lam_ref, mask_ref, fx_ref, fy_ref, en_ref, es_ref, ew_ref, ee_ref):
    lane = lax.broadcasted_iota(jnp.int32, (PAD, CY), 1)
    for t in range(TRACERS):
        levels = slice(t * PAD, (t + 1) * PAD)
        west = east = jnp.zeros((PAD, CY), F32)
        for x in range(CX):
            weighted = lam_ref[x, levels, :] * row(mask_ref, x)
            fy = row(fy_ref, x)
            at = APART * x
            west = jnp.where(lane == at, pltpu.roll(weighted * (flat_mix + 0.5 * fy), at, 1), west)
            east = jnp.where(lane == at, pltpu.roll(weighted * (flat_mix - 0.5 * fy), at + 1, 1), east)
        ew_ref[levels, :] = west
        ee_ref[levels, :] = east
    en_ref[...] = north_edge(lam_ref[0], row(mask_ref, 0), row(fx_ref, 0))
    es_ref[...] = south_edge(lam_ref[CX - 1], row(mask_ref, CX - 1), row(fx_ref, CX - 1))


def edges_kernel(raw_ref, mask_ref, fx_ref, fy_ref, planes_ref, base_ref, en_ref, es_ref, ew_ref, ee_ref):
    planes_ref[...] = jnp.zeros_like(planes_ref)
    for x in range(CX):
        for t in range(TRACERS):
            planes_ref[x, t * PAD : t * PAD + NZ, :] = raw_ref[pl.ds(t * NZ * CX + x, NZ, stride=CX), :]
    put_edges(planes_ref, mask_ref, fx_ref, fy_ref, en_ref, es_ref, ew_ref, ee_ref)
    for x in range(CX):
        base_ref[x] = planes_ref[x] + step_size * local_plane(x, planes_ref, mask_ref, fx_ref, fy_ref)


EDGE = far(FEATS, CY)
PLANE = (CX, FEATS, CY)


def edges(*args):
    return call(edges_kernel, "edges", (far(*PLANE), far(*PLANE), EDGE, EDGE, EDGE, EDGE), args, mib=8)


def last_kernel(mask_ref, fx_ref, fy_ref, hw_ref, he_ref, lam_far, down_far, out_ref, lam, down, sems):
    wait = bring(((0, lam_far, lam), (0, down_far, down)), sems)
    joined = join_lanes(hw_ref, he_ref)
    wait(0)
    for x in range(CX):
        total = local_plane(x, lam, mask_ref, fx_ref, fy_ref) + halo_lanes(x, joined)
        value = lam[x] + step_size * (total + down[x])
        for t in range(TRACERS):
            out_ref[pl.ds(t * NZ * CX + x, NZ, stride=CX), :] = value[t * PAD : t * PAD + NZ]


def last_stencil(lam, down, *args):
    scratch = [near(*PLANE), near(*PLANE), pltpu.SemaphoreType.DMA((2,))]
    (out,) = call(last_kernel, "stencil0", (near(TRACERS * NZ * CX, CY),), args, (lam, down), scratch, mib=8)
    return out


def rows_kernel(part_ref, hn_ref, hs_ref, out_ref):
    for x, halo_ref in ((0, hs_ref), (CX - 1, hn_ref)):
        for t in range(TRACERS):
            rows = pl.ds(t * NZ * CX + x, NZ, stride=CX)
            out_ref[rows, :] = part_ref[rows, :] + step_size * halo_ref[t * PAD : t * PAD + NZ, :]


def add_rows(part, hn, hs):
    (out,) = call(rows_kernel, "rows0", (near(*part.shape),), (part, hn, hs), aliases={0: 0})
    return out


def closure_step(first, got_ref, owner_ref, mask_ref, lam_ref, weight_refs, out_ref, rows_ref, total, wait):
    f1_ref, f2_ref, f3_ref, r3_ref, r2_ref, r1_ref, b2_ref, b3_ref = weight_refs
    for half in range(2):
        for g in range(DEV // 8):
            at = half * (STORE // 2) + g * 128
            lo = first + half * HALF
            main = [got_ref[8 * g + i, lo : lo + HALF, :] for i in range(8)]
            rows_ref[: 2 * PAD, at : at + 128] = jnp.concatenate(main, axis=0).T
    for g in range(DEV // 8):
        rest = [got_ref[8 * g + i, first + SLOT : first + BLOCK, :] for i in range(8)]
        both = jnp.concatenate(rest, axis=0).T
        rows_ref[2 * PAD :, g * 128 : (g + 1) * 128] = both[:PAD]
        at = STORE // 2 + g * 128
        rows_ref[2 * PAD :, at : at + 128] = both[PAD:]

    def wide(ref):
        return jnp.concatenate([ref[i : i + 1, :] for i in range(CX)], axis=1)

    wait("tile")
    owner = wide(owner_ref)
    at = ((owner >> 4) & 1) * (STORE // 2) + (owner >> 5) * HALF + (owner & (HALF - 1))
    level = lax.broadcasted_iota(jnp.int32, (256, COLS), 0)
    picked = None
    for k in range(STORE // 256):
        hot = jnp.where(level == at - 256 * k, 1.0, 0.0).astype(BF)
        part = dot(rows_ref[:, 256 * k : 256 * (k + 1)], hot)
        picked = part if picked is None else picked + part
    row = lax.broadcasted_iota(jnp.int32, (FEATS, COLS), 0)
    inputs = jnp.where(row == NZ, 1.0, picked).astype(BF)

    wait("weights")
    both = dot(f1_ref[...], inputs)
    h1 = jnp.tanh(both[:HID] + both[HID:])
    h1_high, h1_low = split(h1)
    both = dot(f2_ref[...], h1_high)
    h2 = jnp.tanh(both[:HID] + both[HID:] + dot(f2_ref[:HID], h1_low) + b2_ref[...])
    h2_high, h2_low = split(h2)
    both = dot(f3_ref[...], h2_high)
    sig = jax.nn.sigmoid(both[:PAD] + both[PAD:] + dot(f3_ref[:PAD], h2_low) + b3_ref[...])
    inner = lax.broadcasted_iota(jnp.int32, (PAD, COLS), 0) < NZ - 1
    kappa = jnp.where(inner, kappa_top * sig, 0.0)

    wait("lam")
    mask_row = wide(mask_ref).astype(F32)
    slope = jnp.zeros((PAD, COLS), F32)
    direct = []
    for t in range(TRACERS):
        lo, hi = t * PAD, (t + 1) * PAD
        mu = jnp.concatenate([lam_ref[i, lo:hi, :] for i in range(CX)], axis=1) * mask_row
        gap = mu - pltpu.roll(mu, PAD - 1, 0)
        column = picked[lo:hi]
        slope = slope + gap * (pltpu.roll(column, PAD - 1, 0) - column)
        flow = kappa * gap
        direct.append(pltpu.roll(flow, 1, 0) - flow)
    d3 = slope * kappa * (1.0 - sig)
    d3_high, d3_low = split(d3)
    d2 = dot(r3_ref[...], jnp.concatenate([d3_high, d3_high, d3_low], axis=0)) * (1.0 - h2 * h2)
    d2_high, d2_low = split(d2)
    both = dot(r2_ref[...], d2_high)
    d1 = (both[:HID] + both[HID:] + dot(r2_ref[:HID], d2_low)) * (1.0 - h1 * h1)
    d1_high, d1_low = split(d1)
    both = dot(r1_ref[...], d1_high)
    d0 = both[:FEATS] + both[FEATS:] + dot(r1_ref[:FEATS], d1_low)

    for i in range(CX):
        part = slice(i * CY, (i + 1) * CY)
        for t in range(TRACERS):
            lo, hi = t * PAD, (t + 1) * PAD
            out_ref[i, lo:hi, :] = d0[lo:hi, part] + direct[t][:, part]
    wait("out")

    ones = jnp.ones((16, COLS), BF)
    total[:FEATS, :] += dot_nt(inputs, d1_high) + dot_nt(inputs, d1_low)
    both = dot_nt(jnp.concatenate([h1_high, h1_low, ones], axis=0), d2_high)
    other = dot_nt(jnp.concatenate([h1_high, ones], axis=0), d2_low)
    total[FEATS : FEATS + HID, :] += both[:HID] + both[HID : 2 * HID] + other[:HID]
    total[NZ + 1 : NZ + 2, :] += both[2 * HID : 2 * HID + 1] + other[HID : HID + 1]
    d3_both = jnp.concatenate([d3_high, d3_low], axis=0)
    both = dot_nt(d3_both, h2_high)
    total[FEATS + HID :, :] += both[:PAD] + both[PAD:] + dot_nt(d3_high, h2_low)
    both = dot_nt(ones, d3_both)
    total[NZ + 2 : NZ + 3, :PAD] += both[:1, :PAD] + both[:1, PAD:]


def late_kernel(got_ref, *refs):
    sources, (out_ref, total), refs = refs[:12], refs[12:14], refs[14:]
    targets, (rows_ref, down, sems) = refs[:12], refs[12:]
    names = ("tile", "tile") + ("weights",) * 8 + ("lam", "base")
    wait = bring(zip(names, sources, targets), sems)
    owner, mask, *split_weights = targets[:10]
    planes, base = targets[10:]
    total[...] = jnp.zeros_like(total)

    def then(name):
        wait(name)
        if name == "out":
            wait("base")
            for x in range(CX):
                out_ref[x] = base[x] + step_size * down[x]

    closure_step(BLOCK, got_ref, owner, mask, planes, split_weights, down, rows_ref, total, then)


def early_kernel(got_ref, fx_ref, fy_ref, part_ref, before_ref, owner_ref, mask_ref, *refs):
    split_weights, halos, refs = refs[:8], refs[8:12], refs[12:]
    (lam_far, down_far, grads_ref), sides, (rows_ref, lam, down, total, out_sems) = refs[:3], refs[3:7], refs[7:]
    hn_ref, hs_ref, hw_ref, he_ref = halos
    joined = join_lanes(hw_ref, he_ref)
    for x in range(CX):
        halo = halo_lanes(x, joined)
        if x == 0:
            halo = halo + hs_ref[...]
        if x == CX - 1:
            halo = halo + hn_ref[...]
        lam[x] = part_ref[x] + step_size * halo
    lam_copy = pltpu.make_async_copy(lam, lam_far, out_sems.at[0])
    lam_copy.start()
    down_copy = pltpu.make_async_copy(down, down_far, out_sems.at[1])
    put_edges(lam, mask_ref, fx_ref, fy_ref, *sides)
    total[...] = before_ref[...]

    def then(name):
        if name == "out":
            down_copy.start()

    closure_step(0, got_ref, owner_ref, mask_ref, lam, split_weights, down, rows_ref, total, then)
    grads_ref[: 2 * HID, :] = total[:, :128]
    grads_ref[2 * HID :, :] = total[:, 128:]
    lam_copy.wait()
    down_copy.wait()


TILE_WEIGHTS = [near(CX, CY, dtype=jnp.int32)] * 2
TILE_WEIGHTS += [near(*shape, dtype=BF) for shape in WEIGHTS] + [near(HID, 1), near(PAD, 1)]
ROWS = near(FEATS, STORE, dtype=BF)


def late_closure(got, *copied):
    outs = (near(*PLANE), near(2 * HID, HID), *TILE_WEIGHTS)
    scratch = [near(*PLANE), near(*PLANE), ROWS, near(*PLANE), pltpu.SemaphoreType.DMA((12,))]
    return call(late_kernel, "closure1", outs, (got,), copied, scratch, CLOSURE_MIB)


def early_closure(got, fx, fy, part, before, brought, halos):
    outs = ([far(*PLANE)], [far(*PLANE)], far(4 * HID, 128), EDGE, EDGE, EDGE, EDGE)
    scratch = [ROWS, near(*PLANE), near(*PLANE), near(2 * HID, HID), pltpu.SemaphoreType.DMA((2,))]
    args = (got, fx, fy, part, before, *brought, *halos)
    return call(early_kernel, "closure0", outs, args, (), scratch, CLOSURE_MIB)


def sum_kernel(parts_ref, out_ref):
    values = [parts_ref[8 * i : 8 * i + 8, :] for i in range(DEV)]
    while len(values) > 1:
        values = [left + right for left, right in zip(values[::2], values[1::2])]
    value = values[0]
    for i in range(DEV):
        out_ref[8 * i : 8 * i + 8, :] = value


def unpack_kernel(scale, sums_ref, w1_ref, b1_ref, w2_ref, b2_ref, w3t_ref, b3_ref):
    for part in range(2):
        lanes = slice(part * 128, (part + 1) * 128)
        top = part * 2 * HID
        for t in range(TRACERS):
            w1_ref[t * NZ : (t + 1) * NZ, lanes] = sums_ref[top + t * PAD : top + t * PAD + NZ, :] * scale
        b1_ref[:, lanes] = sums_ref[top + NZ : top + NZ + 1, :] * scale
        b2_ref[:, lanes] = sums_ref[top + NZ + 1 : top + NZ + 2, :] * scale
        w2_ref[:, lanes] = sums_ref[top + FEATS : top + FEATS + HID, :] * scale
        w3t_ref[:, lanes] = sums_ref[top + FEATS + HID : top + FEATS + HID + NZ, :] * scale
    b3_ref[...] = sums_ref[NZ + 2 : NZ + 3, :NZ] * scale


def reduce_params(packed):
    parts = lax.all_to_all(packed, ("gx", "gy"), split_axis=0, concat_axis=0, tiled=True)
    (spread,) = call(sum_kernel, "sum", (far(*packed.shape),), (parts,))
    return spread


def finish_params(spread, count):
    sums = lax.all_to_all(spread, ("gx", "gy"), split_axis=0, concat_axis=0, tiled=True)
    shapes = ((TRACERS * NZ, HID), (1, HID), (HID, HID), (1, HID), (NZ, HID), (1, NZ))
    scale = step_size / float(np.sqrt(count))
    outs = tuple(far(*shape) for shape in shapes)
    return call(functools.partial(unpack_kernel, scale), "unpack", outs, (sums,))


def exchange(axis, before, after):
    up = [(i, i + 1) for i in range(lax.axis_size(axis) - 1)]
    down = [(j, i) for i, j in up]
    return lax.ppermute(before, axis, down), lax.ppermute(after, axis, up)


def on_device(
    stored,
    counts,
    owners,
    land_mask,
    flow_x,
    flow_y,
    costate,
    weight_in,
    bias_in,
    weight_mid,
    bias_mid,
    weight_out,
    bias_out,
):
    payload = pack(counts, stored[0].T)
    costate, weight_mid, payload = lax.optimization_barrier((costate, weight_mid, payload))
    got = lax.all_to_all(payload, ("gx", "gy"), split_axis=0, concat_axis=0, tiled=True)
    split_weights = weights(
        weight_in, bias_in[None, :], weight_mid, bias_mid[None, :], weight_out.T, bias_out[None, :]
    )
    planes, base, north, south, west, east = edges(
        costate.reshape(TRACERS * NZ * CX, CY), land_mask, flow_x, flow_y
    )
    halos = exchange("gx", north, south) + exchange("gy", west, east)
    part, grads, *brought = late_closure(got, owners, land_mask, *split_weights, planes, base)
    lam, down, packed, north, south, west, east = early_closure(got, flow_x, flow_y, part, grads, brought, halos)
    halos_y = exchange("gy", west, east)
    spread = reduce_params(packed)
    north, south, spread, halos_y = lax.optimization_barrier((north, south, spread, halos_y))
    halos_x = exchange("gx", north, south)
    lam, down, spread = lax.optimization_barrier((lam, down, spread))
    adjoint = last_stencil(lam, down, land_mask, flow_x, flow_y, *halos_y)
    adjoint = add_rows(adjoint, *halos_x)
    count = CX * CY * lax.axis_size("gx") * lax.axis_size("gy")
    g1, gb1, g2, gb2, g3, gb3 = finish_params(spread, count)
    return (adjoint.reshape(costate.shape), g1, gb1[0], g2, gb2[0], g3.T, gb3[0])


def solution(mesh):
    in_specs = (
        P(("gx", "gy"), None, None),
        P(("gx", "gy"), None),
        P("gx", "gy"),
        P("gx", "gy"),
        P("gx", "gy"),
        P("gx", "gy"),
        P(None, None, "gx", "gy"),
        P(),
        P(),
        P(),
        P(),
        P(),
        P(),
    )
    out_specs = (P(None, None, "gx", "gy"), P(), P(), P(), P(), P(), P())
    return jax.shard_map(
        on_device, mesh=mesh, in_specs=in_specs, out_specs=out_specs, check_vma=False
    )
```
